256 devices in a mesh: pipe: 8 (over x, z_hi), expert: 32 (over y, z_lo, core).
Axes of the slice: x: 4, y: 4, z: 8 (z_hi: 2, z_lo: 4; z = z_hi * 4 + z_lo), core: 2. Of those that a mesh axis runs over, the one named last changes fastest.
Arguments:
- fwd_acts: bfloat16 [8, 2048, 3584], P('pipe', 'expert'), may hold values from -6 to 6
- fwd_routes: int32 [8, 2048, 2], P('pipe', 'expert'), may hold values from 0 to 7, all different within a row; in each aligned block of 64 rows (0 to 63, 64 to 127, ..., all dimensions but the last counted through in order) at most 20 rows name the same one
- fwd_gates: float32 [8, 2048, 2], P('pipe', 'expert'), may hold values from 0.25 to 1
- back_acts: bfloat16 [8, 2048, 3584], P('pipe', 'expert'), may hold values from -6 to 6
- back_routes: int32 [8, 2048, 2], P('pipe', 'expert'), may hold values from 0 to 7, all different within a row; in each aligned block of 64 rows (0 to 63, 64 to 127, ..., all dimensions but the last counted through in order) at most 20 rows name the same one
- back_gates: float32 [8, 2048, 2], P('pipe', 'expert'), may hold values from 0.25 to 1
- back_grads: bfloat16 [8, 2048, 3584], P('pipe', 'expert'), may hold values from -0.59765625 to 0.59765625
- w_up: bfloat16 [8, 32, 3584, 256], P('pipe', 'expert'), may hold values from -0.09375 to 0.09375
- w_down: bfloat16 [8, 32, 256, 3584], P('pipe', 'expert'), may hold values from -0.1875 to 0.1875
Outputs:
- fwd_next: bfloat16 [8, 2048, 3584], P('pipe', 'expert')
- back_next: bfloat16 [8, 2048, 3584], P('pipe', 'expert')
- grad_up: float32 [8, 32, 3584, 256], P('pipe', 'expert')
- grad_down: float32 [8, 32, 256, 3584], P('pipe', 'expert')
The draws below stay inside these ranges and needn't reach their ends.
Inputs may be any that keep to these rules, and one draw needn't show every extreme that they name: `fwd_routes`: in each aligned block of 64 rows of a section the 2 experts of a row differ, and each expert is named by at most 20 rows, by exactly 20 in some block. `back_routes`: as for fwd_routes.
All inputs are finite; a program needn't handle non-finite values.
Results may differ from the reference program's by a relative error of at most 0.005.
Values may be sent and summed in bfloat16 or wider, within the bound.
A program may use at most 192 MiB of HBM per device.

```python
import math
import jax
import jax.numpy as jnp
import numpy as np
from jax import lax

D = 3584
FF = 1024
GROUP = 4
TOP = 2
TOK = 64
FP = 256
EXPERTS = 8
CAP = 20
SECTIONS = 8
TOKENS = 2048
N_EXPERT = 32


def block_scale(stream_key, shape, pieces, smallest, top_value):
    loudness = 1.0
    for axis_at, parts in pieces:
        steps = jax.random.uniform(jax.random.fold_in(jax.random.fold_in(stream_key, 6), axis_at), (parts,), jnp.float32, smallest / len(pieces), top_value / len(pieces))
        loudness = loudness * jnp.repeat(jnp.exp(steps), shape[axis_at] // parts).reshape((-1,) + (1,) * (len(shape) - 1 - axis_at))
    return loudness


def deal_out(rng, own, number, rows, count, top, most, slope):
    ranking = jax.random.permutation(rng, count)
    heavy_load, ordinary = shares(count, rows * top, most, slope, True), shares(count, rows * top, most, slope, False)
    places = jnp.arange(count)

    def named(lengths, rotation):
        used = int((lengths > 0).sum())
        fixed = max(1, used // 4)
        moved = fixed + (places - fixed + rotation * (used - fixed)) % max(1, count - fixed)
        return jnp.zeros((count,), jnp.int32).at[ranking[jnp.where(places < fixed, places, moved)]].set(jnp.asarray(lengths, jnp.int32))

    lengths = jnp.where(number % 4 == 0, named(heavy_load, number // 4), named(ordinary, number - number // 4 - 1))
    mixed = jax.random.permutation(jax.random.fold_in(own, 3), count)
    source_of, taker = mixed[0:count // 2 * 2:2], mixed[1:count // 2 * 2:2]
    room = jnp.minimum(lengths[source_of] - 1, most - lengths[taker]) // 2
    room = jnp.where((source_of == ranking[0]) | (taker == ranking[0]) | (lengths[taker] == 0), 0, jnp.maximum(room, 0))
    moved = jax.random.randint(jax.random.fold_in(own, 4), (count // 2,), 0, 1 << 20) % (room + 1)
    lengths = lengths.at[source_of].add(-moved).at[taker].add(moved)
    items = jnp.searchsorted(jnp.cumsum(lengths), jnp.arange(rows * top), side="right").astype(jnp.int32)
    grid = items.reshape(top, rows).T
    grid = grid[jax.random.permutation(jax.random.fold_in(own, 1), rows)]
    rotation = jax.random.randint(jax.random.fold_in(own, 2), (rows, 1), 0, top)
    return jnp.take_along_axis(grid, (jnp.arange(top)[None, :] + rotation) % top, axis=1)


def shares(count, total, bound, slope, full):
    portions = [(1 << 20) // math.isqrt(rank ** slope) + 1 for rank in range(1, count + 1)]
    largest = bound if full else min(bound, max(-(-total // count), total * portions[0] // sum(portions)))
    least = 1 if total - largest >= count - 1 else 0
    holding, rest = [largest] + [least] * (count - 1), total - largest - least * (count - 1)
    while rest > 0:
        free = [i for i in range(1, count) if holding[i] < largest] or [i for i in range(1, count) if holding[i] < bound]
        mass, remaining = sum([portions[i] for i in free]), rest
        for i in free:
            extra = min(bound - holding[i], max(1, remaining * portions[i] // mass), rest)
            holding[i] = holding[i] + extra
            rest = rest - extra
    return np.array(holding)


def bell_draw(stream_key, extent, scale, bound, shards=(), held_as=jnp.bfloat16):
    result = scale * jax.random.normal(stream_key, extent, jnp.float32)
    if shards:
        result = result * block_scale(stream_key, extent, shards, -0.22, 0.18)
    return jnp.clip(result, -bound, bound).astype(held_as)


def setup_inputs(seed: int = 0) -> dict:
    seeds = jax.random.split(jax.random.key(seed), 10)
    fwd_acts = bell_draw(seeds[0], (SECTIONS, TOKENS, D), 1.0, 6.0, ((0, 8), (1, 32)))
    fwd_routes_keys = jax.random.split(jax.random.fold_in(seeds[1], 1), SECTIONS * TOKENS // TOK)
    fwd_routes_turns = jax.random.permutation(jax.random.fold_in(seeds[1], 3), SECTIONS * TOKENS // TOK)
    fwd_routes = jax.vmap(lambda own, number: deal_out(jax.random.fold_in(seeds[1], 2), own, number, TOK, EXPERTS, TOP, CAP, 1))(fwd_routes_keys, fwd_routes_turns).reshape((SECTIONS, TOKENS, TOP))
    fwd_gates = jnp.clip(0.25 + 0.75 * jax.random.uniform(seeds[2], (SECTIONS, TOKENS, TOP), jnp.float32) ** block_scale(seeds[2], (SECTIONS, TOKENS, TOP), ((0, 8), (1, 32)), -0.2, 0.2), 0.25, 1.0)
    back_acts = bell_draw(seeds[3], (SECTIONS, TOKENS, D), 1.0, 6.0, ((0, 8), (1, 32)))
    back_routes_keys = jax.random.split(jax.random.fold_in(seeds[4], 1), SECTIONS * TOKENS // TOK)
    back_routes_turns = jax.random.permutation(jax.random.fold_in(seeds[4], 3), SECTIONS * TOKENS // TOK)
    back_routes = jax.vmap(lambda own, number: deal_out(jax.random.fold_in(seeds[4], 2), own, number, TOK, EXPERTS, TOP, CAP, 1))(back_routes_keys, back_routes_turns).reshape((SECTIONS, TOKENS, TOP))
    back_gates = jnp.clip(0.25 + 0.75 * jax.random.uniform(seeds[5], (SECTIONS, TOKENS, TOP), jnp.float32) ** block_scale(seeds[5], (SECTIONS, TOKENS, TOP), ((0, 8), (1, 32)), -0.2, 0.2), 0.25, 1.0)
    back_grads = bell_draw(seeds[6], (SECTIONS, TOKENS, D), 0.1, 0.59765625, ((0, 8), (1, 32)))
    w_up = bell_draw(seeds[7], (SECTIONS, N_EXPERT, D, FP), D ** -0.5, 0.09375, ((0, 8), (1, 32)))
    w_down = bell_draw(seeds[8], (SECTIONS, N_EXPERT, FP, D), FF ** -0.5, 0.1875, ((0, 8), (1, 32)))
    return dict(fwd_acts=fwd_acts, fwd_routes=fwd_routes, fwd_gates=fwd_gates, back_acts=back_acts, back_routes=back_routes, back_gates=back_gates, back_grads=back_grads, w_up=w_up, w_down=w_down)


HIGH = lax.Precision.HIGHEST

def silu_grad(value):
    sigma = jax.nn.sigmoid(value)
    return sigma * (1.0 + value * (1.0 - sigma))

def tables(routes, gates):
    blocks, tok_rows, top_count = routes.shape
    flat = routes.reshape(blocks, tok_rows * top_count)
    onehot = (flat[:, :, None] == jnp.arange(EXPERTS, dtype=jnp.int32)[None, None, :]).astype(jnp.int32)
    before = jnp.cumsum(onehot, axis=1) - onehot
    slots = lax.optimization_barrier(jnp.sum(before * onehot, axis=2))
    places = (flat * CAP + slots).reshape(blocks, tok_rows, top_count)
    columns = jnp.arange(EXPERTS * CAP, dtype=jnp.int32)
    hits = (places[..., None] == columns).astype(jnp.float32)
    plain = lax.optimization_barrier(jnp.sum(hits, axis=2))
    gated = lax.optimization_barrier(jnp.sum(hits * gates[..., None], axis=2))
    return (plain, gated)

def dispatch(table, values):
    return jnp.einsum('jtc,jtd->jcd', table, values, precision=HIGH)

def by_expert(rows):
    return rows.reshape(N_EXPERT, EXPERTS, CAP, D).transpose(1, 0, 2, 3).reshape(EXPERTS, N_EXPERT * CAP, D)

def by_block(rows):
    return rows.reshape(EXPERTS, N_EXPERT, CAP, D).transpose(1, 0, 2, 3).reshape(N_EXPERT, EXPERTS * CAP, D)

def expert_forward(operands):
    rows, up_slices, down_slices = operands
    full_up = up_slices.transpose(1, 0, 2).reshape(D, FF).astype(jnp.float32)
    pre = jnp.dot(rows.astype(jnp.float32), full_up, precision=HIGH)
    act = jax.nn.silu(pre).astype(jnp.bfloat16)
    total = jnp.zeros((rows.shape[0], D), jnp.float32)
    for member in range(GROUP):
        part = jnp.dot(act[:, member * FP:(member + 1) * FP].astype(jnp.float32), down_slices[member].astype(jnp.float32), precision=HIGH).astype(jnp.bfloat16)
        total = total + lax.optimization_barrier(part).astype(jnp.float32)
    return total

def expert_backward(operands):
    rows, grad_rows, up_slices, down_slices = operands
    full_up = up_slices.transpose(1, 0, 2).reshape(D, FF).astype(jnp.float32)
    full_down = down_slices.reshape(FF, D).astype(jnp.float32)
    rows_wide = rows.astype(jnp.float32)
    grads_wide = grad_rows.astype(jnp.float32)
    pre = jnp.dot(rows_wide, full_up, precision=HIGH)
    act = jax.nn.silu(pre).astype(jnp.bfloat16)
    dact = jnp.dot(grads_wide, full_down.T, precision=HIGH)
    dpre = (dact * silu_grad(pre)).astype(jnp.bfloat16)
    total = jnp.zeros((rows.shape[0], D), jnp.float32)
    for member in range(GROUP):
        part = jnp.dot(dpre[:, member * FP:(member + 1) * FP].astype(jnp.float32), up_slices[member].astype(jnp.float32).T, precision=HIGH).astype(jnp.bfloat16)
        total = total + lax.optimization_barrier(part).astype(jnp.float32)
    grad_up = jnp.dot(rows_wide.T, dpre.astype(jnp.float32), precision=HIGH)
    grad_up = grad_up.reshape(D, GROUP, FP).transpose(1, 0, 2)
    grad_down = jnp.dot(act.astype(jnp.float32).T, grads_wide, precision=HIGH).reshape(GROUP, FP, D)
    return (total, grad_up, grad_down)

def section(operands):
    fwd_in, fwd_rt, fwd_gt, back_in, back_rt, back_gt, back_dy, up_w, down_w = operands
    up_e = up_w.reshape(EXPERTS, GROUP, D, FP)
    down_e = down_w.reshape(EXPERTS, GROUP, FP, D)
    plain_f, gated_f = tables(fwd_rt.reshape(N_EXPERT, TOK, TOP), fwd_gt.reshape(N_EXPERT, TOK, TOP))
    inputs_f = fwd_in.reshape(N_EXPERT, TOK, D).astype(jnp.float32)
    rows_f = dispatch(plain_f, inputs_f).astype(jnp.bfloat16)
    outs_f = lax.map(expert_forward, (by_expert(rows_f), up_e, down_e))
    merged = jnp.einsum('jtc,jcd->jtd', gated_f, by_block(outs_f), precision=HIGH)
    section_out = (inputs_f + merged).astype(jnp.bfloat16).reshape(TOKENS, D)
    plain_b, gated_b = tables(back_rt.reshape(N_EXPERT, TOK, TOP), back_gt.reshape(N_EXPERT, TOK, TOP))
    inputs_b = back_in.reshape(N_EXPERT, TOK, D).astype(jnp.float32)
    grads_b = back_dy.reshape(N_EXPERT, TOK, D).astype(jnp.float32)
    rows_b = dispatch(plain_b, inputs_b).astype(jnp.bfloat16)
    rows_g = dispatch(gated_b, grads_b).astype(jnp.bfloat16)
    drows, grad_up, grad_down = lax.map(expert_backward, (by_expert(rows_b), by_expert(rows_g), up_e, down_e))
    spread_back = jnp.einsum('jtc,jcd->jtd', plain_b, by_block(drows), precision=HIGH)
    section_grad = (grads_b + spread_back).astype(jnp.bfloat16).reshape(TOKENS, D)
    return (section_out, section_grad, grad_up.reshape(N_EXPERT, D, FP), grad_down.reshape(N_EXPERT, FP, D))

def reference(fwd_acts, fwd_routes, fwd_gates, back_acts, back_routes, back_gates, back_grads, w_up, w_down):
    section_out, section_grad, grad_up, grad_down = lax.map(section, (fwd_acts, fwd_routes, fwd_gates, back_acts, back_routes, back_gates, back_grads, w_up, w_down))
    fwd_next = jnp.roll(section_out, 1, axis=0)
    back_next = jnp.roll(section_grad, -1, axis=0)
    return (fwd_next, back_next, grad_up, grad_down)
```

```python
import jax
import jax.numpy as jnp
from jax import lax
from jax.sharding import PartitionSpec as P

GROUP = 4


HIGH = lax.Precision.HIGHEST


def passed_along(value, axis, steps):
    count = lax.axis_size(axis)
    pairs = [(source, (source + steps) % count) for source in range(count)]
    return lax.ppermute(value, axis, pairs)


def silu_grad(value):
    sigma = jax.nn.sigmoid(value)
    return sigma * (1.0 + value * (1.0 - sigma))


def tables(routes, gates, experts, slot_cap):
    tok_rows, top_count = routes.shape
    flat = routes.reshape(tok_rows * top_count)
    onehot = (flat[:, None] == jnp.arange(experts, dtype=jnp.int32)[None, :]).astype(jnp.int32)
    before = jnp.cumsum(onehot, axis=0) - onehot
    slots = jnp.sum(before * onehot, axis=1)
    places = flat * slot_cap + slots
    columns = jnp.arange(experts * slot_cap, dtype=jnp.int32)
    hits = (
        (places[:, None] == columns[None, :])
        .astype(jnp.float32)
        .reshape(tok_rows, top_count, experts * slot_cap)
    )
    plain = jnp.sum(hits, axis=1)
    gated = jnp.sum(hits * gates[:, :, None], axis=1)
    return (plain, gated)


def gather_rows(plain, values):
    return lax.dot_general(
        plain.astype(jnp.bfloat16),
        values,
        (((0,), (0,)), ((), ())),
        preferred_element_type=jnp.float32,
    ).astype(jnp.bfloat16)


def send_rows(stacked, experts, slot_cap):
    count, _, model_width = stacked.shape
    chunks = stacked.reshape(count, experts, slot_cap, model_width)
    received = lax.all_to_all(chunks, "eg", split_axis=1, concat_axis=1, tiled=True)
    gathered = lax.all_gather(received, "em", axis=1, tiled=True)
    return gathered.reshape(count, -1, model_width)


def send_back(parts, experts, slot_cap):
    count, _, model_width = parts.shape
    arranged = parts.reshape(count, GROUP, experts * slot_cap, model_width)
    received = lax.all_to_all(arranged, "em", split_axis=1, concat_axis=1, tiled=True)
    summed = jnp.sum(received, axis=1, dtype=jnp.float32).astype(jnp.bfloat16)
    summed = summed.reshape(count, experts, slot_cap, model_width)
    back = lax.all_to_all(summed, "eg", split_axis=1, concat_axis=1, tiled=True)
    return back.reshape(count, experts * slot_cap, model_width).astype(jnp.float32)


def expert_forward(rows, up_proj, down_proj):
    pre = jnp.dot(rows, up_proj, preferred_element_type=jnp.float32)
    act = jax.nn.silu(pre).astype(jnp.bfloat16)
    return jnp.dot(act, down_proj, preferred_element_type=jnp.float32).astype(jnp.bfloat16)


def expert_backward(rows, grad_rows, up_proj, down_proj):
    pre = jnp.dot(rows, up_proj, preferred_element_type=jnp.float32)
    act = jax.nn.silu(pre).astype(jnp.bfloat16)
    dact = lax.dot_general(
        grad_rows, down_proj, (((1,), (1,)), ((), ())), preferred_element_type=jnp.float32
    )
    dpre = (dact * silu_grad(pre)).astype(jnp.bfloat16)
    dpart = lax.dot_general(
        dpre, up_proj, (((1,), (1,)), ((), ())), preferred_element_type=jnp.float32
    ).astype(jnp.bfloat16)
    grad_up = lax.dot_general(
        rows, dpre, (((0,), (0,)), ((), ())), preferred_element_type=jnp.float32
    )
    grad_down = lax.dot_general(
        act, grad_rows, (((0,), (0,)), ((), ())), preferred_element_type=jnp.float32
    )
    return (dpart, grad_up, grad_down)


def local(
    fwd_acts, fwd_routes, fwd_gates, back_acts, back_routes, back_gates, back_grads, w_up, w_down
):
    devices = lax.axis_size("eg") * lax.axis_size("em")
    experts = devices // GROUP
    tok_rows = fwd_acts.shape[1]
    top_count = fwd_routes.shape[2]
    slot_cap = GROUP * (5 * tok_rows * top_count // (4 * devices))
    up_proj = w_up[0, 0]
    down_proj = w_down[0, 0]
    fwd_input = fwd_acts[0]
    back_input = back_acts[0]
    out_grad = back_grads[0]
    plain_f, gated_f = tables(fwd_routes[0], fwd_gates[0], experts, slot_cap)
    plain_b, gated_b = tables(back_routes[0], back_gates[0], experts, slot_cap)
    buffer_f = gather_rows(plain_f, fwd_input)
    buffer_x = gather_rows(plain_b, back_input)
    buffer_g = lax.dot_general(
        gated_b, out_grad.astype(jnp.float32), (((0,), (0,)), ((), ())), precision=HIGH
    ).astype(jnp.bfloat16)
    got_f = send_rows(buffer_f[None], experts, slot_cap)
    part = expert_forward(got_f[0], up_proj, down_proj)
    summed_f = send_back(part[None], experts, slot_cap)[0]
    got_b = send_rows(jnp.stack([buffer_x, buffer_g]), experts, slot_cap)
    dpart, grad_up, grad_down = expert_backward(got_b[0], got_b[1], up_proj, down_proj)
    summed_b = send_back(dpart[None], experts, slot_cap)[0]
    merged = jnp.dot(gated_f, summed_f, precision=HIGH)
    section_out = (fwd_input.astype(jnp.float32) + merged).astype(jnp.bfloat16)
    spread_back = jnp.dot(plain_b, summed_b, precision=HIGH)
    section_grad = (out_grad.astype(jnp.float32) + spread_back).astype(jnp.bfloat16)
    fwd_next = passed_along(section_out[None], "pipe", 1)
    back_next = passed_along(section_grad[None], "pipe", -1)
    return (fwd_next, back_next, grad_up[None, None], grad_down[None, None])


def solution(mesh):
    groups = mesh.shape["expert"] // GROUP
    devices = mesh.devices.reshape(mesh.shape["pipe"], groups, GROUP)
    mesh = jax.sharding.Mesh(devices, ("pipe", "eg", "em"))
    in_specs = (
        P("pipe", ("eg", "em"), None),
        P("pipe", ("eg", "em"), None),
        P("pipe", ("eg", "em"), None),
        P("pipe", ("eg", "em"), None),
        P("pipe", ("eg", "em"), None),
        P("pipe", ("eg", "em"), None),
        P("pipe", ("eg", "em"), None),
        P("pipe", ("eg", "em"), None, None),
        P("pipe", ("eg", "em"), None, None),
    )
    out_specs = (
        P("pipe", ("eg", "em"), None),
        P("pipe", ("eg", "em"), None),
        P("pipe", ("eg", "em"), None, None),
        P("pipe", ("eg", "em"), None, None),
    )
    return jax.shard_map(local, mesh=mesh, in_specs=in_specs, out_specs=out_specs, check_vma=False)
```

```python
import jax
import jax.numpy as jnp
from jax import lax
from jax.sharding import PartitionSpec as P

GROUP = 4


HIGH = lax.Precision.HIGHEST


def passed_along(value, axis, steps):
    count = lax.axis_size(axis)
    pairs = [(source, (source + steps) % count) for source in range(count)]
    return lax.ppermute(value, axis, pairs)


def silu_grad(value):
    sigma = jax.nn.sigmoid(value)
    return sigma * (1.0 + value * (1.0 - sigma))


def tables(routes, gates, experts, slot_cap):
    tok_rows, top_count = routes.shape
    flat = routes.reshape(tok_rows * top_count)
    onehot = (flat[:, None] == jnp.arange(experts, dtype=jnp.int32)[None, :]).astype(jnp.int32)
    before = jnp.cumsum(onehot, axis=0) - onehot
    slots = jnp.sum(before * onehot, axis=1)
    places = flat * slot_cap + slots
    columns = jnp.arange(experts * slot_cap, dtype=jnp.int32)
    hits = (
        (places[:, None] == columns[None, :])
        .astype(jnp.float32)
        .reshape(tok_rows, top_count, experts * slot_cap)
    )
    plain = jnp.sum(hits, axis=1)
    gated = jnp.sum(hits * gates[:, :, None], axis=1)
    return (plain, gated)


def gather_rows(plain, values):
    return lax.dot_general(
        plain.astype(jnp.bfloat16),
        values,
        (((0,), (0,)), ((), ())),
        preferred_element_type=jnp.float32,
    ).astype(jnp.bfloat16)


def to_wire(rows, *lead):
    return rows.reshape(*lead, -1, 128)


def send_rows(rows, experts, slot_cap):
    model_width = rows.shape[-1]
    chunks = to_wire(rows, experts)
    received = lax.all_to_all(chunks, "eg", split_axis=0, concat_axis=0, tiled=True)
    across = lax.all_gather(received, "ez", axis=0)
    gathered = lax.all_gather(across, "ec", axis=0)
    return gathered.reshape(-1, model_width)


def send_back(parts, experts):
    model_width = parts.shape[-1]
    wire = to_wire(parts, 2, 2, experts)
    mine = lax.all_to_all(wire, "ec", split_axis=0, concat_axis=0, tiled=True)
    pair = jnp.sum(mine.astype(jnp.float32), axis=0)
    other = lax.all_to_all(pair, "ez", split_axis=0, concat_axis=0, tiled=True)
    summed = jnp.sum(other, axis=0).astype(jnp.bfloat16)
    back = lax.all_to_all(summed, "eg", split_axis=0, concat_axis=0, tiled=True)
    return back.reshape(-1, model_width).astype(jnp.float32)


def expert_forward(rows, up_proj, down_proj):
    pre = jnp.einsum("...d,df->...f", rows, up_proj, preferred_element_type=jnp.float32)
    act = jax.nn.silu(pre).astype(jnp.bfloat16)
    return jnp.einsum(
        "...f,fd->...d", act, down_proj, preferred_element_type=jnp.float32
    ).astype(jnp.bfloat16)


def expert_backward(rows, grad_rows, up_proj, down_proj):
    pre = jnp.einsum("...d,df->...f", rows, up_proj, preferred_element_type=jnp.float32)
    act = jax.nn.silu(pre).astype(jnp.bfloat16)
    dact = jnp.einsum("...d,fd->...f", grad_rows, down_proj, preferred_element_type=jnp.float32)
    dpre = (dact * silu_grad(pre)).astype(jnp.bfloat16)
    dpart = jnp.einsum(
        "...f,df->...d", dpre, up_proj, preferred_element_type=jnp.float32
    ).astype(jnp.bfloat16)
    grad_up = jnp.einsum("rd,rf->df", rows, dpre, preferred_element_type=jnp.float32)
    grad_down = jnp.einsum("rf,rd->fd", act, grad_rows, preferred_element_type=jnp.float32)
    return (dpart, grad_up, grad_down)


def local(
    fwd_acts, fwd_routes, fwd_gates, back_acts, back_routes, back_gates, back_grads, w_up, w_down
):
    devices = lax.axis_size("eg") * GROUP
    experts = devices // GROUP
    tok_rows = fwd_acts.shape[1]
    top_count = fwd_routes.shape[2]
    slot_cap = GROUP * (5 * tok_rows * top_count // (4 * devices))
    up_proj = w_up[0, 0]
    down_proj = w_down[0, 0]
    fwd_input = fwd_acts[0]
    back_input = back_acts[0]
    out_grad = back_grads[0]
    plain_f, gated_f = tables(fwd_routes[0], fwd_gates[0], experts, slot_cap)
    plain_b, gated_b = tables(back_routes[0], back_gates[0], experts, slot_cap)
    buffer_f = gather_rows(plain_f, fwd_input)
    buffer_x = gather_rows(plain_b, back_input)
    buffer_g = lax.dot_general(
        gated_b, out_grad.astype(jnp.float32), (((0,), (0,)), ((), ())), precision=HIGH
    ).astype(jnp.bfloat16)
    got_f = send_rows(buffer_f, experts, slot_cap)
    part = expert_forward(got_f, up_proj, down_proj)
    summed_f = send_back(part, experts)
    got_x = send_rows(buffer_x, experts, slot_cap)
    got_g = send_rows(buffer_g, experts, slot_cap)
    dpart, grad_up, grad_down = expert_backward(got_x, got_g, up_proj, down_proj)
    summed_b = send_back(dpart, experts)
    merged = jnp.dot(gated_f, summed_f, precision=HIGH)
    section_out = (fwd_input.astype(jnp.float32) + merged).astype(jnp.bfloat16)
    spread_back = jnp.dot(plain_b, summed_b, precision=HIGH)
    section_grad = (out_grad.astype(jnp.float32) + spread_back).astype(jnp.bfloat16)
    fwd_next = passed_along(section_out[None], "pipe", 1)
    back_next = passed_along(section_grad[None], "pipe", -1)
    return (fwd_next, back_next, grad_up[None, None], grad_down[None, None])


def solution(mesh):
    groups = mesh.shape["expert"] // GROUP
    devices = mesh.devices.reshape(mesh.shape["pipe"], groups, 2, GROUP // 2)
    mesh = jax.sharding.Mesh(devices, ("pipe", "eg", "ez", "ec"))
    in_specs = (
        P("pipe", ("eg", "ez", "ec"), None),
        P("pipe", ("eg", "ez", "ec"), None),
        P("pipe", ("eg", "ez", "ec"), None),
        P("pipe", ("eg", "ez", "ec"), None),
        P("pipe", ("eg", "ez", "ec"), None),
        P("pipe", ("eg", "ez", "ec"), None),
        P("pipe", ("eg", "ez", "ec"), None),
        P("pipe", ("eg", "ez", "ec"), None, None),
        P("pipe", ("eg", "ez", "ec"), None, None),
    )
    out_specs = (
        P("pipe", ("eg", "ez", "ec"), None),
        P("pipe", ("eg", "ez", "ec"), None),
        P("pipe", ("eg", "ez", "ec"), None, None),
        P("pipe", ("eg", "ez", "ec"), None, None),
    )
    return jax.shard_map(local, mesh=mesh, in_specs=in_specs, out_specs=out_specs, check_vma=False)
```

```python
import jax
import jax.numpy as jnp
from jax import lax
from jax.sharding import PartitionSpec as P
from jax.experimental import pallas as pl
from jax.experimental.pallas import tpu as pltpu
import functools

GROUP = 4


HIGH = lax.Precision.HIGHEST


def passed_along(value, axis, steps):
    count = lax.axis_size(axis)
    pairs = [(source, (source + steps) % count) for source in range(count)]
    return lax.ppermute(value, axis, pairs)


def silu_grad(value):
    sigma = jax.nn.sigmoid(value)
    return sigma * (1.0 + value * (1.0 - sigma))


def tables(routes, gates, experts, slot_cap):
    tok_rows, top_count = routes.shape
    flat = routes.reshape(tok_rows * top_count)
    onehot = (flat[:, None] == jnp.arange(experts, dtype=jnp.int32)[None, :]).astype(jnp.int32)
    before = jnp.cumsum(onehot, axis=0) - onehot
    slots = jnp.sum(before * onehot, axis=1)
    places = flat * slot_cap + slots
    columns = jnp.arange(experts * slot_cap, dtype=jnp.int32)
    hits = (
        (places[:, None] == columns[None, :])
        .astype(jnp.float32)
        .reshape(tok_rows, top_count, experts * slot_cap)
    )
    plain = jnp.sum(hits, axis=1)
    gated = jnp.sum(hits * gates[:, :, None], axis=1)
    return (plain, gated)


def gather_rows(plain, values):
    return lax.dot_general(
        plain.astype(jnp.bfloat16),
        values,
        (((0,), (0,)), ((), ())),
        preferred_element_type=jnp.float32,
    ).astype(jnp.bfloat16)


def to_wire(rows, *lead):
    return rows.reshape(*lead, -1, 128)


def dispatch_kernel(groups, *refs):
    sources = refs[:3]
    out, local_sem, send1, recv1, xs_send, xs_recv, cs_send, cs_recv, fw_send, fw_recv = refs[3:]
    mesh_kind = pl.DeviceIdType.MESH
    pipe = lax.axis_index("pipe")
    me = lax.axis_index("eg")
    chip = lax.axis_index("ez")
    core = lax.axis_index("ec")
    across = (pipe, me, 1 - chip, core)
    partner = (pipe, me, chip, 1 - core)
    peers = [(pipe, lax.rem(me + step, groups), chip, core) for step in range(1, groups)]
    barrier = pltpu.get_barrier_semaphore()
    for peer in peers + [across, partner]:
        pl.semaphore_signal(barrier, 1, device_id=peer, device_id_type=mesh_kind)
    pl.semaphore_wait(barrier, len(peers) + 2)
    first = []
    for index, source in enumerate(sources):
        own = pltpu.make_async_copy(source.at[me], out.at[index, core, chip, me], local_sem.at[index])
        own.start()
        copies = []
        for step in range(1, groups):
            copy = pltpu.make_async_remote_copy(
                src_ref=source.at[peers[step - 1][1]],
                dst_ref=out.at[index, core, chip, me],
                send_sem=send1.at[index, step],
                recv_sem=recv1.at[index, step],
                device_id=peers[step - 1],
                device_id_type=mesh_kind,
            )
            copy.start()
            copies.append(copy)
        first.append((own, copies))
    second = []
    for index in range(len(sources)):
        own, copies = first[index]
        own.wait()
        for copy in copies:
            copy.wait_recv()
        block = out.at[index, core, chip]
        far = pltpu.make_async_remote_copy(
            src_ref=block, dst_ref=block, send_sem=xs_send.at[index], recv_sem=xs_recv.at[index],
            device_id=across, device_id_type=mesh_kind,
        )
        far.start()
        near = pltpu.make_async_remote_copy(
            src_ref=block, dst_ref=block, send_sem=cs_send.at[index], recv_sem=cs_recv.at[index],
            device_id=partner, device_id_type=mesh_kind,
        )
        near.start()
        second.append((far, near))
    third = []
    for index in range(len(sources)):
        far, near = second[index]
        far.wait_recv()
        relay = out.at[index, core, 1 - chip]
        onward = pltpu.make_async_remote_copy(
            src_ref=relay, dst_ref=relay, send_sem=fw_send.at[index], recv_sem=fw_recv.at[index],
            device_id=partner, device_id_type=mesh_kind,
        )
        onward.start()
        third.append(onward)
    for index in range(len(sources)):
        own, copies = first[index]
        for copy in copies:
            copy.wait_send()
        far, near = second[index]
        far.wait_send()
        near.wait_send()
        near.wait_recv()
        third[index].wait_send()
        third[index].wait_recv()


def dispatch(wires):
    groups = wires[0].shape[0]
    count = len(wires)
    tail = wires[0].shape[1:]
    dma = pltpu.SemaphoreType.DMA
    return pl.pallas_call(
        functools.partial(dispatch_kernel, groups),
        out_shape=jax.ShapeDtypeStruct((count, 2, 2, groups) + tail, wires[0].dtype),
        in_specs=[pl.BlockSpec(memory_space=pl.ANY)] * count,
        out_specs=pl.BlockSpec(memory_space=pl.ANY),
        scratch_shapes=[
            dma((count,)),
            dma((count, groups)),
            dma((count, groups)),
            dma((count,)),
            dma((count,)),
            dma((count,)),
            dma((count,)),
            dma((count,)),
            dma((count,)),
        ],
        compiler_params=pltpu.CompilerParams(collective_id=0, has_side_effects=True),
    )(*wires)


def to_wire(rows, *lead):
    return rows.reshape(*lead, -1, 128)


def send_back(parts, experts):
    model_width = parts.shape[-1]
    wire = to_wire(parts, 2, 2, experts)
    mine = lax.all_to_all(wire, "ec", split_axis=0, concat_axis=0, tiled=True)
    pair = jnp.sum(mine.astype(jnp.float32), axis=0).astype(jnp.bfloat16)
    other = lax.all_to_all(pair, "ez", split_axis=0, concat_axis=0, tiled=True)
    summed = jnp.sum(other.astype(jnp.float32), axis=0).astype(jnp.bfloat16)
    back = lax.all_to_all(summed, "eg", split_axis=0, concat_axis=0, tiled=True)
    return back.reshape(-1, model_width).astype(jnp.float32)


def expert_forward(rows, up_proj, down_proj):
    pre = jnp.einsum("...d,df->...f", rows, up_proj, preferred_element_type=jnp.float32)
    act = jax.nn.silu(pre).astype(jnp.bfloat16)
    return jnp.einsum(
        "...f,fd->...d", act, down_proj, preferred_element_type=jnp.float32
    ).astype(jnp.bfloat16)


def expert_backward(rows, grad_rows, up_proj, down_proj):
    pre = jnp.einsum("...d,df->...f", rows, up_proj, preferred_element_type=jnp.float32)
    act = jax.nn.silu(pre).astype(jnp.bfloat16)
    dact = jnp.einsum("...d,fd->...f", grad_rows, down_proj, preferred_element_type=jnp.float32)
    dpre = (dact * silu_grad(pre)).astype(jnp.bfloat16)
    dpart = jnp.einsum(
        "...f,df->...d", dpre, up_proj, preferred_element_type=jnp.float32
    ).astype(jnp.bfloat16)
    grad_up = jnp.einsum("rd,rf->df", rows, dpre, preferred_element_type=jnp.float32)
    grad_down = jnp.einsum("rf,rd->fd", act, grad_rows, preferred_element_type=jnp.float32)
    return (dpart, grad_up, grad_down)


def local(
    fwd_acts, fwd_routes, fwd_gates, back_acts, back_routes, back_gates, back_grads, w_up, w_down
):
    devices = lax.axis_size("eg") * GROUP
    experts = devices // GROUP
    tok_rows = fwd_acts.shape[1]
    top_count = fwd_routes.shape[2]
    slot_cap = GROUP * (5 * tok_rows * top_count // (4 * devices))
    up_proj = w_up[0, 0]
    down_proj = w_down[0, 0]
    fwd_input = fwd_acts[0]
    back_input = back_acts[0]
    out_grad = back_grads[0]
    plain_f, gated_f = tables(fwd_routes[0], fwd_gates[0], experts, slot_cap)
    plain_b, gated_b = tables(back_routes[0], back_gates[0], experts, slot_cap)
    buffer_f = gather_rows(plain_f, fwd_input)
    buffer_x = gather_rows(plain_b, back_input)
    buffer_g = lax.dot_general(
        gated_b, out_grad.astype(jnp.float32), (((0,), (0,)), ((), ())), precision=HIGH
    ).astype(jnp.bfloat16)
    model_width = fwd_input.shape[-1]
    got = dispatch([to_wire(b, experts) for b in (buffer_f, buffer_x, buffer_g)])
    got_f, got_x, got_g = [got[index].reshape(-1, model_width) for index in range(3)]
    part = expert_forward(got_f, up_proj, down_proj)
    summed_f = send_back(part, experts)
    dpart, grad_up, grad_down = expert_backward(got_x, got_g, up_proj, down_proj)
    summed_b = send_back(dpart, experts)
    merged = jnp.dot(gated_f, summed_f, precision=HIGH)
    section_out = (fwd_input.astype(jnp.float32) + merged).astype(jnp.bfloat16)
    spread_back = jnp.dot(plain_b, summed_b, precision=HIGH)
    section_grad = (out_grad.astype(jnp.float32) + spread_back).astype(jnp.bfloat16)
    fwd_next = passed_along(section_out[None], "pipe", 1)
    back_next = passed_along(section_grad[None], "pipe", -1)
    return (fwd_next, back_next, grad_up[None, None], grad_down[None, None])


def solution(mesh):
    groups = mesh.shape["expert"] // GROUP
    devices = mesh.devices.reshape(mesh.shape["pipe"], groups, 2, GROUP // 2)
    mesh = jax.sharding.Mesh(devices, ("pipe", "eg", "ez", "ec"))
    in_specs = (
        P("pipe", ("eg", "ez", "ec"), None),
        P("pipe", ("eg", "ez", "ec"), None),
        P("pipe", ("eg", "ez", "ec"), None),
        P("pipe", ("eg", "ez", "ec"), None),
        P("pipe", ("eg", "ez", "ec"), None),
        P("pipe", ("eg", "ez", "ec"), None),
        P("pipe", ("eg", "ez", "ec"), None),
        P("pipe", ("eg", "ez", "ec"), None, None),
        P("pipe", ("eg", "ez", "ec"), None, None),
    )
    out_specs = (
        P("pipe", ("eg", "ez", "ec"), None),
        P("pipe", ("eg", "ez", "ec"), None),
        P("pipe", ("eg", "ez", "ec"), None, None),
        P("pipe", ("eg", "ez", "ec"), None, None),
    )
    return jax.shard_map(local, mesh=mesh, in_specs=in_specs, out_specs=out_specs, check_vma=False)
```

```python
import jax
import jax.numpy as jnp
from jax import lax
from jax.sharding import PartitionSpec as P
from jax.experimental import pallas as pl
from jax.experimental.pallas import tpu as pltpu
import functools

GROUP = 4


HIGH = lax.Precision.HIGHEST


def passed_along(value, axis, steps):
    count = lax.axis_size(axis)
    pairs = [(source, (source + steps) % count) for source in range(count)]
    return lax.ppermute(value, axis, pairs)


def silu_grad(value):
    sigma = jax.nn.sigmoid(value)
    return sigma * (1.0 + value * (1.0 - sigma))


def tables(routes, gates, experts, slot_cap):
    tok_rows, top_count = routes.shape
    flat = routes.reshape(tok_rows * top_count)
    onehot = (flat[:, None] == jnp.arange(experts, dtype=jnp.int32)[None, :]).astype(jnp.int32)
    before = jnp.cumsum(onehot, axis=0) - onehot
    slots = jnp.sum(before * onehot, axis=1)
    places = flat * slot_cap + slots
    columns = jnp.arange(experts * slot_cap, dtype=jnp.int32)
    hits = (
        (places[:, None] == columns[None, :])
        .astype(jnp.float32)
        .reshape(tok_rows, top_count, experts * slot_cap)
    )
    plain = jnp.sum(hits, axis=1)
    gated = jnp.sum(hits * gates[:, :, None], axis=1)
    return (plain, gated)


def gather_rows(plain, values):
    return lax.dot_general(
        plain.astype(jnp.bfloat16),
        values,
        (((0,), (0,)), ((), ())),
        preferred_element_type=jnp.float32,
    ).astype(jnp.bfloat16)


def to_wire(rows, *lead):
    return rows.reshape(*lead, -1, 128)


def dispatch_kernel(groups, *refs):
    sources = refs[:3]
    out, local_sem, send1, recv1, xs_send, xs_recv, cs_send, cs_recv, fw_send, fw_recv = refs[3:]
    mesh_kind = pl.DeviceIdType.MESH
    pipe = lax.axis_index("pipe")
    me = lax.axis_index("eg")
    chip = lax.axis_index("ez")
    core = lax.axis_index("ec")
    across = (pipe, me, 1 - chip, core)
    partner = (pipe, me, chip, 1 - core)
    peers = [(pipe, lax.rem(me + step, groups), chip, core) for step in range(1, groups)]
    barrier = pltpu.get_barrier_semaphore()
    for peer in peers + [across, partner]:
        pl.semaphore_signal(barrier, 1, device_id=peer, device_id_type=mesh_kind)
    pl.semaphore_wait(barrier, len(peers) + 2)
    first = []
    for index, source in enumerate(sources):
        own = pltpu.make_async_copy(source.at[me], out.at[index, core, chip, me], local_sem.at[index])
        own.start()
        copies = []
        for step in range(1, groups):
            copy = pltpu.make_async_remote_copy(
                src_ref=source.at[peers[step - 1][1]],
                dst_ref=out.at[index, core, chip, me],
                send_sem=send1.at[index, step],
                recv_sem=recv1.at[index, step],
                device_id=peers[step - 1],
                device_id_type=mesh_kind,
            )
            copy.start()
            copies.append(copy)
        first.append((own, copies))
    second = []
    for index in range(len(sources)):
        own, copies = first[index]
        own.wait()
        for copy in copies:
            copy.wait_recv()
        block = out.at[index, core, chip]
        far = pltpu.make_async_remote_copy(
            src_ref=block, dst_ref=block, send_sem=xs_send.at[index], recv_sem=xs_recv.at[index],
            device_id=across, device_id_type=mesh_kind,
        )
        far.start()
        near = pltpu.make_async_remote_copy(
            src_ref=block, dst_ref=block, send_sem=cs_send.at[index], recv_sem=cs_recv.at[index],
            device_id=partner, device_id_type=mesh_kind,
        )
        near.start()
        second.append((far, near))
    third = []
    for index in range(len(sources)):
        far, near = second[index]
        far.wait_recv()
        relay = out.at[index, core, 1 - chip]
        onward = pltpu.make_async_remote_copy(
            src_ref=relay, dst_ref=relay, send_sem=fw_send.at[index], recv_sem=fw_recv.at[index],
            device_id=partner, device_id_type=mesh_kind,
        )
        onward.start()
        third.append(onward)
    for index in range(len(sources)):
        own, copies = first[index]
        for copy in copies:
            copy.wait_send()
        far, near = second[index]
        far.wait_send()
        near.wait_send()
        near.wait_recv()
        third[index].wait_send()
        third[index].wait_recv()


def dispatch(wires):
    groups = wires[0].shape[0]
    count = len(wires)
    tail = wires[0].shape[1:]
    dma = pltpu.SemaphoreType.DMA
    return pl.pallas_call(
        functools.partial(dispatch_kernel, groups),
        out_shape=jax.ShapeDtypeStruct((count, 2, 2, groups) + tail, wires[0].dtype),
        in_specs=[pl.BlockSpec(memory_space=pl.ANY)] * count,
        out_specs=pl.BlockSpec(memory_space=pl.ANY),
        scratch_shapes=[
            dma((count,)),
            dma((count, groups)),
            dma((count, groups)),
            dma((count,)),
            dma((count,)),
            dma((count,)),
            dma((count,)),
            dma((count,)),
            dma((count,)),
        ],
        compiler_params=pltpu.CompilerParams(collective_id=0, has_side_effects=True),
    )(*wires)


def to_wire(rows, *lead):
    return rows.reshape(*lead, -1, 128)


def return_kernel(groups, *refs):
    count = len(refs) - 4
    sources = refs[:count]
    out, local_sem, send1, recv1 = refs[count:]
    mesh_kind = pl.DeviceIdType.MESH
    pipe = lax.axis_index("pipe")
    me = lax.axis_index("eg")
    chip = lax.axis_index("ez")
    core = lax.axis_index("ec")
    peers = [(pipe, lax.rem(me + step, groups), chip, core) for step in range(1, groups)]
    barrier = pltpu.get_barrier_semaphore()
    for peer in peers:
        pl.semaphore_signal(barrier, 1, device_id=peer, device_id_type=mesh_kind)
    pl.semaphore_wait(barrier, len(peers))
    started = []
    for index, source in enumerate(sources):
        own = pltpu.make_async_copy(source.at[me], out.at[index, me], local_sem.at[index])
        own.start()
        copies = []
        for step in range(1, groups):
            copy = pltpu.make_async_remote_copy(
                src_ref=source.at[peers[step - 1][1]],
                dst_ref=out.at[index, me],
                send_sem=send1.at[index, step],
                recv_sem=recv1.at[index, step],
                device_id=peers[step - 1],
                device_id_type=mesh_kind,
            )
            copy.start()
            copies.append(copy)
        started.append((own, copies))
    for own, copies in started:
        own.wait()
        for copy in copies:
            copy.wait_send()
            copy.wait_recv()


def send_home(wires):
    groups = wires[0].shape[0]
    count = len(wires)
    dma = pltpu.SemaphoreType.DMA
    return pl.pallas_call(
        functools.partial(return_kernel, groups),
        out_shape=jax.ShapeDtypeStruct((count,) + wires[0].shape, wires[0].dtype),
        in_specs=[pl.BlockSpec(memory_space=pl.ANY)] * count,
        out_specs=pl.BlockSpec(memory_space=pl.ANY),
        scratch_shapes=[dma((count,)), dma((count, groups)), dma((count, groups))],
        compiler_params=pltpu.CompilerParams(collective_id=1, has_side_effects=True),
    )(*wires)


def group_sum(parts, experts):
    model_width = parts.shape[-1]
    blocks = parts.reshape(2, 2, -1, model_width)
    mine = lax.all_to_all(blocks, "ec", split_axis=0, concat_axis=0, tiled=True)
    pair = jnp.sum(mine.astype(jnp.float32), axis=0).astype(jnp.bfloat16)
    other = lax.all_to_all(pair, "ez", split_axis=0, concat_axis=0, tiled=True)
    summed = jnp.sum(other.astype(jnp.float32), axis=0).astype(jnp.bfloat16)
    return to_wire(summed, experts)


def expert_forward(rows, up_proj, down_proj):
    pre = jnp.einsum("...d,df->...f", rows, up_proj, preferred_element_type=jnp.float32)
    act = jax.nn.silu(pre).astype(jnp.bfloat16)
    return jnp.einsum(
        "...f,fd->...d", act, down_proj, preferred_element_type=jnp.float32
    ).astype(jnp.bfloat16)


def expert_backward(rows, grad_rows, up_proj, down_proj):
    pre = jnp.einsum("...d,df->...f", rows, up_proj, preferred_element_type=jnp.float32)
    act = jax.nn.silu(pre).astype(jnp.bfloat16)
    dact = jnp.einsum("...d,fd->...f", grad_rows, down_proj, preferred_element_type=jnp.float32)
    dpre = (dact * silu_grad(pre)).astype(jnp.bfloat16)
    dpart = jnp.einsum(
        "...f,df->...d", dpre, up_proj, preferred_element_type=jnp.float32
    ).astype(jnp.bfloat16)
    grad_up = jnp.einsum("rd,rf->df", rows, dpre, preferred_element_type=jnp.float32)
    grad_down = jnp.einsum("rf,rd->fd", act, grad_rows, preferred_element_type=jnp.float32)
    return (dpart, grad_up, grad_down)


def local(
    fwd_acts, fwd_routes, fwd_gates, back_acts, back_routes, back_gates, back_grads, w_up, w_down
):
    devices = lax.axis_size("eg") * GROUP
    experts = devices // GROUP
    tok_rows = fwd_acts.shape[1]
    top_count = fwd_routes.shape[2]
    slot_cap = GROUP * (5 * tok_rows * top_count // (4 * devices))
    up_proj = w_up[0, 0]
    down_proj = w_down[0, 0]
    fwd_input = fwd_acts[0]
    back_input = back_acts[0]
    out_grad = back_grads[0]
    plain_f, gated_f = tables(fwd_routes[0], fwd_gates[0], experts, slot_cap)
    plain_b, gated_b = tables(back_routes[0], back_gates[0], experts, slot_cap)
    buffer_f = gather_rows(plain_f, fwd_input)
    buffer_x = gather_rows(plain_b, back_input)
    buffer_g = lax.dot_general(
        gated_b, out_grad.astype(jnp.float32), (((0,), (0,)), ((), ())), precision=HIGH
    ).astype(jnp.bfloat16)
    model_width = fwd_input.shape[-1]
    got = dispatch([to_wire(b, experts) for b in (buffer_f, buffer_x, buffer_g)])
    got_f, got_x, got_g = [got[index].reshape(-1, model_width) for index in range(3)]
    part = expert_forward(got_f, up_proj, down_proj)
    wire_f = group_sum(part, experts)
    dpart, grad_up, grad_down = expert_backward(got_x, got_g, up_proj, down_proj)
    wire_b = group_sum(dpart, experts)
    home = send_home([wire_f, wire_b])
    summed_f = home[0].reshape(-1, model_width).astype(jnp.float32)
    summed_b = home[1].reshape(-1, model_width).astype(jnp.float32)
    merged = jnp.dot(gated_f, summed_f, precision=HIGH)
    section_out = (fwd_input.astype(jnp.float32) + merged).astype(jnp.bfloat16)
    spread_back = jnp.dot(plain_b, summed_b, precision=HIGH)
    section_grad = (out_grad.astype(jnp.float32) + spread_back).astype(jnp.bfloat16)
    fwd_next = passed_along(section_out[None], "pipe", 1)
    back_next = passed_along(section_grad[None], "pipe", -1)
    return (fwd_next, back_next, grad_up[None, None], grad_down[None, None])


def solution(mesh):
    groups = mesh.shape["expert"] // GROUP
    devices = mesh.devices.reshape(mesh.shape["pipe"], groups, 2, GROUP // 2)
    mesh = jax.sharding.Mesh(devices, ("pipe", "eg", "ez", "ec"))
    in_specs = (
        P("pipe", ("eg", "ez", "ec"), None),
        P("pipe", ("eg", "ez", "ec"), None),
        P("pipe", ("eg", "ez", "ec"), None),
        P("pipe", ("eg", "ez", "ec"), None),
        P("pipe", ("eg", "ez", "ec"), None),
        P("pipe", ("eg", "ez", "ec"), None),
        P("pipe", ("eg", "ez", "ec"), None),
        P("pipe", ("eg", "ez", "ec"), None, None),
        P("pipe", ("eg", "ez", "ec"), None, None),
    )
    out_specs = (
        P("pipe", ("eg", "ez", "ec"), None),
        P("pipe", ("eg", "ez", "ec"), None),
        P("pipe", ("eg", "ez", "ec"), None, None),
        P("pipe", ("eg", "ez", "ec"), None, None),
    )
    return jax.shard_map(local, mesh=mesh, in_specs=in_specs, out_specs=out_specs, check_vma=False)
```

```python
import jax
import jax.numpy as jnp
from jax import lax
from jax.sharding import PartitionSpec as P
from jax.experimental import pallas as pl
from jax.experimental.pallas import tpu as pltpu
import functools

GROUP = 4


HIGH = lax.Precision.HIGHEST


def passed_along(value, axis, steps):
    count = lax.axis_size(axis)
    pairs = [(source, (source + steps) % count) for source in range(count)]
    return lax.ppermute(value, axis, pairs)


def silu_grad(value):
    sigma = jax.nn.sigmoid(value)
    return sigma * (1.0 + value * (1.0 - sigma))


def tables(routes, gates, experts, slot_cap):
    tok_rows, top_count = routes.shape
    flat = routes.reshape(tok_rows * top_count)
    onehot = (flat[:, None] == jnp.arange(experts, dtype=jnp.int32)[None, :]).astype(jnp.int32)
    before = jnp.cumsum(onehot, axis=0) - onehot
    slots = jnp.sum(before * onehot, axis=1)
    places = flat * slot_cap + slots
    columns = jnp.arange(experts * slot_cap, dtype=jnp.int32)
    hits = (
        (places[:, None] == columns[None, :])
        .astype(jnp.float32)
        .reshape(tok_rows, top_count, experts * slot_cap)
    )
    plain = jnp.sum(hits, axis=1)
    gated = jnp.sum(hits * gates[:, :, None], axis=1)
    return (plain, gated)


def gather_rows(plain, values):
    return lax.dot_general(
        plain.astype(jnp.bfloat16),
        values,
        (((0,), (0,)), ((), ())),
        preferred_element_type=jnp.float32,
    ).astype(jnp.bfloat16)


def to_wire(rows, *lead):
    return rows.reshape(*lead, -1, 128)


def dispatch_kernel(groups, *refs):
    sources = refs[:3]
    outs = refs[3:6]
    local_sem, send1, recv1, xs_send, xs_recv, cs_send, cs_recv, fw_send, fw_recv = refs[6:]
    mesh_kind = pl.DeviceIdType.MESH
    pipe = lax.axis_index("pipe")
    me = lax.axis_index("eg")
    chip = lax.axis_index("ez")
    core = lax.axis_index("ec")
    across = (pipe, me, 1 - chip, core)
    partner = (pipe, me, chip, 1 - core)
    peers = [(pipe, lax.rem(me + step, groups), chip, core) for step in range(1, groups)]
    barrier = pltpu.get_barrier_semaphore()
    for peer in peers + [across, partner]:
        pl.semaphore_signal(barrier, 1, device_id=peer, device_id_type=mesh_kind)
    pl.semaphore_wait(barrier, len(peers) + 2)
    first = []
    for index, source in enumerate(sources):
        own = pltpu.make_async_copy(source.at[me], outs[index].at[core, chip, me], local_sem.at[index])
        own.start()
        copies = []
        for step in range(1, groups):
            copy = pltpu.make_async_remote_copy(
                src_ref=source.at[peers[step - 1][1]],
                dst_ref=outs[index].at[core, chip, me],
                send_sem=send1.at[index, step],
                recv_sem=recv1.at[index, step],
                device_id=peers[step - 1],
                device_id_type=mesh_kind,
            )
            copy.start()
            copies.append(copy)
        first.append((own, copies))
    second = []
    for index in range(len(sources)):
        own, copies = first[index]
        own.wait()
        for copy in copies:
            copy.wait_recv()
        block = outs[index].at[core, chip]
        far = pltpu.make_async_remote_copy(
            src_ref=block, dst_ref=block, send_sem=xs_send.at[index], recv_sem=xs_recv.at[index],
            device_id=across, device_id_type=mesh_kind,
        )
        far.start()
        near = pltpu.make_async_remote_copy(
            src_ref=block, dst_ref=block, send_sem=cs_send.at[index], recv_sem=cs_recv.at[index],
            device_id=partner, device_id_type=mesh_kind,
        )
        near.start()
        second.append((far, near))
    third = []
    for index in range(len(sources)):
        far, near = second[index]
        far.wait_recv()
        relay = outs[index].at[core, 1 - chip]
        onward = pltpu.make_async_remote_copy(
            src_ref=relay, dst_ref=relay, send_sem=fw_send.at[index], recv_sem=fw_recv.at[index],
            device_id=partner, device_id_type=mesh_kind,
        )
        onward.start()
        third.append(onward)
    for index in range(len(sources)):
        own, copies = first[index]
        for copy in copies:
            copy.wait_send()
        far, near = second[index]
        far.wait_send()
        near.wait_send()
        near.wait_recv()
        third[index].wait_send()
        third[index].wait_recv()


def dispatch(wires):
    groups = wires[0].shape[0]
    count = len(wires)
    tail = wires[0].shape[1:]
    dma = pltpu.SemaphoreType.DMA
    return pl.pallas_call(
        functools.partial(dispatch_kernel, groups),
        out_shape=[jax.ShapeDtypeStruct((2, 2, groups) + tail, wires[0].dtype)] * count,
        in_specs=[pl.BlockSpec(memory_space=pl.ANY)] * count,
        out_specs=[pl.BlockSpec(memory_space=pl.ANY)] * count,
        scratch_shapes=[
            dma((count,)),
            dma((count, groups)),
            dma((count, groups)),
            dma((count,)),
            dma((count,)),
            dma((count,)),
            dma((count,)),
            dma((count,)),
            dma((count,)),
        ],
        compiler_params=pltpu.CompilerParams(collective_id=0, has_side_effects=True),
    )(*wires)


def to_wire(rows, *lead):
    return rows.reshape(*lead, -1, 128)


def return_kernel(groups, *refs):
    count = len(refs) - 4
    sources = refs[:count]
    out, local_sem, send1, recv1 = refs[count:]
    mesh_kind = pl.DeviceIdType.MESH
    pipe = lax.axis_index("pipe")
    me = lax.axis_index("eg")
    chip = lax.axis_index("ez")
    core = lax.axis_index("ec")
    peers = [(pipe, lax.rem(me + step, groups), chip, core) for step in range(1, groups)]
    barrier = pltpu.get_barrier_semaphore()
    for peer in peers:
        pl.semaphore_signal(barrier, 1, device_id=peer, device_id_type=mesh_kind)
    pl.semaphore_wait(barrier, len(peers))
    started = []
    for index, source in enumerate(sources):
        own = pltpu.make_async_copy(source.at[me], out.at[index, me], local_sem.at[index])
        own.start()
        copies = []
        for step in range(1, groups):
            copy = pltpu.make_async_remote_copy(
                src_ref=source.at[peers[step - 1][1]],
                dst_ref=out.at[index, me],
                send_sem=send1.at[index, step],
                recv_sem=recv1.at[index, step],
                device_id=peers[step - 1],
                device_id_type=mesh_kind,
            )
            copy.start()
            copies.append(copy)
        started.append((own, copies))
    for own, copies in started:
        own.wait()
        for copy in copies:
            copy.wait_send()
            copy.wait_recv()


def send_home(wires, tag):
    groups = wires[0].shape[0]
    count = len(wires)
    dma = pltpu.SemaphoreType.DMA
    return pl.pallas_call(
        functools.partial(return_kernel, groups),
        out_shape=jax.ShapeDtypeStruct((count,) + wires[0].shape, wires[0].dtype),
        in_specs=[pl.BlockSpec(memory_space=pl.ANY)] * count,
        out_specs=pl.BlockSpec(memory_space=pl.ANY),
        scratch_shapes=[dma((count,)), dma((count, groups)), dma((count, groups))],
        compiler_params=pltpu.CompilerParams(collective_id=tag, has_side_effects=True),
    )(*wires)


def group_sum(parts, experts):
    model_width = parts.shape[-1]
    blocks = parts.reshape(2, 2, -1, model_width)
    mine = lax.all_to_all(blocks, "ec", split_axis=0, concat_axis=0, tiled=True)
    pair = jnp.sum(mine.astype(jnp.float32), axis=0).astype(jnp.bfloat16)
    other = lax.all_to_all(pair, "ez", split_axis=0, concat_axis=0, tiled=True)
    summed = jnp.sum(other.astype(jnp.float32), axis=0).astype(jnp.bfloat16)
    return to_wire(summed, experts)


def expert_forward(rows, up_proj, down_proj):
    pre = jnp.einsum("...d,df->...f", rows, up_proj, preferred_element_type=jnp.float32)
    act = jax.nn.silu(pre).astype(jnp.bfloat16)
    return jnp.einsum(
        "...f,fd->...d", act, down_proj, preferred_element_type=jnp.float32
    ).astype(jnp.bfloat16)


def expert_backward(rows, grad_rows, up_proj, down_proj):
    pre = jnp.einsum("...d,df->...f", rows, up_proj, preferred_element_type=jnp.float32)
    act = jax.nn.silu(pre).astype(jnp.bfloat16)
    dact = jnp.einsum("...d,fd->...f", grad_rows, down_proj, preferred_element_type=jnp.float32)
    dpre = (dact * silu_grad(pre)).astype(jnp.bfloat16)
    dpart = jnp.einsum(
        "...f,df->...d", dpre, up_proj, preferred_element_type=jnp.float32
    ).astype(jnp.bfloat16)
    grad_up = jnp.einsum("rd,rf->df", rows, dpre, preferred_element_type=jnp.float32)
    grad_down = jnp.einsum("rf,rd->fd", act, grad_rows, preferred_element_type=jnp.float32)
    return (dpart, grad_up, grad_down)


def local(
    fwd_acts, fwd_routes, fwd_gates, back_acts, back_routes, back_gates, back_grads, w_up, w_down
):
    devices = lax.axis_size("eg") * GROUP
    experts = devices // GROUP
    tok_rows = fwd_acts.shape[1]
    top_count = fwd_routes.shape[2]
    slot_cap = GROUP * (5 * tok_rows * top_count // (4 * devices))
    up_proj = w_up[0, 0]
    down_proj = w_down[0, 0]
    fwd_input = fwd_acts[0]
    back_input = back_acts[0]
    out_grad = back_grads[0]
    plain_f, gated_f = tables(fwd_routes[0], fwd_gates[0], experts, slot_cap)
    plain_b, gated_b = tables(back_routes[0], back_gates[0], experts, slot_cap)
    buffer_f = gather_rows(plain_f, fwd_input)
    buffer_x = gather_rows(plain_b, back_input)
    buffer_g = lax.dot_general(
        gated_b, out_grad.astype(jnp.float32), (((0,), (0,)), ((), ())), precision=HIGH
    ).astype(jnp.bfloat16)
    model_width = fwd_input.shape[-1]
    got = dispatch([to_wire(b, experts) for b in (buffer_f, buffer_x, buffer_g)])
    got_f, got_x, got_g = [got[index].reshape(-1, model_width) for index in range(3)]
    part = expert_forward(got_f, up_proj, down_proj)
    wire_f = group_sum(part, experts)
    dpart, grad_up, grad_down = expert_backward(got_x, got_g, up_proj, down_proj)
    wire_b = group_sum(dpart, experts)
    summed_f = send_home([wire_f], 1)[0].reshape(-1, model_width).astype(jnp.float32)
    summed_b = send_home([wire_b], 2)[0].reshape(-1, model_width).astype(jnp.float32)
    merged = jnp.dot(gated_f, summed_f, precision=HIGH)
    section_out = (fwd_input.astype(jnp.float32) + merged).astype(jnp.bfloat16)
    spread_back = jnp.dot(plain_b, summed_b, precision=HIGH)
    section_grad = (out_grad.astype(jnp.float32) + spread_back).astype(jnp.bfloat16)
    fwd_next = passed_along(section_out[None], "pipe", 1)
    back_next = passed_along(section_grad[None], "pipe", -1)
    return (fwd_next, back_next, grad_up[None, None], grad_down[None, None])


def solution(mesh):
    groups = mesh.shape["expert"] // GROUP
    devices = mesh.devices.reshape(mesh.shape["pipe"], groups, 2, GROUP // 2)
    mesh = jax.sharding.Mesh(devices, ("pipe", "eg", "ez", "ec"))
    in_specs = (
        P("pipe", ("eg", "ez", "ec"), None),
        P("pipe", ("eg", "ez", "ec"), None),
        P("pipe", ("eg", "ez", "ec"), None),
        P("pipe", ("eg", "ez", "ec"), None),
        P("pipe", ("eg", "ez", "ec"), None),
        P("pipe", ("eg", "ez", "ec"), None),
        P("pipe", ("eg", "ez", "ec"), None),
        P("pipe", ("eg", "ez", "ec"), None, None),
        P("pipe", ("eg", "ez", "ec"), None, None),
    )
    out_specs = (
        P("pipe", ("eg", "ez", "ec"), None),
        P("pipe", ("eg", "ez", "ec"), None),
        P("pipe", ("eg", "ez", "ec"), None, None),
        P("pipe", ("eg", "ez", "ec"), None, None),
    )
    return jax.shard_map(local, mesh=mesh, in_specs=in_specs, out_specs=out_specs, check_vma=False)
```

```python
import jax
import jax.numpy as jnp
from jax import lax
from jax.sharding import PartitionSpec as P
from jax.experimental import pallas as pl
from jax.experimental.pallas import tpu as pltpu
import functools

GROUP = 4


HIGH = lax.Precision.HIGHEST


def passed_along(value, axis, steps):
    count = lax.axis_size(axis)
    pairs = [(source, (source + steps) % count) for source in range(count)]
    return lax.ppermute(value, axis, pairs)


def silu_grad(value):
    sigma = jax.nn.sigmoid(value)
    return sigma * (1.0 + value * (1.0 - sigma))


def tables(routes, gates, experts, slot_cap):
    tok_rows, top_count = routes.shape
    flat = routes.reshape(tok_rows * top_count)
    onehot = (flat[:, None] == jnp.arange(experts, dtype=jnp.int32)[None, :]).astype(jnp.int32)
    before = jnp.cumsum(onehot, axis=0) - onehot
    slots = jnp.sum(before * onehot, axis=1)
    places = flat * slot_cap + slots
    columns = jnp.arange(experts * slot_cap, dtype=jnp.int32)
    hits = (
        (places[:, None] == columns[None, :])
        .astype(jnp.float32)
        .reshape(tok_rows, top_count, experts * slot_cap)
    )
    plain = jnp.sum(hits, axis=1)
    gated = jnp.sum(hits * gates[:, :, None], axis=1)
    return (plain, gated)


def gather_rows(plain, values):
    return lax.dot_general(
        plain.astype(jnp.bfloat16),
        values,
        (((0,), (0,)), ((), ())),
        preferred_element_type=jnp.float32,
    ).astype(jnp.bfloat16)


def to_wire(rows, *lead):
    return rows.reshape(*lead, -1, 128)


def dispatch_kernel(groups, *refs):
    sources = refs[:3]
    outs = refs[3:6]
    local_sem, send1, recv1, xs_send, xs_recv, cs_send, cs_recv, fw_send, fw_recv = refs[6:]
    mesh_kind = pl.DeviceIdType.MESH
    pipe = lax.axis_index("pipe")
    me = lax.axis_index("eg")
    chip = lax.axis_index("ez")
    core = lax.axis_index("ec")
    across = (pipe, me, 1 - chip, core)
    partner = (pipe, me, chip, 1 - core)
    peers = [(pipe, lax.rem(me + step, groups), chip, core) for step in range(1, groups)]
    barrier = pltpu.get_barrier_semaphore()
    for peer in peers + [across, partner]:
        pl.semaphore_signal(barrier, 1, device_id=peer, device_id_type=mesh_kind)
    pl.semaphore_wait(barrier, len(peers) + 2)
    first = []
    for index, source in enumerate(sources):
        own = pltpu.make_async_copy(source.at[me], outs[index].at[chip, core, me], local_sem.at[index])
        own.start()
        copies = []
        for step in range(1, groups):
            copy = pltpu.make_async_remote_copy(
                src_ref=source.at[peers[step - 1][1]],
                dst_ref=outs[index].at[chip, core, me],
                send_sem=send1.at[index, step],
                recv_sem=recv1.at[index, step],
                device_id=peers[step - 1],
                device_id_type=mesh_kind,
            )
            copy.start()
            copies.append(copy)
        first.append((own, copies))
    second = []
    for index in range(len(sources)):
        own, copies = first[index]
        own.wait()
        for copy in copies:
            copy.wait_recv()
        block = outs[index].at[chip, core]
        far = pltpu.make_async_remote_copy(
            src_ref=block, dst_ref=block, send_sem=xs_send.at[index], recv_sem=xs_recv.at[index],
            device_id=across, device_id_type=mesh_kind,
        )
        far.start()
        near = pltpu.make_async_remote_copy(
            src_ref=block, dst_ref=block, send_sem=cs_send.at[index], recv_sem=cs_recv.at[index],
            device_id=partner, device_id_type=mesh_kind,
        )
        near.start()
        second.append((far, near))
    third = []
    for index in range(len(sources)):
        far, near = second[index]
        far.wait_recv()
        relay = outs[index].at[1 - chip, core]
        onward = pltpu.make_async_remote_copy(
            src_ref=relay, dst_ref=relay, send_sem=fw_send.at[index], recv_sem=fw_recv.at[index],
            device_id=partner, device_id_type=mesh_kind,
        )
        onward.start()
        third.append(onward)
    for index in range(len(sources)):
        own, copies = first[index]
        for copy in copies:
            copy.wait_send()
        far, near = second[index]
        far.wait_send()
        near.wait_send()
        near.wait_recv()
        third[index].wait_send()
        third[index].wait_recv()


def dispatch(wires):
    groups = wires[0].shape[0]
    count = len(wires)
    tail = wires[0].shape[1:]
    dma = pltpu.SemaphoreType.DMA
    return pl.pallas_call(
        functools.partial(dispatch_kernel, groups),
        out_shape=[jax.ShapeDtypeStruct((2, 2, groups) + tail, wires[0].dtype)] * count,
        in_specs=[pl.BlockSpec(memory_space=pl.ANY)] * count,
        out_specs=[pl.BlockSpec(memory_space=pl.ANY)] * count,
        scratch_shapes=[
            dma((count,)),
            dma((count, groups)),
            dma((count, groups)),
            dma((count,)),
            dma((count,)),
            dma((count,)),
            dma((count,)),
            dma((count,)),
            dma((count,)),
        ],
        compiler_params=pltpu.CompilerParams(collective_id=0, has_side_effects=True),
    )(*wires)


def to_wire(rows, *lead):
    return rows.reshape(*lead, -1, 128)


def return_kernel(groups, *refs):
    count = len(refs) - 4
    sources = refs[:count]
    out, local_sem, send1, recv1 = refs[count:]
    mesh_kind = pl.DeviceIdType.MESH
    pipe = lax.axis_index("pipe")
    me = lax.axis_index("eg")
    chip = lax.axis_index("ez")
    core = lax.axis_index("ec")
    peers = [(pipe, lax.rem(me + step, groups), chip, core) for step in range(1, groups)]
    barrier = pltpu.get_barrier_semaphore()
    for peer in peers:
        pl.semaphore_signal(barrier, 1, device_id=peer, device_id_type=mesh_kind)
    pl.semaphore_wait(barrier, len(peers))
    started = []
    for index, source in enumerate(sources):
        own = pltpu.make_async_copy(source.at[me], out.at[index, me], local_sem.at[index])
        own.start()
        copies = []
        for step in range(1, groups):
            copy = pltpu.make_async_remote_copy(
                src_ref=source.at[peers[step - 1][1]],
                dst_ref=out.at[index, me],
                send_sem=send1.at[index, step],
                recv_sem=recv1.at[index, step],
                device_id=peers[step - 1],
                device_id_type=mesh_kind,
            )
            copy.start()
            copies.append(copy)
        started.append((own, copies))
    for own, copies in started:
        own.wait()
        for copy in copies:
            copy.wait_send()
            copy.wait_recv()


def send_home(wires, tag):
    groups = wires[0].shape[0]
    count = len(wires)
    dma = pltpu.SemaphoreType.DMA
    return pl.pallas_call(
        functools.partial(return_kernel, groups),
        out_shape=jax.ShapeDtypeStruct((count,) + wires[0].shape, wires[0].dtype),
        in_specs=[pl.BlockSpec(memory_space=pl.ANY)] * count,
        out_specs=pl.BlockSpec(memory_space=pl.ANY),
        scratch_shapes=[dma((count,)), dma((count, groups)), dma((count, groups))],
        compiler_params=pltpu.CompilerParams(collective_id=tag, has_side_effects=True),
    )(*wires)


def group_sum(parts, experts):
    model_width = parts.shape[-1]
    blocks = parts.reshape(GROUP, -1, model_width)
    summed = lax.psum_scatter(blocks, ("ez", "ec"), scatter_dimension=0, tiled=True)
    return to_wire(summed.reshape(-1, model_width), experts)


def expert_forward(rows, up_proj, down_proj):
    pre = jnp.einsum("...d,df->...f", rows, up_proj, preferred_element_type=jnp.float32)
    act = jax.nn.silu(pre).astype(jnp.bfloat16)
    return jnp.einsum(
        "...f,fd->...d", act, down_proj, preferred_element_type=jnp.float32
    ).astype(jnp.bfloat16)


def expert_backward(rows, grad_rows, up_proj, down_proj):
    pre = jnp.einsum("...d,df->...f", rows, up_proj, preferred_element_type=jnp.float32)
    act = jax.nn.silu(pre).astype(jnp.bfloat16)
    dact = jnp.einsum("...d,fd->...f", grad_rows, down_proj, preferred_element_type=jnp.float32)
    dpre = (dact * silu_grad(pre)).astype(jnp.bfloat16)
    dpart = jnp.einsum(
        "...f,df->...d", dpre, up_proj, preferred_element_type=jnp.float32
    ).astype(jnp.bfloat16)
    grad_up = jnp.einsum("rd,rf->df", rows, dpre, preferred_element_type=jnp.float32)
    grad_down = jnp.einsum("rf,rd->fd", act, grad_rows, preferred_element_type=jnp.float32)
    return (dpart, grad_up, grad_down)


def local(
    fwd_acts, fwd_routes, fwd_gates, back_acts, back_routes, back_gates, back_grads, w_up, w_down
):
    devices = lax.axis_size("eg") * GROUP
    experts = devices // GROUP
    tok_rows = fwd_acts.shape[1]
    top_count = fwd_routes.shape[2]
    slot_cap = GROUP * (5 * tok_rows * top_count // (4 * devices))
    up_proj = w_up[0, 0]
    down_proj = w_down[0, 0]
    fwd_input = fwd_acts[0]
    back_input = back_acts[0]
    out_grad = back_grads[0]
    plain_f, gated_f = tables(fwd_routes[0], fwd_gates[0], experts, slot_cap)
    plain_b, gated_b = tables(back_routes[0], back_gates[0], experts, slot_cap)
    buffer_f = gather_rows(plain_f, fwd_input)
    buffer_x = gather_rows(plain_b, back_input)
    buffer_g = lax.dot_general(
        gated_b, out_grad.astype(jnp.float32), (((0,), (0,)), ((), ())), precision=HIGH
    ).astype(jnp.bfloat16)
    model_width = fwd_input.shape[-1]
    got = dispatch([to_wire(b, experts) for b in (buffer_f, buffer_x, buffer_g)])
    got_f, got_x, got_g = [got[index].reshape(-1, model_width) for index in range(3)]
    part = expert_forward(got_f, up_proj, down_proj)
    wire_f = group_sum(part, experts)
    dpart, grad_up, grad_down = expert_backward(got_x, got_g, up_proj, down_proj)
    wire_b = group_sum(dpart, experts)
    summed_f = send_home([wire_f], 1)[0].reshape(-1, model_width).astype(jnp.float32)
    summed_b = send_home([wire_b], 2)[0].reshape(-1, model_width).astype(jnp.float32)
    merged = jnp.dot(gated_f, summed_f, precision=HIGH)
    section_out = (fwd_input.astype(jnp.float32) + merged).astype(jnp.bfloat16)
    spread_back = jnp.dot(plain_b, summed_b, precision=HIGH)
    section_grad = (out_grad.astype(jnp.float32) + spread_back).astype(jnp.bfloat16)
    fwd_next = passed_along(section_out[None], "pipe", 1)
    back_next = passed_along(section_grad[None], "pipe", -1)
    return (fwd_next, back_next, grad_up[None, None], grad_down[None, None])


def solution(mesh):
    groups = mesh.shape["expert"] // GROUP
    devices = mesh.devices.reshape(mesh.shape["pipe"], groups, 2, GROUP // 2)
    mesh = jax.sharding.Mesh(devices, ("pipe", "eg", "ez", "ec"))
    in_specs = (
        P("pipe", ("eg", "ez", "ec"), None),
        P("pipe", ("eg", "ez", "ec"), None),
        P("pipe", ("eg", "ez", "ec"), None),
        P("pipe", ("eg", "ez", "ec"), None),
        P("pipe", ("eg", "ez", "ec"), None),
        P("pipe", ("eg", "ez", "ec"), None),
        P("pipe", ("eg", "ez", "ec"), None),
        P("pipe", ("eg", "ez", "ec"), None, None),
        P("pipe", ("eg", "ez", "ec"), None, None),
    )
    out_specs = (
        P("pipe", ("eg", "ez", "ec"), None),
        P("pipe", ("eg", "ez", "ec"), None),
        P("pipe", ("eg", "ez", "ec"), None, None),
        P("pipe", ("eg", "ez", "ec"), None, None),
    )
    return jax.shard_map(local, mesh=mesh, in_specs=in_specs, out_specs=out_specs, check_vma=False)
```

```python
import jax
import jax.numpy as jnp
from jax import lax
from jax.sharding import PartitionSpec as P
from jax.experimental import pallas as pl
from jax.experimental.pallas import tpu as pltpu
import functools

GROUP = 4


HIGH = lax.Precision.HIGHEST


def passed_along(value, axis, steps):
    count = lax.axis_size(axis)
    pairs = [(source, (source + steps) % count) for source in range(count)]
    return lax.ppermute(value, axis, pairs)


def silu_grad(value):
    sigma = jax.nn.sigmoid(value)
    return sigma * (1.0 + value * (1.0 - sigma))


def tables(routes, gates, experts, slot_cap):
    tok_rows, top_count = routes.shape
    flat = routes.reshape(tok_rows * top_count)
    onehot = (flat[:, None] == jnp.arange(experts, dtype=jnp.int32)[None, :]).astype(jnp.int32)
    before = jnp.cumsum(onehot, axis=0) - onehot
    slots = jnp.sum(before * onehot, axis=1)
    places = flat * slot_cap + slots
    columns = jnp.arange(experts * slot_cap, dtype=jnp.int32)
    hits = (
        (places[:, None] == columns[None, :])
        .astype(jnp.float32)
        .reshape(tok_rows, top_count, experts * slot_cap)
    )
    plain = jnp.sum(hits, axis=1)
    gated = jnp.sum(hits * gates[:, :, None], axis=1)
    return (plain, gated)


def gather_rows(plain, values):
    return lax.dot_general(
        plain.astype(jnp.bfloat16),
        values,
        (((0,), (0,)), ((), ())),
        preferred_element_type=jnp.float32,
    ).astype(jnp.bfloat16)


def to_wire(rows, *lead):
    return rows.reshape(*lead, -1, 128)


def dispatch_kernel(groups, *refs):
    sources = refs[:3]
    outs = refs[3:6]
    local_sem, send1, recv1, xs_send, xs_recv, cs_send, cs_recv, fw_send, fw_recv = refs[6:]
    mesh_kind = pl.DeviceIdType.MESH
    pipe = lax.axis_index("pipe")
    me = lax.axis_index("eg")
    chip = lax.axis_index("ez")
    core = lax.axis_index("ec")
    across = (pipe, me, 1 - chip, core)
    partner = (pipe, me, chip, 1 - core)
    peers = [(pipe, lax.rem(me + step, groups), chip, core) for step in range(1, groups)]
    barrier = pltpu.get_barrier_semaphore()
    for peer in peers + [across, partner]:
        pl.semaphore_signal(barrier, 1, device_id=peer, device_id_type=mesh_kind)
    pl.semaphore_wait(barrier, len(peers) + 2)
    def launch(index):
        source = sources[index]
        own = pltpu.make_async_copy(source.at[me], outs[index].at[core, chip, me], local_sem.at[index])
        own.start()
        copies = []
        for step in range(1, groups):
            copy = pltpu.make_async_remote_copy(
                src_ref=source.at[peers[step - 1][1]],
                dst_ref=outs[index].at[core, chip, me],
                send_sem=send1.at[index, step],
                recv_sem=recv1.at[index, step],
                device_id=peers[step - 1],
                device_id_type=mesh_kind,
            )
            copy.start()
            copies.append(copy)
        return own, copies

    def relay(index, far):
        far.wait_recv()
        held = outs[index].at[core, 1 - chip]
        onward = pltpu.make_async_remote_copy(
            src_ref=held, dst_ref=held, send_sem=fw_send.at[index], recv_sem=fw_recv.at[index],
            device_id=partner, device_id_type=mesh_kind,
        )
        onward.start()
        return onward

    count = len(sources)
    first = [launch(0)]
    second = []
    third = []
    for index in range(count):
        own, copies = first[index]
        own.wait()
        for copy in copies:
            copy.wait_recv()
        if index + 1 < count:
            first.append(launch(index + 1))
        block = outs[index].at[core, chip]
        far = pltpu.make_async_remote_copy(
            src_ref=block, dst_ref=block, send_sem=xs_send.at[index], recv_sem=xs_recv.at[index],
            device_id=across, device_id_type=mesh_kind,
        )
        far.start()
        near = pltpu.make_async_remote_copy(
            src_ref=block, dst_ref=block, send_sem=cs_send.at[index], recv_sem=cs_recv.at[index],
            device_id=partner, device_id_type=mesh_kind,
        )
        near.start()
        second.append((far, near))
        if index >= 1:
            third.append(relay(index - 1, second[index - 1][0]))
    third.append(relay(count - 1, second[count - 1][0]))
    for index in range(count):
        own, copies = first[index]
        for copy in copies:
            copy.wait_send()
        far, near = second[index]
        far.wait_send()
        near.wait_send()
        near.wait_recv()
        third[index].wait_send()
        third[index].wait_recv()


def dispatch(wires):
    groups = wires[0].shape[0]
    count = len(wires)
    tail = wires[0].shape[1:]
    dma = pltpu.SemaphoreType.DMA
    return pl.pallas_call(
        functools.partial(dispatch_kernel, groups),
        out_shape=[jax.ShapeDtypeStruct((2, 2, groups) + tail, wires[0].dtype)] * count,
        in_specs=[pl.BlockSpec(memory_space=pl.ANY)] * count,
        out_specs=[pl.BlockSpec(memory_space=pl.ANY)] * count,
        scratch_shapes=[
            dma((count,)),
            dma((count, groups)),
            dma((count, groups)),
            dma((count,)),
            dma((count,)),
            dma((count,)),
            dma((count,)),
            dma((count,)),
            dma((count,)),
        ],
        compiler_params=pltpu.CompilerParams(collective_id=0, has_side_effects=True),
    )(*wires)


def to_wire(rows, *lead):
    return rows.reshape(*lead, -1, 128)


def return_kernel(groups, *refs):
    count = len(refs) - 4
    sources = refs[:count]
    out, local_sem, send1, recv1 = refs[count:]
    mesh_kind = pl.DeviceIdType.MESH
    pipe = lax.axis_index("pipe")
    me = lax.axis_index("eg")
    chip = lax.axis_index("ez")
    core = lax.axis_index("ec")
    peers = [(pipe, lax.rem(me + step, groups), chip, core) for step in range(1, groups)]
    barrier = pltpu.get_barrier_semaphore()
    for peer in peers:
        pl.semaphore_signal(barrier, 1, device_id=peer, device_id_type=mesh_kind)
    pl.semaphore_wait(barrier, len(peers))
    started = []
    for index, source in enumerate(sources):
        own = pltpu.make_async_copy(source.at[me], out.at[index, me], local_sem.at[index])
        own.start()
        copies = []
        for step in range(1, groups):
            copy = pltpu.make_async_remote_copy(
                src_ref=source.at[peers[step - 1][1]],
                dst_ref=out.at[index, me],
                send_sem=send1.at[index, step],
                recv_sem=recv1.at[index, step],
                device_id=peers[step - 1],
                device_id_type=mesh_kind,
            )
            copy.start()
            copies.append(copy)
        started.append((own, copies))
    for own, copies in started:
        own.wait()
        for copy in copies:
            copy.wait_send()
            copy.wait_recv()


def send_home(wires, tag):
    groups = wires[0].shape[0]
    count = len(wires)
    dma = pltpu.SemaphoreType.DMA
    return pl.pallas_call(
        functools.partial(return_kernel, groups),
        out_shape=jax.ShapeDtypeStruct((count,) + wires[0].shape, wires[0].dtype),
        in_specs=[pl.BlockSpec(memory_space=pl.ANY)] * count,
        out_specs=pl.BlockSpec(memory_space=pl.ANY),
        scratch_shapes=[dma((count,)), dma((count, groups)), dma((count, groups))],
        compiler_params=pltpu.CompilerParams(collective_id=tag, has_side_effects=True),
    )(*wires)


def group_sum(parts, experts):
    model_width = parts.shape[-1]
    blocks = parts.reshape(2, 2, -1, model_width)
    mine = lax.all_to_all(blocks, "ec", split_axis=0, concat_axis=0, tiled=True)
    pair = jnp.sum(mine.astype(jnp.float32), axis=0).astype(jnp.bfloat16)
    other = lax.all_to_all(pair, "ez", split_axis=0, concat_axis=0, tiled=True)
    summed = jnp.sum(other.astype(jnp.float32), axis=0).astype(jnp.bfloat16)
    return to_wire(summed, experts)


def expert_forward(rows, up_proj, down_proj):
    pre = jnp.einsum("...d,df->...f", rows, up_proj, preferred_element_type=jnp.float32)
    act = jax.nn.silu(pre).astype(jnp.bfloat16)
    return jnp.einsum(
        "...f,fd->...d", act, down_proj, preferred_element_type=jnp.float32
    ).astype(jnp.bfloat16)


def expert_backward(rows, grad_rows, up_proj, down_proj):
    pre = jnp.einsum("...d,df->...f", rows, up_proj, preferred_element_type=jnp.float32)
    act = jax.nn.silu(pre).astype(jnp.bfloat16)
    dact = jnp.einsum("...d,fd->...f", grad_rows, down_proj, preferred_element_type=jnp.float32)
    dpre = (dact * silu_grad(pre)).astype(jnp.bfloat16)
    dpart = jnp.einsum(
        "...f,df->...d", dpre, up_proj, preferred_element_type=jnp.float32
    ).astype(jnp.bfloat16)
    grad_up = jnp.einsum("rd,rf->df", rows, dpre, preferred_element_type=jnp.float32)
    grad_down = jnp.einsum("rf,rd->fd", act, grad_rows, preferred_element_type=jnp.float32)
    return (dpart, grad_up, grad_down)


def local(
    fwd_acts, fwd_routes, fwd_gates, back_acts, back_routes, back_gates, back_grads, w_up, w_down
):
    devices = lax.axis_size("eg") * GROUP
    experts = devices // GROUP
    tok_rows = fwd_acts.shape[1]
    top_count = fwd_routes.shape[2]
    slot_cap = GROUP * (5 * tok_rows * top_count // (4 * devices))
    up_proj = w_up[0, 0]
    down_proj = w_down[0, 0]
    fwd_input = fwd_acts[0]
    back_input = back_acts[0]
    out_grad = back_grads[0]
    plain_f, gated_f = tables(fwd_routes[0], fwd_gates[0], experts, slot_cap)
    plain_b, gated_b = tables(back_routes[0], back_gates[0], experts, slot_cap)
    buffer_f = gather_rows(plain_f, fwd_input)
    buffer_x = gather_rows(plain_b, back_input)
    buffer_g = lax.dot_general(
        gated_b, out_grad.astype(jnp.float32), (((0,), (0,)), ((), ())), precision=HIGH
    ).astype(jnp.bfloat16)
    model_width = fwd_input.shape[-1]
    got = dispatch([to_wire(b, experts) for b in (buffer_f, buffer_x, buffer_g)])
    got_f, got_x, got_g = [got[index].reshape(-1, model_width) for index in range(3)]
    part = expert_forward(got_f, up_proj, down_proj)
    wire_f = group_sum(part, experts)
    dpart, grad_up, grad_down = expert_backward(got_x, got_g, up_proj, down_proj)
    wire_b = group_sum(dpart, experts)
    summed_f = send_home([wire_f], 1)[0].reshape(-1, model_width).astype(jnp.float32)
    summed_b = send_home([wire_b], 2)[0].reshape(-1, model_width).astype(jnp.float32)
    merged = jnp.dot(gated_f, summed_f, precision=HIGH)
    section_out = (fwd_input.astype(jnp.float32) + merged).astype(jnp.bfloat16)
    spread_back = jnp.dot(plain_b, summed_b, precision=HIGH)
    section_grad = (out_grad.astype(jnp.float32) + spread_back).astype(jnp.bfloat16)
    fwd_next = passed_along(section_out[None], "pipe", 1)
    back_next = passed_along(section_grad[None], "pipe", -1)
    return (fwd_next, back_next, grad_up[None, None], grad_down[None, None])


def solution(mesh):
    groups = mesh.shape["expert"] // GROUP
    devices = mesh.devices.reshape(mesh.shape["pipe"], groups, 2, GROUP // 2)
    mesh = jax.sharding.Mesh(devices, ("pipe", "eg", "ez", "ec"))
    in_specs = (
        P("pipe", ("eg", "ez", "ec"), None),
        P("pipe", ("eg", "ez", "ec"), None),
        P("pipe", ("eg", "ez", "ec"), None),
        P("pipe", ("eg", "ez", "ec"), None),
        P("pipe", ("eg", "ez", "ec"), None),
        P("pipe", ("eg", "ez", "ec"), None),
        P("pipe", ("eg", "ez", "ec"), None),
        P("pipe", ("eg", "ez", "ec"), None, None),
        P("pipe", ("eg", "ez", "ec"), None, None),
    )
    out_specs = (
        P("pipe", ("eg", "ez", "ec"), None),
        P("pipe", ("eg", "ez", "ec"), None),
        P("pipe", ("eg", "ez", "ec"), None, None),
        P("pipe", ("eg", "ez", "ec"), None, None),
    )
    return jax.shard_map(local, mesh=mesh, in_specs=in_specs, out_specs=out_specs, check_vma=False)
```

```python
import jax
import jax.numpy as jnp
from jax import lax
from jax.sharding import PartitionSpec as P
from jax.experimental import pallas as pl
from jax.experimental.pallas import tpu as pltpu
import functools

GROUP = 4


HIGH = lax.Precision.HIGHEST


def passed_along(value, axis, steps):
    count = lax.axis_size(axis)
    pairs = [(source, (source + steps) % count) for source in range(count)]
    return lax.ppermute(value, axis, pairs)


def silu_grad(value):
    sigma = jax.nn.sigmoid(value)
    return sigma * (1.0 + value * (1.0 - sigma))


def tables(routes, gates, experts, slot_cap):
    tok_rows, top_count = routes.shape
    flat = routes.reshape(tok_rows * top_count)
    onehot = (flat[:, None] == jnp.arange(experts, dtype=jnp.int32)[None, :]).astype(jnp.int32)
    before = jnp.cumsum(onehot, axis=0) - onehot
    slots = jnp.sum(before * onehot, axis=1)
    places = flat * slot_cap + slots
    columns = jnp.arange(experts * slot_cap, dtype=jnp.int32)
    hits = (
        (places[:, None] == columns[None, :])
        .astype(jnp.float32)
        .reshape(tok_rows, top_count, experts * slot_cap)
    )
    plain = jnp.sum(hits, axis=1)
    gated = jnp.sum(hits * gates[:, :, None], axis=1)
    return (plain, gated)


def gather_rows(plain, values):
    return lax.dot_general(
        plain.astype(jnp.bfloat16),
        values,
        (((0,), (0,)), ((), ())),
        preferred_element_type=jnp.float32,
    ).astype(jnp.bfloat16)


def split_slots(table, experts, slot_cap, main):
    lead = table.shape[0]
    shaped = table.reshape(lead, experts, slot_cap)
    return (shaped[:, :, :main].reshape(lead, -1), shaped[:, :, main:].reshape(lead, -1))


def to_wire(rows, *lead):
    return rows.reshape(*lead, -1, 128)


def dispatch_kernel(groups, *refs):
    count = (len(refs) - 9) // 2
    sources = refs[:count]
    outs = refs[count:2 * count]
    local_sem, send1, recv1, xs_send, xs_recv, cs_send, cs_recv, fw_send, fw_recv = refs[2 * count:]
    mesh_kind = pl.DeviceIdType.MESH
    pipe = lax.axis_index("pipe")
    me = lax.axis_index("eg")
    chip = lax.axis_index("ez")
    core = lax.axis_index("ec")
    across = (pipe, me, 1 - chip, core)
    partner = (pipe, me, chip, 1 - core)
    peers = [(pipe, lax.rem(me + step, groups), chip, core) for step in range(1, groups)]
    barrier = pltpu.get_barrier_semaphore()
    for peer in peers + [across, partner]:
        pl.semaphore_signal(barrier, 1, device_id=peer, device_id_type=mesh_kind)
    pl.semaphore_wait(barrier, len(peers) + 2)
    def launch(index):
        source = sources[index]
        own = pltpu.make_async_copy(source.at[me], outs[index].at[core, chip, me], local_sem.at[index])
        own.start()
        copies = []
        for step in range(1, groups):
            copy = pltpu.make_async_remote_copy(
                src_ref=source.at[peers[step - 1][1]],
                dst_ref=outs[index].at[core, chip, me],
                send_sem=send1.at[index, step],
                recv_sem=recv1.at[index, step],
                device_id=peers[step - 1],
                device_id_type=mesh_kind,
            )
            copy.start()
            copies.append(copy)
        return own, copies

    def relay(index, far):
        far.wait_recv()
        held = outs[index].at[core, 1 - chip]
        onward = pltpu.make_async_remote_copy(
            src_ref=held, dst_ref=held, send_sem=fw_send.at[index], recv_sem=fw_recv.at[index],
            device_id=partner, device_id_type=mesh_kind,
        )
        onward.start()
        return onward

    count = len(sources)
    first = [launch(0)]
    second = []
    third = []
    for index in range(count):
        own, copies = first[index]
        own.wait()
        for copy in copies:
            copy.wait_recv()
        if index + 1 < count:
            first.append(launch(index + 1))
        block = outs[index].at[core, chip]
        far = pltpu.make_async_remote_copy(
            src_ref=block, dst_ref=block, send_sem=xs_send.at[index], recv_sem=xs_recv.at[index],
            device_id=across, device_id_type=mesh_kind,
        )
        far.start()
        near = pltpu.make_async_remote_copy(
            src_ref=block, dst_ref=block, send_sem=cs_send.at[index], recv_sem=cs_recv.at[index],
            device_id=partner, device_id_type=mesh_kind,
        )
        near.start()
        second.append((far, near))
        if index >= 1:
            third.append(relay(index - 1, second[index - 1][0]))
    third.append(relay(count - 1, second[count - 1][0]))
    for index in range(count):
        own, copies = first[index]
        for copy in copies:
            copy.wait_send()
        far, near = second[index]
        far.wait_send()
        near.wait_send()
        near.wait_recv()
        third[index].wait_send()
        third[index].wait_recv()


def dispatch(wires):
    groups = wires[0].shape[0]
    count = len(wires)
    dma = pltpu.SemaphoreType.DMA
    return pl.pallas_call(
        functools.partial(dispatch_kernel, groups),
        out_shape=[jax.ShapeDtypeStruct((2, 2) + wire.shape, wire.dtype) for wire in wires],
        in_specs=[pl.BlockSpec(memory_space=pl.ANY)] * count,
        out_specs=[pl.BlockSpec(memory_space=pl.ANY)] * count,
        scratch_shapes=[
            dma((count,)),
            dma((count, groups)),
            dma((count, groups)),
            dma((count,)),
            dma((count,)),
            dma((count,)),
            dma((count,)),
            dma((count,)),
            dma((count,)),
        ],
        compiler_params=pltpu.CompilerParams(collective_id=0, has_side_effects=True),
    )(*wires)


def split_slots(table, experts, slot_cap, main):
    lead = table.shape[0]
    shaped = table.reshape(lead, experts, slot_cap)
    return (shaped[:, :, :main].reshape(lead, -1), shaped[:, :, main:].reshape(lead, -1))


def to_wire(rows, *lead):
    return rows.reshape(*lead, -1, 128)


def return_kernel(groups, *refs):
    count = (len(refs) - 3) // 2
    sources = refs[:count]
    outs = refs[count:2 * count]
    local_sem, send1, recv1 = refs[2 * count:]
    mesh_kind = pl.DeviceIdType.MESH
    pipe = lax.axis_index("pipe")
    me = lax.axis_index("eg")
    chip = lax.axis_index("ez")
    core = lax.axis_index("ec")
    peers = [(pipe, lax.rem(me + step, groups), chip, core) for step in range(1, groups)]
    barrier = pltpu.get_barrier_semaphore()
    for peer in peers:
        pl.semaphore_signal(barrier, 1, device_id=peer, device_id_type=mesh_kind)
    pl.semaphore_wait(barrier, len(peers))
    started = []
    for index, source in enumerate(sources):
        own = pltpu.make_async_copy(source.at[me], outs[index].at[me], local_sem.at[index])
        own.start()
        copies = []
        for step in range(1, groups):
            copy = pltpu.make_async_remote_copy(
                src_ref=source.at[peers[step - 1][1]],
                dst_ref=outs[index].at[me],
                send_sem=send1.at[index, step],
                recv_sem=recv1.at[index, step],
                device_id=peers[step - 1],
                device_id_type=mesh_kind,
            )
            copy.start()
            copies.append(copy)
        started.append((own, copies))
    for own, copies in started:
        own.wait()
        for copy in copies:
            copy.wait_send()
            copy.wait_recv()


def send_home(wires, tag):
    groups = wires[0].shape[0]
    count = len(wires)
    dma = pltpu.SemaphoreType.DMA
    return pl.pallas_call(
        functools.partial(return_kernel, groups),
        out_shape=[jax.ShapeDtypeStruct(wire.shape, wire.dtype) for wire in wires],
        in_specs=[pl.BlockSpec(memory_space=pl.ANY)] * count,
        out_specs=[pl.BlockSpec(memory_space=pl.ANY)] * count,
        scratch_shapes=[dma((count,)), dma((count, groups)), dma((count, groups))],
        compiler_params=pltpu.CompilerParams(collective_id=tag, has_side_effects=True),
    )(*wires)


def group_sum(parts):
    model_width = parts.shape[-1]
    blocks = parts.reshape(2, 2, -1, model_width)
    mine = lax.all_to_all(blocks, "ec", split_axis=0, concat_axis=0, tiled=True)
    pair = jnp.sum(mine.astype(jnp.float32), axis=0).astype(jnp.bfloat16)
    other = lax.all_to_all(pair, "ez", split_axis=0, concat_axis=0, tiled=True)
    return jnp.sum(other.astype(jnp.float32), axis=0).astype(jnp.bfloat16)


def expert_forward(rows, up_proj, down_proj):
    pre = jnp.einsum("...d,df->...f", rows, up_proj, preferred_element_type=jnp.float32)
    act = jax.nn.silu(pre).astype(jnp.bfloat16)
    return jnp.einsum(
        "...f,fd->...d", act, down_proj, preferred_element_type=jnp.float32
    ).astype(jnp.bfloat16)


def expert_backward(rows, grad_rows, up_proj, down_proj):
    pre = jnp.einsum("...d,df->...f", rows, up_proj, preferred_element_type=jnp.float32)
    act = jax.nn.silu(pre).astype(jnp.bfloat16)
    dact = jnp.einsum("...d,fd->...f", grad_rows, down_proj, preferred_element_type=jnp.float32)
    dpre = (dact * silu_grad(pre)).astype(jnp.bfloat16)
    dpart = jnp.einsum(
        "...f,df->...d", dpre, up_proj, preferred_element_type=jnp.float32
    ).astype(jnp.bfloat16)
    grad_up = jnp.einsum("rd,rf->df", rows, dpre, preferred_element_type=jnp.float32)
    grad_down = jnp.einsum("rf,rd->fd", act, grad_rows, preferred_element_type=jnp.float32)
    return (dpart, grad_up, grad_down)


def local(
    fwd_acts, fwd_routes, fwd_gates, back_acts, back_routes, back_gates, back_grads, w_up, w_down
):
    devices = lax.axis_size("eg") * GROUP
    experts = devices // GROUP
    tok_rows = fwd_acts.shape[1]
    top_count = fwd_routes.shape[2]
    slot_cap = GROUP * (5 * tok_rows * top_count // (4 * devices))
    up_proj = w_up[0, 0]
    down_proj = w_down[0, 0]
    fwd_input = fwd_acts[0]
    back_input = back_acts[0]
    out_grad = back_grads[0]
    plain_f, gated_f = tables(fwd_routes[0], fwd_gates[0], experts, slot_cap)
    plain_b, gated_b = tables(back_routes[0], back_gates[0], experts, slot_cap)
    main = slot_cap // 8 * 8
    model_width = fwd_input.shape[-1]
    split = functools.partial(split_slots, experts=experts, slot_cap=slot_cap, main=main)
    plain_f, gated_f, plain_b, gated_b = [split(table) for table in (plain_f, gated_f, plain_b, gated_b)]
    grads_wide = out_grad.astype(jnp.float32)
    wires = []
    for index in range(2):
        rows_f = gather_rows(plain_f[index], fwd_input)
        rows_x = gather_rows(plain_b[index], back_input)
        rows_g = lax.dot_general(
            gated_b[index], grads_wide, (((0,), (0,)), ((), ())), precision=HIGH
        ).astype(jnp.bfloat16)
        if index == 0:
            wires.append([rows.reshape(experts, main, model_width) for rows in (rows_f, rows_x, rows_g)])
        else:
            wires.append([to_wire(rows, experts) for rows in (rows_f, rows_x, rows_g)])
    got = dispatch(wires[0] + wires[1])
    got = [got[:3], got[3:]]
    summed_f = []
    summed_b = []
    grad_up = 0.0
    grad_down = 0.0
    for index in range(2):
        got_f, got_x, got_g = [block.reshape(-1, model_width) for block in got[index]]
        part = expert_forward(got_f, up_proj, down_proj)
        summed_f.append(group_sum(part))
        dpart, more_up, more_down = expert_backward(got_x, got_g, up_proj, down_proj)
        grad_up = grad_up + more_up
        grad_down = grad_down + more_down
        summed_b.append(group_sum(dpart))

    def home(summed, tag):
        shaped = [summed[0].reshape(experts, main, model_width), to_wire(summed[1], experts)]
        return [block.reshape(-1, model_width).astype(jnp.float32) for block in send_home(shaped, tag)]

    back_f = home(summed_f, 1)
    back_b = home(summed_b, 2)
    merged = jnp.dot(gated_f[0], back_f[0], precision=HIGH) + jnp.dot(gated_f[1], back_f[1], precision=HIGH)
    section_out = (fwd_input.astype(jnp.float32) + merged).astype(jnp.bfloat16)
    spread_back = jnp.dot(plain_b[0], back_b[0], precision=HIGH) + jnp.dot(plain_b[1], back_b[1], precision=HIGH)
    section_grad = (grads_wide + spread_back).astype(jnp.bfloat16)
    fwd_next = passed_along(section_out[None], "pipe", 1)
    back_next = passed_along(section_grad[None], "pipe", -1)
    return (fwd_next, back_next, grad_up[None, None], grad_down[None, None])


def solution(mesh):
    groups = mesh.shape["expert"] // GROUP
    devices = mesh.devices.reshape(mesh.shape["pipe"], groups, 2, GROUP // 2)
    mesh = jax.sharding.Mesh(devices, ("pipe", "eg", "ez", "ec"))
    in_specs = (
        P("pipe", ("eg", "ez", "ec"), None),
        P("pipe", ("eg", "ez", "ec"), None),
        P("pipe", ("eg", "ez", "ec"), None),
        P("pipe", ("eg", "ez", "ec"), None),
        P("pipe", ("eg", "ez", "ec"), None),
        P("pipe", ("eg", "ez", "ec"), None),
        P("pipe", ("eg", "ez", "ec"), None),
        P("pipe", ("eg", "ez", "ec"), None, None),
        P("pipe", ("eg", "ez", "ec"), None, None),
    )
    out_specs = (
        P("pipe", ("eg", "ez", "ec"), None),
        P("pipe", ("eg", "ez", "ec"), None),
        P("pipe", ("eg", "ez", "ec"), None, None),
        P("pipe", ("eg", "ez", "ec"), None, None),
    )
    return jax.shard_map(local, mesh=mesh, in_specs=in_specs, out_specs=out_specs, check_vma=False)
```

```python
import jax
import jax.numpy as jnp
from jax import lax
from jax.sharding import PartitionSpec as P
from jax.experimental import pallas as pl
from jax.experimental.pallas import tpu as pltpu
import functools

GROUP = 4


HIGH = lax.Precision.HIGHEST


def passed_along(value, axis, steps):
    count = lax.axis_size(axis)
    pairs = [(source, (source + steps) % count) for source in range(count)]
    return lax.ppermute(value, axis, pairs)


def silu_grad(value):
    sigma = jax.nn.sigmoid(value)
    return sigma * (1.0 + value * (1.0 - sigma))


def tables(routes, gates, experts, slot_cap):
    tok_rows, top_count = routes.shape
    flat = routes.reshape(tok_rows * top_count)
    onehot = (flat[:, None] == jnp.arange(experts, dtype=jnp.int32)[None, :]).astype(jnp.int32)
    before = jnp.cumsum(onehot, axis=0) - onehot
    slots = jnp.sum(before * onehot, axis=1)
    places = flat * slot_cap + slots
    columns = jnp.arange(experts * slot_cap, dtype=jnp.int32)
    hits = (
        (places[:, None] == columns[None, :])
        .astype(jnp.float32)
        .reshape(tok_rows, top_count, experts * slot_cap)
    )
    plain = jnp.sum(hits, axis=1)
    gated = jnp.sum(hits * gates[:, :, None], axis=1)
    return (plain, gated)


def gather_rows(plain, values):
    return lax.dot_general(
        plain.astype(jnp.bfloat16),
        values,
        (((0,), (0,)), ((), ())),
        preferred_element_type=jnp.float32,
    ).astype(jnp.bfloat16)


def split_slots(table, experts, slot_cap, main):
    lead = table.shape[0]
    shaped = table.reshape(lead, experts, slot_cap)
    return (shaped[:, :, :main].reshape(lead, -1), shaped[:, :, main:].reshape(lead, -1))


def to_wire(rows, *lead):
    return rows.reshape(*lead, -1, 128)


def dispatch_kernel(groups, *refs):
    count = (len(refs) - 9) // 2
    sources = refs[:count]
    outs = refs[count:2 * count]
    local_sem, send1, recv1, xs_send, xs_recv, cs_send, cs_recv, fw_send, fw_recv = refs[2 * count:]
    mesh_kind = pl.DeviceIdType.MESH
    pipe = lax.axis_index("pipe")
    me = lax.axis_index("eg")
    chip = lax.axis_index("ez")
    core = lax.axis_index("ec")
    across = (pipe, me, 1 - chip, core)
    partner = (pipe, me, chip, 1 - core)
    peers = [(pipe, lax.rem(me + step, groups), chip, core) for step in range(1, groups)]
    barrier = pltpu.get_barrier_semaphore()
    for peer in peers + [across, partner]:
        pl.semaphore_signal(barrier, 1, device_id=peer, device_id_type=mesh_kind)
    pl.semaphore_wait(barrier, len(peers) + 2)
    def launch(index):
        source = sources[index]
        own = pltpu.make_async_copy(source.at[me], outs[index].at[core, chip, me], local_sem.at[index])
        own.start()
        copies = []
        for step in range(1, groups):
            copy = pltpu.make_async_remote_copy(
                src_ref=source.at[peers[step - 1][1]],
                dst_ref=outs[index].at[core, chip, me],
                send_sem=send1.at[index, step],
                recv_sem=recv1.at[index, step],
                device_id=peers[step - 1],
                device_id_type=mesh_kind,
            )
            copy.start()
            copies.append(copy)
        return own, copies

    def relay(index, far):
        far.wait_recv()
        held = outs[index].at[core, 1 - chip]
        onward = pltpu.make_async_remote_copy(
            src_ref=held, dst_ref=held, send_sem=fw_send.at[index], recv_sem=fw_recv.at[index],
            device_id=partner, device_id_type=mesh_kind,
        )
        onward.start()
        return onward

    count = len(sources)
    first = [launch(0)]
    second = []
    third = []
    for index in range(count):
        own, copies = first[index]
        own.wait()
        for copy in copies:
            copy.wait_recv()
        if index + 1 < count:
            first.append(launch(index + 1))
        block = outs[index].at[core, chip]
        far = pltpu.make_async_remote_copy(
            src_ref=block, dst_ref=block, send_sem=xs_send.at[index], recv_sem=xs_recv.at[index],
            device_id=across, device_id_type=mesh_kind,
        )
        far.start()
        near = pltpu.make_async_remote_copy(
            src_ref=block, dst_ref=block, send_sem=cs_send.at[index], recv_sem=cs_recv.at[index],
            device_id=partner, device_id_type=mesh_kind,
        )
        near.start()
        second.append((far, near))
        if index >= 1:
            third.append(relay(index - 1, second[index - 1][0]))
    third.append(relay(count - 1, second[count - 1][0]))
    for index in range(count):
        own, copies = first[index]
        for copy in copies:
            copy.wait_send()
        far, near = second[index]
        far.wait_send()
        near.wait_send()
        near.wait_recv()
        third[index].wait_send()
        third[index].wait_recv()


def dispatch(wires):
    groups = wires[0].shape[0]
    count = len(wires)
    dma = pltpu.SemaphoreType.DMA
    return pl.pallas_call(
        functools.partial(dispatch_kernel, groups),
        out_shape=[jax.ShapeDtypeStruct((2, 2) + wire.shape, wire.dtype) for wire in wires],
        in_specs=[pl.BlockSpec(memory_space=pl.ANY)] * count,
        out_specs=[pl.BlockSpec(memory_space=pl.ANY)] * count,
        scratch_shapes=[
            dma((count,)),
            dma((count, groups)),
            dma((count, groups)),
            dma((count,)),
            dma((count,)),
            dma((count,)),
            dma((count,)),
            dma((count,)),
            dma((count,)),
        ],
        compiler_params=pltpu.CompilerParams(collective_id=0, has_side_effects=True),
    )(*wires)


def split_slots(table, experts, slot_cap, main):
    lead = table.shape[0]
    shaped = table.reshape(lead, experts, slot_cap)
    return (shaped[:, :, :main].reshape(lead, -1), shaped[:, :, main:].reshape(lead, -1))


def to_wire(rows, *lead):
    return rows.reshape(*lead, -1, 128)


def return_kernel(groups, *refs):
    count = (len(refs) - 3) // 2
    sources = refs[:count]
    outs = refs[count:2 * count]
    local_sem, send1, recv1 = refs[2 * count:]
    mesh_kind = pl.DeviceIdType.MESH
    pipe = lax.axis_index("pipe")
    me = lax.axis_index("eg")
    chip = lax.axis_index("ez")
    core = lax.axis_index("ec")
    peers = [(pipe, lax.rem(me + step, groups), chip, core) for step in range(1, groups)]
    barrier = pltpu.get_barrier_semaphore()
    for peer in peers:
        pl.semaphore_signal(barrier, 1, device_id=peer, device_id_type=mesh_kind)
    pl.semaphore_wait(barrier, len(peers))
    started = []
    for index, source in enumerate(sources):
        own = pltpu.make_async_copy(source.at[me], outs[index].at[me], local_sem.at[index])
        own.start()
        copies = []
        for step in range(1, groups):
            copy = pltpu.make_async_remote_copy(
                src_ref=source.at[peers[step - 1][1]],
                dst_ref=outs[index].at[me],
                send_sem=send1.at[index, step],
                recv_sem=recv1.at[index, step],
                device_id=peers[step - 1],
                device_id_type=mesh_kind,
            )
            copy.start()
            copies.append(copy)
        started.append((own, copies))
    for own, copies in started:
        own.wait()
        for copy in copies:
            copy.wait_send()
            copy.wait_recv()


def send_home(wires, tag):
    groups = wires[0].shape[0]
    count = len(wires)
    dma = pltpu.SemaphoreType.DMA
    return pl.pallas_call(
        functools.partial(return_kernel, groups),
        out_shape=[jax.ShapeDtypeStruct(wire.shape, wire.dtype) for wire in wires],
        in_specs=[pl.BlockSpec(memory_space=pl.ANY)] * count,
        out_specs=[pl.BlockSpec(memory_space=pl.ANY)] * count,
        scratch_shapes=[dma((count,)), dma((count, groups)), dma((count, groups))],
        compiler_params=pltpu.CompilerParams(collective_id=tag, has_side_effects=True),
    )(*wires)


def group_sum(parts):
    model_width = parts.shape[-1]
    blocks = parts.reshape(2, 2, -1, model_width)
    mine = lax.all_to_all(blocks, "ec", split_axis=0, concat_axis=0, tiled=True)
    pair = jnp.sum(mine.astype(jnp.float32), axis=0).astype(jnp.bfloat16)
    other = lax.all_to_all(pair, "ez", split_axis=0, concat_axis=0, tiled=True)
    return jnp.sum(other.astype(jnp.float32), axis=0).astype(jnp.bfloat16)


def expert_forward(rows, up_proj, down_proj):
    pre = jnp.einsum("...d,df->...f", rows, up_proj, preferred_element_type=jnp.float32)
    act = jax.nn.silu(pre).astype(jnp.bfloat16)
    return jnp.einsum(
        "...f,fd->...d", act, down_proj, preferred_element_type=jnp.float32
    ).astype(jnp.bfloat16)


def expert_backward(rows, grad_rows, up_proj, down_proj):
    pre = jnp.einsum("...d,df->...f", rows, up_proj, preferred_element_type=jnp.float32)
    act = jax.nn.silu(pre).astype(jnp.bfloat16)
    dact = jnp.einsum("...d,fd->...f", grad_rows, down_proj, preferred_element_type=jnp.float32)
    dpre = (dact * silu_grad(pre)).astype(jnp.bfloat16)
    dpart = jnp.einsum(
        "...f,df->...d", dpre, up_proj, preferred_element_type=jnp.float32
    ).astype(jnp.bfloat16)
    grad_up = jnp.einsum("rd,rf->df", rows, dpre, preferred_element_type=jnp.float32)
    grad_down = jnp.einsum("rf,rd->fd", act, grad_rows, preferred_element_type=jnp.float32)
    return (dpart, grad_up, grad_down)


def local(
    fwd_acts, fwd_routes, fwd_gates, back_acts, back_routes, back_gates, back_grads, w_up, w_down
):
    devices = lax.axis_size("eg") * GROUP
    experts = devices // GROUP
    tok_rows = fwd_acts.shape[1]
    top_count = fwd_routes.shape[2]
    slot_cap = GROUP * (5 * tok_rows * top_count // (4 * devices))
    up_proj = w_up[0, 0]
    down_proj = w_down[0, 0]
    fwd_input = fwd_acts[0]
    back_input = back_acts[0]
    out_grad = back_grads[0]
    plain_f, gated_f = tables(fwd_routes[0], fwd_gates[0], experts, slot_cap)
    plain_b, gated_b = tables(back_routes[0], back_gates[0], experts, slot_cap)
    main = slot_cap // 8 * 8
    model_width = fwd_input.shape[-1]
    split = functools.partial(split_slots, experts=experts, slot_cap=slot_cap, main=main)
    plain_f, gated_f, plain_b, gated_b = [split(table) for table in (plain_f, gated_f, plain_b, gated_b)]
    grads_wide = out_grad.astype(jnp.float32)
    wires = []
    for index in range(2):
        rows_f = gather_rows(plain_f[index], fwd_input)
        rows_x = gather_rows(plain_b[index], back_input)
        rows_g = lax.dot_general(
            gated_b[index], grads_wide, (((0,), (0,)), ((), ())), precision=HIGH
        ).astype(jnp.bfloat16)
        if index == 0:
            wires.append([rows.reshape(experts, main, model_width) for rows in (rows_f, rows_x, rows_g)])
        else:
            wires.append([to_wire(rows, experts) for rows in (rows_f, rows_x, rows_g)])
    got = dispatch(wires[0] + wires[1])
    got = [got[:3], got[3:]]
    grad_up = 0.0
    grad_down = 0.0
    parts_f = []
    parts_b = []
    for index in range(2):
        got_f, got_x, got_g = [block.reshape(-1, model_width) for block in got[index]]
        parts_f.append(expert_forward(got_f, up_proj, down_proj).reshape(2, 2, -1, model_width))
        dpart, more_up, more_down = expert_backward(got_x, got_g, up_proj, down_proj)
        grad_up = grad_up + more_up
        grad_down = grad_down + more_down
        parts_b.append(dpart.reshape(2, 2, -1, model_width))
    cut = experts * main
    whole_f = group_sum(jnp.concatenate(parts_f, axis=2))
    whole_b = group_sum(jnp.concatenate(parts_b, axis=2))
    summed_f = [whole_f[:cut], whole_f[cut:]]
    summed_b = [whole_b[:cut], whole_b[cut:]]

    def home(summed, tag):
        shaped = [summed[0].reshape(experts, main, model_width), to_wire(summed[1], experts)]
        return [block.reshape(-1, model_width).astype(jnp.float32) for block in send_home(shaped, tag)]

    back_f = home(summed_f, 1)
    back_b = home(summed_b, 2)
    merged = jnp.dot(gated_f[0], back_f[0], precision=HIGH) + jnp.dot(gated_f[1], back_f[1], precision=HIGH)
    section_out = (fwd_input.astype(jnp.float32) + merged).astype(jnp.bfloat16)
    spread_back = jnp.dot(plain_b[0], back_b[0], precision=HIGH) + jnp.dot(plain_b[1], back_b[1], precision=HIGH)
    section_grad = (grads_wide + spread_back).astype(jnp.bfloat16)
    fwd_next = passed_along(section_out[None], "pipe", 1)
    back_next = passed_along(section_grad[None], "pipe", -1)
    return (fwd_next, back_next, grad_up[None, None], grad_down[None, None])


def solution(mesh):
    groups = mesh.shape["expert"] // GROUP
    devices = mesh.devices.reshape(mesh.shape["pipe"], groups, 2, GROUP // 2)
    mesh = jax.sharding.Mesh(devices, ("pipe", "eg", "ez", "ec"))
    in_specs = (
        P("pipe", ("eg", "ez", "ec"), None),
        P("pipe", ("eg", "ez", "ec"), None),
        P("pipe", ("eg", "ez", "ec"), None),
        P("pipe", ("eg", "ez", "ec"), None),
        P("pipe", ("eg", "ez", "ec"), None),
        P("pipe", ("eg", "ez", "ec"), None),
        P("pipe", ("eg", "ez", "ec"), None),
        P("pipe", ("eg", "ez", "ec"), None, None),
        P("pipe", ("eg", "ez", "ec"), None, None),
    )
    out_specs = (
        P("pipe", ("eg", "ez", "ec"), None),
        P("pipe", ("eg", "ez", "ec"), None),
        P("pipe", ("eg", "ez", "ec"), None, None),
        P("pipe", ("eg", "ez", "ec"), None, None),
    )
    return jax.shard_map(local, mesh=mesh, in_specs=in_specs, out_specs=out_specs, check_vma=False)
```

```python
import jax
import jax.numpy as jnp
from jax import lax
from jax.sharding import PartitionSpec as P
from jax.experimental import pallas as pl
from jax.experimental.pallas import tpu as pltpu
import functools

GROUP = 4


HIGH = lax.Precision.HIGHEST


def passed_along(value, axis, steps):
    count = lax.axis_size(axis)
    pairs = [(source, (source + steps) % count) for source in range(count)]
    return lax.ppermute(value, axis, pairs)


def silu_grad(value):
    sigma = jax.nn.sigmoid(value)
    return sigma * (1.0 + value * (1.0 - sigma))


def tables(routes, gates, experts, slot_cap):
    tok_rows, top_count = routes.shape
    flat = routes.reshape(tok_rows * top_count)
    onehot = (flat[:, None] == jnp.arange(experts, dtype=jnp.int32)[None, :]).astype(jnp.int32)
    before = jnp.cumsum(onehot, axis=0) - onehot
    slots = jnp.sum(before * onehot, axis=1)
    places = flat * slot_cap + slots
    columns = jnp.arange(experts * slot_cap, dtype=jnp.int32)
    hits = (
        (places[:, None] == columns[None, :])
        .astype(jnp.float32)
        .reshape(tok_rows, top_count, experts * slot_cap)
    )
    plain = jnp.sum(hits, axis=1)
    gated = jnp.sum(hits * gates[:, :, None], axis=1)
    return (plain, gated)


def gather_rows(plain, values):
    return lax.dot_general(
        plain.astype(jnp.bfloat16),
        values,
        (((0,), (0,)), ((), ())),
        preferred_element_type=jnp.float32,
    ).astype(jnp.bfloat16)


def to_wire(rows, *lead):
    return rows.reshape(*lead, -1, 128)


def dispatch_kernel(groups, *refs):
    sources = refs[:3]
    outs = refs[3:6]
    local_sem, send1, recv1, xs_send, xs_recv, cs_send, cs_recv, fw_send, fw_recv = refs[6:]
    mesh_kind = pl.DeviceIdType.MESH
    pipe = lax.axis_index("pipe")
    me = lax.axis_index("eg")
    chip = lax.axis_index("ez")
    core = lax.axis_index("ec")
    across = (pipe, me, 1 - chip, core)
    partner = (pipe, me, chip, 1 - core)
    peers = [(pipe, lax.rem(me + step, groups), chip, core) for step in range(1, groups)]
    barrier = pltpu.get_barrier_semaphore()
    for peer in peers + [across, partner]:
        pl.semaphore_signal(barrier, 1, device_id=peer, device_id_type=mesh_kind)
    pl.semaphore_wait(barrier, len(peers) + 2)
    def launch(index):
        source = sources[index]
        own = pltpu.make_async_copy(source.at[me], outs[index].at[core, chip, me], local_sem.at[index])
        own.start()
        copies = []
        for step in range(1, groups):
            copy = pltpu.make_async_remote_copy(
                src_ref=source.at[peers[step - 1][1]],
                dst_ref=outs[index].at[core, chip, me],
                send_sem=send1.at[index, step],
                recv_sem=recv1.at[index, step],
                device_id=peers[step - 1],
                device_id_type=mesh_kind,
            )
            copy.start()
            copies.append(copy)
        return own, copies

    def relay(index, far):
        far.wait_recv()
        held = outs[index].at[core, 1 - chip]
        onward = pltpu.make_async_remote_copy(
            src_ref=held, dst_ref=held, send_sem=fw_send.at[index], recv_sem=fw_recv.at[index],
            device_id=partner, device_id_type=mesh_kind,
        )
        onward.start()
        return onward

    count = len(sources)
    first = [launch(0)]
    second = []
    third = []
    for index in range(count):
        own, copies = first[index]
        own.wait()
        for copy in copies:
            copy.wait_recv()
        if index + 1 < count:
            first.append(launch(index + 1))
        block = outs[index].at[core, chip]
        far = pltpu.make_async_remote_copy(
            src_ref=block, dst_ref=block, send_sem=xs_send.at[index], recv_sem=xs_recv.at[index],
            device_id=across, device_id_type=mesh_kind,
        )
        far.start()
        near = pltpu.make_async_remote_copy(
            src_ref=block, dst_ref=block, send_sem=cs_send.at[index], recv_sem=cs_recv.at[index],
            device_id=partner, device_id_type=mesh_kind,
        )
        near.start()
        second.append((far, near))
        if index >= 1:
            third.append(relay(index - 1, second[index - 1][0]))
    third.append(relay(count - 1, second[count - 1][0]))
    for index in range(count):
        own, copies = first[index]
        for copy in copies:
            copy.wait_send()
        far, near = second[index]
        far.wait_send()
        near.wait_send()
        near.wait_recv()
        third[index].wait_send()
        third[index].wait_recv()


def dispatch(wires):
    groups = wires[0].shape[0]
    count = len(wires)
    tail = wires[0].shape[1:]
    dma = pltpu.SemaphoreType.DMA
    return pl.pallas_call(
        functools.partial(dispatch_kernel, groups),
        out_shape=[jax.ShapeDtypeStruct((2, 2, groups) + tail, wires[0].dtype)] * count,
        in_specs=[pl.BlockSpec(memory_space=pl.ANY)] * count,
        out_specs=[pl.BlockSpec(memory_space=pl.ANY)] * count,
        scratch_shapes=[
            dma((count,)),
            dma((count, groups)),
            dma((count, groups)),
            dma((count,)),
            dma((count,)),
            dma((count,)),
            dma((count,)),
            dma((count,)),
            dma((count,)),
        ],
        compiler_params=pltpu.CompilerParams(collective_id=0, has_side_effects=True),
    )(*wires)


def to_wire(rows, *lead):
    return rows.reshape(*lead, -1, 128)


def return_kernel(groups, *refs):
    count = len(refs) - 4
    sources = refs[:count]
    out, local_sem, send1, recv1 = refs[count:]
    mesh_kind = pl.DeviceIdType.MESH
    pipe = lax.axis_index("pipe")
    me = lax.axis_index("eg")
    chip = lax.axis_index("ez")
    core = lax.axis_index("ec")
    peers = [(pipe, lax.rem(me + step, groups), chip, core) for step in range(1, groups)]
    barrier = pltpu.get_barrier_semaphore()
    for peer in peers:
        pl.semaphore_signal(barrier, 1, device_id=peer, device_id_type=mesh_kind)
    pl.semaphore_wait(barrier, len(peers))
    started = []
    for index, source in enumerate(sources):
        own = pltpu.make_async_copy(source.at[me], out.at[index, me], local_sem.at[index])
        own.start()
        copies = []
        for step in range(1, groups):
            copy = pltpu.make_async_remote_copy(
                src_ref=source.at[peers[step - 1][1]],
                dst_ref=out.at[index, me],
                send_sem=send1.at[index, step],
                recv_sem=recv1.at[index, step],
                device_id=peers[step - 1],
                device_id_type=mesh_kind,
            )
            copy.start()
            copies.append(copy)
        started.append((own, copies))
    for own, copies in started:
        own.wait()
        for copy in copies:
            copy.wait_send()
            copy.wait_recv()


def send_home(wires, tag):
    groups = wires[0].shape[0]
    count = len(wires)
    dma = pltpu.SemaphoreType.DMA
    return pl.pallas_call(
        functools.partial(return_kernel, groups),
        out_shape=jax.ShapeDtypeStruct((count,) + wires[0].shape, wires[0].dtype),
        in_specs=[pl.BlockSpec(memory_space=pl.ANY)] * count,
        out_specs=pl.BlockSpec(memory_space=pl.ANY),
        scratch_shapes=[dma((count,)), dma((count, groups)), dma((count, groups))],
        compiler_params=pltpu.CompilerParams(collective_id=tag, has_side_effects=True),
    )(*wires)


def group_sum(parts, experts):
    model_width = parts.shape[-1]
    blocks = parts.reshape(2, 2, -1, model_width)
    mine = lax.all_to_all(blocks, "ec", split_axis=0, concat_axis=0, tiled=True)
    pair = jnp.sum(mine.astype(jnp.float32), axis=0).astype(jnp.bfloat16)
    other = lax.all_to_all(pair, "ez", split_axis=0, concat_axis=0, tiled=True)
    summed = jnp.sum(other.astype(jnp.float32), axis=0).astype(jnp.bfloat16)
    return to_wire(summed, experts)


def expert_forward(rows, up_proj, down_proj):
    pre = jnp.einsum("...d,df->...f", rows, up_proj, preferred_element_type=jnp.float32)
    act = jax.nn.silu(pre).astype(jnp.bfloat16)
    return jnp.einsum(
        "...f,fd->...d", act, down_proj, preferred_element_type=jnp.float32
    ).astype(jnp.bfloat16)


def expert_backward(rows, grad_rows, up_proj, down_proj):
    pre = jnp.einsum("...d,df->...f", rows, up_proj, preferred_element_type=jnp.float32)
    act = jax.nn.silu(pre).astype(jnp.bfloat16)
    dact = jnp.einsum("...d,fd->...f", grad_rows, down_proj, preferred_element_type=jnp.float32)
    dpre = (dact * silu_grad(pre)).astype(jnp.bfloat16)
    dpart = jnp.einsum(
        "...f,df->...d", dpre, up_proj, preferred_element_type=jnp.float32
    ).astype(jnp.bfloat16)
    grad_up = jnp.einsum("rd,rf->df", rows, dpre, preferred_element_type=jnp.float32)
    grad_down = jnp.einsum("rf,rd->fd", act, grad_rows, preferred_element_type=jnp.float32)
    return (dpart, grad_up, grad_down)


def local(
    fwd_acts, fwd_routes, fwd_gates, back_acts, back_routes, back_gates, back_grads, w_up, w_down
):
    devices = lax.axis_size("eg") * GROUP
    experts = devices // GROUP
    tok_rows = fwd_acts.shape[1]
    top_count = fwd_routes.shape[2]
    slot_cap = GROUP * (5 * tok_rows * top_count // (4 * devices))
    up_proj = w_up[0, 0]
    down_proj = w_down[0, 0]
    fwd_input = fwd_acts[0]
    back_input = back_acts[0]
    out_grad = back_grads[0]
    plain_f, gated_f = tables(fwd_routes[0], fwd_gates[0], experts, slot_cap)
    plain_b, gated_b = tables(back_routes[0], back_gates[0], experts, slot_cap)
    buffer_f = gather_rows(plain_f, fwd_input)
    buffer_x = gather_rows(plain_b, back_input)
    buffer_g = lax.dot_general(
        gated_b, out_grad.astype(jnp.float32), (((0,), (0,)), ((), ())), precision=HIGH
    ).astype(jnp.bfloat16)
    model_width = fwd_input.shape[-1]
    got = dispatch([to_wire(b, experts) for b in (buffer_f, buffer_x, buffer_g)])
    got_f, got_x, got_g = [got[index].reshape(-1, model_width) for index in range(3)]
    part = expert_forward(got_f, up_proj, down_proj)
    wire_f = group_sum(part, experts)
    summed_f = send_home([wire_f], 1)[0].reshape(-1, model_width).astype(jnp.float32)
    merged = jnp.dot(gated_f, summed_f, precision=HIGH)
    section_out = (fwd_input.astype(jnp.float32) + merged).astype(jnp.bfloat16)
    section_out, got_x, got_g = lax.optimization_barrier((section_out, got_x, got_g))
    dpart, grad_up, grad_down = expert_backward(got_x, got_g, up_proj, down_proj)
    wire_b = group_sum(dpart, experts)
    summed_b = send_home([wire_b], 2)[0].reshape(-1, model_width).astype(jnp.float32)
    spread_back = jnp.dot(plain_b, summed_b, precision=HIGH)
    section_grad = (out_grad.astype(jnp.float32) + spread_back).astype(jnp.bfloat16)
    fwd_next = passed_along(section_out[None], "pipe", 1)
    back_next = passed_along(section_grad[None], "pipe", -1)
    return (fwd_next, back_next, grad_up[None, None], grad_down[None, None])


def solution(mesh):
    groups = mesh.shape["expert"] // GROUP
    devices = mesh.devices.reshape(mesh.shape["pipe"], groups, 2, GROUP // 2)
    mesh = jax.sharding.Mesh(devices, ("pipe", "eg", "ez", "ec"))
    in_specs = (
        P("pipe", ("eg", "ez", "ec"), None),
        P("pipe", ("eg", "ez", "ec"), None),
        P("pipe", ("eg", "ez", "ec"), None),
        P("pipe", ("eg", "ez", "ec"), None),
        P("pipe", ("eg", "ez", "ec"), None),
        P("pipe", ("eg", "ez", "ec"), None),
        P("pipe", ("eg", "ez", "ec"), None),
        P("pipe", ("eg", "ez", "ec"), None, None),
        P("pipe", ("eg", "ez", "ec"), None, None),
    )
    out_specs = (
        P("pipe", ("eg", "ez", "ec"), None),
        P("pipe", ("eg", "ez", "ec"), None),
        P("pipe", ("eg", "ez", "ec"), None, None),
        P("pipe", ("eg", "ez", "ec"), None, None),
    )
    return jax.shard_map(local, mesh=mesh, in_specs=in_specs, out_specs=out_specs, check_vma=False)
```

```python
import jax
import jax.numpy as jnp
from jax import lax
from jax.sharding import PartitionSpec as P
from jax.experimental import pallas as pl
from jax.experimental.pallas import tpu as pltpu
import functools

GROUP = 4


HIGH = lax.Precision.HIGHEST


def passed_along(value, axis, steps):
    count = lax.axis_size(axis)
    pairs = [(source, (source + steps) % count) for source in range(count)]
    return lax.ppermute(value, axis, pairs)


def silu_grad(value):
    sigma = jax.nn.sigmoid(value)
    return sigma * (1.0 + value * (1.0 - sigma))


def tables(routes, gates, experts, slot_cap):
    tok_rows, top_count = routes.shape
    flat = routes.reshape(tok_rows * top_count)
    onehot = (flat[:, None] == jnp.arange(experts, dtype=jnp.int32)[None, :]).astype(jnp.int32)
    before = jnp.cumsum(onehot, axis=0) - onehot
    slots = jnp.sum(before * onehot, axis=1)
    places = flat * slot_cap + slots
    columns = jnp.arange(experts * slot_cap, dtype=jnp.int32)
    hits = (
        (places[:, None] == columns[None, :])
        .astype(jnp.float32)
        .reshape(tok_rows, top_count, experts * slot_cap)
    )
    plain = jnp.sum(hits, axis=1)
    gated = jnp.sum(hits * gates[:, :, None], axis=1)
    return (plain, gated)


def gather_rows(plain, values):
    return lax.dot_general(
        plain.astype(jnp.bfloat16),
        values,
        (((0,), (0,)), ((), ())),
        preferred_element_type=jnp.float32,
    ).astype(jnp.bfloat16)


def to_wire(rows, *lead):
    return rows.reshape(*lead, -1, 128)


def dispatch_kernel(groups, *refs):
    sources = refs[:3]
    outs = refs[3:6]
    local_sem, send1, recv1, xs_send, xs_recv, cs_send, cs_recv, fw_send, fw_recv = refs[6:]
    mesh_kind = pl.DeviceIdType.MESH
    pipe = lax.axis_index("pipe")
    me = lax.axis_index("eg")
    chip = lax.axis_index("ez")
    core = lax.axis_index("ec")
    across = (pipe, me, 1 - chip, core)
    partner = (pipe, me, chip, 1 - core)
    peers = [(pipe, lax.rem(me + step, groups), chip, core) for step in range(1, groups)]
    barrier = pltpu.get_barrier_semaphore()
    for peer in peers + [across, partner]:
        pl.semaphore_signal(barrier, 1, device_id=peer, device_id_type=mesh_kind)
    pl.semaphore_wait(barrier, len(peers) + 2)
    def launch(index):
        source = sources[index]
        own = pltpu.make_async_copy(source.at[me], outs[index].at[core, chip, me], local_sem.at[index])
        own.start()
        copies = []
        for step in range(1, groups):
            copy = pltpu.make_async_remote_copy(
                src_ref=source.at[peers[step - 1][1]],
                dst_ref=outs[index].at[core, chip, me],
                send_sem=send1.at[index, step],
                recv_sem=recv1.at[index, step],
                device_id=peers[step - 1],
                device_id_type=mesh_kind,
            )
            copy.start()
            copies.append(copy)
        return own, copies

    def relay(index, far):
        far.wait_recv()
        held = outs[index].at[core, 1 - chip]
        onward = pltpu.make_async_remote_copy(
            src_ref=held, dst_ref=held, send_sem=fw_send.at[index], recv_sem=fw_recv.at[index],
            device_id=partner, device_id_type=mesh_kind,
        )
        onward.start()
        return onward

    count = len(sources)
    first = [launch(0)]
    second = []
    third = []
    for index in range(count):
        own, copies = first[index]
        own.wait()
        for copy in copies:
            copy.wait_recv()
        if index + 1 < count:
            first.append(launch(index + 1))
        block = outs[index].at[core, chip]
        far = pltpu.make_async_remote_copy(
            src_ref=block, dst_ref=block, send_sem=xs_send.at[index], recv_sem=xs_recv.at[index],
            device_id=across, device_id_type=mesh_kind,
        )
        far.start()
        near = pltpu.make_async_remote_copy(
            src_ref=block, dst_ref=block, send_sem=cs_send.at[index], recv_sem=cs_recv.at[index],
            device_id=partner, device_id_type=mesh_kind,
        )
        near.start()
        second.append((far, near))
        if index >= 1:
            third.append(relay(index - 1, second[index - 1][0]))
    third.append(relay(count - 1, second[count - 1][0]))
    for index in range(count):
        own, copies = first[index]
        for copy in copies:
            copy.wait_send()
        far, near = second[index]
        far.wait_send()
        near.wait_send()
        near.wait_recv()
        third[index].wait_send()
        third[index].wait_recv()


def dispatch(wires):
    groups = wires[0].shape[0]
    count = len(wires)
    tail = wires[0].shape[1:]
    dma = pltpu.SemaphoreType.DMA
    return pl.pallas_call(
        functools.partial(dispatch_kernel, groups),
        out_shape=[jax.ShapeDtypeStruct((2, 2, groups) + tail, wires[0].dtype)] * count,
        in_specs=[pl.BlockSpec(memory_space=pl.ANY)] * count,
        out_specs=[pl.BlockSpec(memory_space=pl.ANY)] * count,
        scratch_shapes=[
            dma((count,)),
            dma((count, groups)),
            dma((count, groups)),
            dma((count,)),
            dma((count,)),
            dma((count,)),
            dma((count,)),
            dma((count,)),
            dma((count,)),
        ],
        compiler_params=pltpu.CompilerParams(collective_id=0, has_side_effects=True),
    )(*wires)


def to_wire(rows, *lead):
    return rows.reshape(*lead, -1, 128)


def return_kernel(groups, *refs):
    count = len(refs) - 4
    sources = refs[:count]
    out, local_sem, send1, recv1 = refs[count:]
    mesh_kind = pl.DeviceIdType.MESH
    pipe = lax.axis_index("pipe")
    me = lax.axis_index("eg")
    chip = lax.axis_index("ez")
    core = lax.axis_index("ec")
    peers = [(pipe, lax.rem(me + step, groups), chip, core) for step in range(1, groups)]
    barrier = pltpu.get_barrier_semaphore()
    for peer in peers:
        pl.semaphore_signal(barrier, 1, device_id=peer, device_id_type=mesh_kind)
    pl.semaphore_wait(barrier, len(peers))
    started = []
    for index, source in enumerate(sources):
        own = pltpu.make_async_copy(source.at[me], out.at[index, me], local_sem.at[index])
        own.start()
        copies = []
        for step in range(1, groups):
            copy = pltpu.make_async_remote_copy(
                src_ref=source.at[peers[step - 1][1]],
                dst_ref=out.at[index, me],
                send_sem=send1.at[index, step],
                recv_sem=recv1.at[index, step],
                device_id=peers[step - 1],
                device_id_type=mesh_kind,
            )
            copy.start()
            copies.append(copy)
        started.append((own, copies))
    for own, copies in started:
        own.wait()
        for copy in copies:
            copy.wait_send()
            copy.wait_recv()


def send_home(wires, tag):
    groups = wires[0].shape[0]
    count = len(wires)
    dma = pltpu.SemaphoreType.DMA
    return pl.pallas_call(
        functools.partial(return_kernel, groups),
        out_shape=jax.ShapeDtypeStruct((count,) + wires[0].shape, wires[0].dtype),
        in_specs=[pl.BlockSpec(memory_space=pl.ANY)] * count,
        out_specs=pl.BlockSpec(memory_space=pl.ANY),
        scratch_shapes=[dma((count,)), dma((count, groups)), dma((count, groups))],
        compiler_params=pltpu.CompilerParams(collective_id=tag, has_side_effects=True),
    )(*wires)


def group_sum(parts, experts):
    model_width = parts.shape[-1]
    blocks = parts.reshape(2, 2, -1, model_width)
    mine = lax.all_to_all(blocks, "ec", split_axis=0, concat_axis=0, tiled=True)
    pair = jnp.sum(mine.astype(jnp.float32), axis=0).astype(jnp.bfloat16)
    other = lax.all_to_all(pair, "ez", split_axis=0, concat_axis=0, tiled=True)
    summed = jnp.sum(other.astype(jnp.float32), axis=0).astype(jnp.bfloat16)
    return to_wire(summed, experts)


def expert_forward(rows, up_proj, down_proj):
    pre = jnp.einsum("...d,df->...f", rows, up_proj, preferred_element_type=jnp.float32)
    act = jax.nn.silu(pre).astype(jnp.bfloat16)
    return jnp.einsum(
        "...f,fd->...d", act, down_proj, preferred_element_type=jnp.float32
    ).astype(jnp.bfloat16)


def expert_backward(rows, grad_rows, up_proj, down_proj):
    pre = jnp.einsum("...d,df->...f", rows, up_proj, preferred_element_type=jnp.float32)
    act = jax.nn.silu(pre).astype(jnp.bfloat16)
    dact = jnp.einsum("...d,fd->...f", grad_rows, down_proj, preferred_element_type=jnp.float32)
    dpre = (dact * silu_grad(pre)).astype(jnp.bfloat16)
    dpart = jnp.einsum(
        "...f,df->...d", dpre, up_proj, preferred_element_type=jnp.float32
    ).astype(jnp.bfloat16)
    grad_up = jnp.einsum("rd,rf->df", rows, dpre, preferred_element_type=jnp.float32)
    grad_down = jnp.einsum("rf,rd->fd", act, grad_rows, preferred_element_type=jnp.float32)
    return (dpart, grad_up, grad_down)


def local(
    fwd_acts, fwd_routes, fwd_gates, back_acts, back_routes, back_gates, back_grads, w_up, w_down
):
    devices = lax.axis_size("eg") * GROUP
    experts = devices // GROUP
    tok_rows = fwd_acts.shape[1]
    top_count = fwd_routes.shape[2]
    slot_cap = GROUP * (5 * tok_rows * top_count // (4 * devices))
    up_proj = w_up[0, 0]
    down_proj = w_down[0, 0]
    fwd_input = fwd_acts[0]
    back_input = back_acts[0]
    out_grad = back_grads[0]
    plain_f, gated_f = tables(fwd_routes[0], fwd_gates[0], experts, slot_cap)
    plain_b, gated_b = tables(back_routes[0], back_gates[0], experts, slot_cap)
    buffer_f = gather_rows(plain_f, fwd_input)
    buffer_x = gather_rows(plain_b, back_input)
    buffer_g = lax.dot_general(
        gated_b, out_grad.astype(jnp.float32), (((0,), (0,)), ((), ())), precision=HIGH
    ).astype(jnp.bfloat16)
    model_width = fwd_input.shape[-1]
    got = dispatch([to_wire(b, experts) for b in (buffer_f, buffer_x, buffer_g)])
    got_f, got_x, got_g = [got[index].reshape(-1, model_width) for index in range(3)]
    part = expert_forward(got_f, up_proj, down_proj)
    wire_f = group_sum(part, experts)
    dpart, grad_up, grad_down = expert_backward(got_x, got_g, up_proj, down_proj)
    wire_b = group_sum(dpart, experts)
    summed_f, summed_b = [
        block.reshape(-1, model_width).astype(jnp.float32) for block in send_home([wire_f, wire_b], 1)
    ]
    merged = jnp.dot(gated_f, summed_f, precision=HIGH)
    section_out = (fwd_input.astype(jnp.float32) + merged).astype(jnp.bfloat16)
    spread_back = jnp.dot(plain_b, summed_b, precision=HIGH)
    section_grad = (out_grad.astype(jnp.float32) + spread_back).astype(jnp.bfloat16)
    fwd_next = passed_along(section_out[None], "pipe", 1)
    back_next = passed_along(section_grad[None], "pipe", -1)
    return (fwd_next, back_next, grad_up[None, None], grad_down[None, None])


def solution(mesh):
    groups = mesh.shape["expert"] // GROUP
    devices = mesh.devices.reshape(mesh.shape["pipe"], groups, 2, GROUP // 2)
    mesh = jax.sharding.Mesh(devices, ("pipe", "eg", "ez", "ec"))
    in_specs = (
        P("pipe", ("eg", "ez", "ec"), None),
        P("pipe", ("eg", "ez", "ec"), None),
        P("pipe", ("eg", "ez", "ec"), None),
        P("pipe", ("eg", "ez", "ec"), None),
        P("pipe", ("eg", "ez", "ec"), None),
        P("pipe", ("eg", "ez", "ec"), None),
        P("pipe", ("eg", "ez", "ec"), None),
        P("pipe", ("eg", "ez", "ec"), None, None),
        P("pipe", ("eg", "ez", "ec"), None, None),
    )
    out_specs = (
        P("pipe", ("eg", "ez", "ec"), None),
        P("pipe", ("eg", "ez", "ec"), None),
        P("pipe", ("eg", "ez", "ec"), None, None),
        P("pipe", ("eg", "ez", "ec"), None, None),
    )
    return jax.shard_map(local, mesh=mesh, in_specs=in_specs, out_specs=out_specs, check_vma=False)
```

```python
import jax
import jax.numpy as jnp
from jax import lax
from jax.sharding import PartitionSpec as P
from jax.experimental import pallas as pl
from jax.experimental.pallas import tpu as pltpu
import functools

GROUP = 4


HIGH = lax.Precision.HIGHEST


def passed_along(value, axis, steps):
    count = lax.axis_size(axis)
    pairs = [(source, (source + steps) % count) for source in range(count)]
    return lax.ppermute(value, axis, pairs)


def silu_grad(value):
    sigma = jax.nn.sigmoid(value)
    return sigma * (1.0 + value * (1.0 - sigma))


def tables(routes, gates, experts, slot_cap):
    tok_rows, top_count = routes.shape
    flat = routes.reshape(tok_rows * top_count)
    onehot = (flat[:, None] == jnp.arange(experts, dtype=jnp.int32)[None, :]).astype(jnp.int32)
    before = jnp.cumsum(onehot, axis=0) - onehot
    slots = jnp.sum(before * onehot, axis=1)
    places = flat * slot_cap + slots
    columns = jnp.arange(experts * slot_cap, dtype=jnp.int32)
    hits = (
        (places[:, None] == columns[None, :])
        .astype(jnp.float32)
        .reshape(tok_rows, top_count, experts * slot_cap)
    )
    plain = jnp.sum(hits, axis=1)
    gated = jnp.sum(hits * gates[:, :, None], axis=1)
    return (plain, gated)


def gather_rows(plain, values):
    return lax.dot_general(
        plain.astype(jnp.bfloat16),
        values,
        (((0,), (0,)), ((), ())),
        preferred_element_type=jnp.float32,
    ).astype(jnp.bfloat16)


def to_wire(rows, *lead):
    return rows.reshape(*lead, -1, 128)


def dispatch_kernel(groups, *refs):
    sources = refs[:3]
    outs = refs[3:6]
    local_sem, send1, recv1, xs_send, xs_recv, cs_send, cs_recv, fw_send, fw_recv = refs[6:]
    mesh_kind = pl.DeviceIdType.MESH
    pipe = lax.axis_index("pipe")
    me = lax.axis_index("eg")
    chip = lax.axis_index("ez")
    core = lax.axis_index("ec")
    across = (pipe, me, 1 - chip, core)
    partner = (pipe, me, chip, 1 - core)
    peers = [(pipe, lax.rem(me + step, groups), chip, core) for step in range(1, groups)]
    barrier = pltpu.get_barrier_semaphore()
    for peer in peers + [across, partner]:
        pl.semaphore_signal(barrier, 1, device_id=peer, device_id_type=mesh_kind)
    pl.semaphore_wait(barrier, len(peers) + 2)
    def launch(index):
        source = sources[index]
        own = pltpu.make_async_copy(source.at[me], outs[index].at[core, chip, me], local_sem.at[index])
        own.start()
        copies = []
        for step in range(1, groups):
            copy = pltpu.make_async_remote_copy(
                src_ref=source.at[peers[step - 1][1]],
                dst_ref=outs[index].at[core, chip, me],
                send_sem=send1.at[index, step],
                recv_sem=recv1.at[index, step],
                device_id=peers[step - 1],
                device_id_type=mesh_kind,
            )
            copy.start()
            copies.append(copy)
        return own, copies

    def relay(index, far):
        far.wait_recv()
        held = outs[index].at[core, 1 - chip]
        onward = pltpu.make_async_remote_copy(
            src_ref=held, dst_ref=held, send_sem=fw_send.at[index], recv_sem=fw_recv.at[index],
            device_id=partner, device_id_type=mesh_kind,
        )
        onward.start()
        return onward

    count = len(sources)
    first = [launch(0)]
    second = []
    third = []
    for index in range(count):
        own, copies = first[index]
        own.wait()
        for copy in copies:
            copy.wait_recv()
        if index + 1 < count:
            first.append(launch(index + 1))
        block = outs[index].at[core, chip]
        far = pltpu.make_async_remote_copy(
            src_ref=block, dst_ref=block, send_sem=xs_send.at[index], recv_sem=xs_recv.at[index],
            device_id=across, device_id_type=mesh_kind,
        )
        far.start()
        near = pltpu.make_async_remote_copy(
            src_ref=block, dst_ref=block, send_sem=cs_send.at[index], recv_sem=cs_recv.at[index],
            device_id=partner, device_id_type=mesh_kind,
        )
        near.start()
        second.append((far, near))
        if index >= 1:
            third.append(relay(index - 1, second[index - 1][0]))
    third.append(relay(count - 1, second[count - 1][0]))
    for index in range(count):
        own, copies = first[index]
        for copy in copies:
            copy.wait_send()
        far, near = second[index]
        far.wait_send()
        near.wait_send()
        near.wait_recv()
        third[index].wait_send()
        third[index].wait_recv()


def dispatch(wires):
    groups = wires[0].shape[0]
    count = len(wires)
    tail = wires[0].shape[1:]
    dma = pltpu.SemaphoreType.DMA
    return pl.pallas_call(
        functools.partial(dispatch_kernel, groups),
        out_shape=[jax.ShapeDtypeStruct((2, 2, groups) + tail, wires[0].dtype)] * count,
        in_specs=[pl.BlockSpec(memory_space=pl.ANY)] * count,
        out_specs=[pl.BlockSpec(memory_space=pl.ANY)] * count,
        scratch_shapes=[
            dma((count,)),
            dma((count, groups)),
            dma((count, groups)),
            dma((count,)),
            dma((count,)),
            dma((count,)),
            dma((count,)),
            dma((count,)),
            dma((count,)),
        ],
        compiler_params=pltpu.CompilerParams(collective_id=0, has_side_effects=True),
    )(*wires)


def to_wire(rows, *lead):
    return rows.reshape(*lead, -1, 128)


def return_kernel(groups, *refs):
    count = len(refs) - 4
    sources = refs[:count]
    out, local_sem, send1, recv1 = refs[count:]
    mesh_kind = pl.DeviceIdType.MESH
    pipe = lax.axis_index("pipe")
    me = lax.axis_index("eg")
    chip = lax.axis_index("ez")
    core = lax.axis_index("ec")
    peers = [(pipe, lax.rem(me + step, groups), chip, core) for step in range(1, groups)]
    barrier = pltpu.get_barrier_semaphore()
    for peer in peers:
        pl.semaphore_signal(barrier, 1, device_id=peer, device_id_type=mesh_kind)
    pl.semaphore_wait(barrier, len(peers))
    started = []
    for index, source in enumerate(sources):
        own = pltpu.make_async_copy(source.at[me], out.at[index, me], local_sem.at[index])
        own.start()
        copies = []
        for step in range(1, groups):
            copy = pltpu.make_async_remote_copy(
                src_ref=source.at[peers[step - 1][1]],
                dst_ref=out.at[index, me],
                send_sem=send1.at[index, step],
                recv_sem=recv1.at[index, step],
                device_id=peers[step - 1],
                device_id_type=mesh_kind,
            )
            copy.start()
            copies.append(copy)
        started.append((own, copies))
    for own, copies in started:
        own.wait()
        for copy in copies:
            copy.wait_send()
            copy.wait_recv()


def send_home(wires, tag):
    groups = wires[0].shape[0]
    count = len(wires)
    dma = pltpu.SemaphoreType.DMA
    return pl.pallas_call(
        functools.partial(return_kernel, groups),
        out_shape=jax.ShapeDtypeStruct((count,) + wires[0].shape, wires[0].dtype),
        in_specs=[pl.BlockSpec(memory_space=pl.ANY)] * count,
        out_specs=pl.BlockSpec(memory_space=pl.ANY),
        scratch_shapes=[dma((count,)), dma((count, groups)), dma((count, groups))],
        compiler_params=pltpu.CompilerParams(collective_id=tag, has_side_effects=True),
    )(*wires)


def group_sum(parts, experts):
    model_width = parts.shape[-1]
    blocks = parts.reshape(2, 2, -1, model_width)
    pair = lax.psum_scatter(blocks, "ec", scatter_dimension=0, tiled=True)
    pair = pair.reshape(blocks.shape[1:])
    other = lax.all_to_all(pair, "ez", split_axis=0, concat_axis=0, tiled=True)
    summed = jnp.sum(other.astype(jnp.float32), axis=0).astype(jnp.bfloat16)
    return to_wire(summed, experts)


def expert_forward(rows, up_proj, down_proj):
    pre = jnp.einsum("...d,df->...f", rows, up_proj, preferred_element_type=jnp.float32)
    act = jax.nn.silu(pre).astype(jnp.bfloat16)
    return jnp.einsum(
        "...f,fd->...d", act, down_proj, preferred_element_type=jnp.float32
    ).astype(jnp.bfloat16)


def expert_backward(rows, grad_rows, up_proj, down_proj):
    pre = jnp.einsum("...d,df->...f", rows, up_proj, preferred_element_type=jnp.float32)
    act = jax.nn.silu(pre).astype(jnp.bfloat16)
    dact = jnp.einsum("...d,fd->...f", grad_rows, down_proj, preferred_element_type=jnp.float32)
    dpre = (dact * silu_grad(pre)).astype(jnp.bfloat16)
    dpart = jnp.einsum(
        "...f,df->...d", dpre, up_proj, preferred_element_type=jnp.float32
    ).astype(jnp.bfloat16)
    grad_up = jnp.einsum("rd,rf->df", rows, dpre, preferred_element_type=jnp.float32)
    grad_down = jnp.einsum("rf,rd->fd", act, grad_rows, preferred_element_type=jnp.float32)
    return (dpart, grad_up, grad_down)


def local(
    fwd_acts, fwd_routes, fwd_gates, back_acts, back_routes, back_gates, back_grads, w_up, w_down
):
    devices = lax.axis_size("eg") * GROUP
    experts = devices // GROUP
    tok_rows = fwd_acts.shape[1]
    top_count = fwd_routes.shape[2]
    slot_cap = GROUP * (5 * tok_rows * top_count // (4 * devices))
    up_proj = w_up[0, 0]
    down_proj = w_down[0, 0]
    fwd_input = fwd_acts[0]
    back_input = back_acts[0]
    out_grad = back_grads[0]
    plain_f, gated_f = tables(fwd_routes[0], fwd_gates[0], experts, slot_cap)
    plain_b, gated_b = tables(back_routes[0], back_gates[0], experts, slot_cap)
    buffer_f = gather_rows(plain_f, fwd_input)
    buffer_x = gather_rows(plain_b, back_input)
    buffer_g = lax.dot_general(
        gated_b, out_grad.astype(jnp.float32), (((0,), (0,)), ((), ())), precision=HIGH
    ).astype(jnp.bfloat16)
    model_width = fwd_input.shape[-1]
    got = dispatch([to_wire(b, experts) for b in (buffer_f, buffer_x, buffer_g)])
    got_f, got_x, got_g = [got[index].reshape(-1, model_width) for index in range(3)]
    part = expert_forward(got_f, up_proj, down_proj)
    wire_f = group_sum(part, experts)
    dpart, grad_up, grad_down = expert_backward(got_x, got_g, up_proj, down_proj)
    wire_b = group_sum(dpart, experts)
    summed_f = send_home([wire_f], 1)[0].reshape(-1, model_width).astype(jnp.float32)
    summed_b = send_home([wire_b], 2)[0].reshape(-1, model_width).astype(jnp.float32)
    merged = jnp.dot(gated_f, summed_f, precision=HIGH)
    section_out = (fwd_input.astype(jnp.float32) + merged).astype(jnp.bfloat16)
    spread_back = jnp.dot(plain_b, summed_b, precision=HIGH)
    section_grad = (out_grad.astype(jnp.float32) + spread_back).astype(jnp.bfloat16)
    fwd_next = passed_along(section_out[None], "pipe", 1)
    back_next = passed_along(section_grad[None], "pipe", -1)
    return (fwd_next, back_next, grad_up[None, None], grad_down[None, None])


def solution(mesh):
    groups = mesh.shape["expert"] // GROUP
    devices = mesh.devices.reshape(mesh.shape["pipe"], groups, 2, GROUP // 2)
    mesh = jax.sharding.Mesh(devices, ("pipe", "eg", "ez", "ec"))
    in_specs = (
        P("pipe", ("eg", "ez", "ec"), None),
        P("pipe", ("eg", "ez", "ec"), None),
        P("pipe", ("eg", "ez", "ec"), None),
        P("pipe", ("eg", "ez", "ec"), None),
        P("pipe", ("eg", "ez", "ec"), None),
        P("pipe", ("eg", "ez", "ec"), None),
        P("pipe", ("eg", "ez", "ec"), None),
        P("pipe", ("eg", "ez", "ec"), None, None),
        P("pipe", ("eg", "ez", "ec"), None, None),
    )
    out_specs = (
        P("pipe", ("eg", "ez", "ec"), None),
        P("pipe", ("eg", "ez", "ec"), None),
        P("pipe", ("eg", "ez", "ec"), None, None),
        P("pipe", ("eg", "ez", "ec"), None, None),
    )
    return jax.shard_map(local, mesh=mesh, in_specs=in_specs, out_specs=out_specs, check_vma=False)
```

```python
import jax
import jax.numpy as jnp
from jax import lax
from jax.sharding import PartitionSpec as P
from jax.experimental import pallas as pl
from jax.experimental.pallas import tpu as pltpu
import functools

GROUP = 4


HIGH = lax.Precision.HIGHEST


def passed_along(value, axis, steps):
    count = lax.axis_size(axis)
    pairs = [(source, (source + steps) % count) for source in range(count)]
    return lax.ppermute(value, axis, pairs)


def silu_grad(value):
    sigma = jax.nn.sigmoid(value)
    return sigma * (1.0 + value * (1.0 - sigma))


def tables(routes, gates, experts, slot_cap):
    tok_rows, top_count = routes.shape
    flat = routes.reshape(tok_rows * top_count)
    onehot = (flat[:, None] == jnp.arange(experts, dtype=jnp.int32)[None, :]).astype(jnp.int32)
    before = jnp.cumsum(onehot, axis=0) - onehot
    slots = jnp.sum(before * onehot, axis=1)
    places = flat * slot_cap + slots
    columns = jnp.arange(experts * slot_cap, dtype=jnp.int32)
    hits = (
        (places[:, None] == columns[None, :])
        .astype(jnp.float32)
        .reshape(tok_rows, top_count, experts * slot_cap)
    )
    plain = jnp.sum(hits, axis=1)
    gated = jnp.sum(hits * gates[:, :, None], axis=1)
    return (plain, gated)


def gather_rows(plain, values):
    return lax.dot_general(
        plain.astype(jnp.bfloat16),
        values,
        (((0,), (0,)), ((), ())),
        preferred_element_type=jnp.float32,
    ).astype(jnp.bfloat16)


def to_wire(rows, *lead):
    return rows.reshape(*lead, -1, 128)


def dispatch_kernel(groups, *refs):
    sources = refs[:3]
    outs = refs[3:6]
    local_sem, send1, recv1, xs_send, xs_recv, cs_send, cs_recv, fw_send, fw_recv = refs[6:]
    mesh_kind = pl.DeviceIdType.MESH
    pipe = lax.axis_index("pipe")
    me = lax.axis_index("eg")
    chip = lax.axis_index("ez")
    core = lax.axis_index("ec")
    across = (pipe, me, 1 - chip, core)
    partner = (pipe, me, chip, 1 - core)
    peers = [(pipe, lax.rem(me + step, groups), chip, core) for step in range(1, groups)]
    barrier = pltpu.get_barrier_semaphore()
    for peer in peers + [across, partner]:
        pl.semaphore_signal(barrier, 1, device_id=peer, device_id_type=mesh_kind)
    pl.semaphore_wait(barrier, len(peers) + 2)
    def launch(index):
        source = sources[index]
        own = pltpu.make_async_copy(source.at[me], outs[index].at[core, chip, me], local_sem.at[index])
        own.start()
        copies = []
        for step in range(1, groups):
            copy = pltpu.make_async_remote_copy(
                src_ref=source.at[peers[step - 1][1]],
                dst_ref=outs[index].at[core, chip, me],
                send_sem=send1.at[index, step],
                recv_sem=recv1.at[index, step],
                device_id=peers[step - 1],
                device_id_type=mesh_kind,
            )
            copy.start()
            copies.append(copy)
        return own, copies

    def relay(index, far):
        far.wait_recv()
        held = outs[index].at[core, 1 - chip]
        onward = pltpu.make_async_remote_copy(
            src_ref=held, dst_ref=held, send_sem=fw_send.at[index], recv_sem=fw_recv.at[index],
            device_id=partner, device_id_type=mesh_kind,
        )
        onward.start()
        return onward

    count = len(sources)
    first = [launch(0)]
    second = []
    third = []
    for index in range(count):
        own, copies = first[index]
        own.wait()
        for copy in copies:
            copy.wait_recv()
        if index + 1 < count:
            first.append(launch(index + 1))
        block = outs[index].at[core, chip]
        far = pltpu.make_async_remote_copy(
            src_ref=block, dst_ref=block, send_sem=xs_send.at[index], recv_sem=xs_recv.at[index],
            device_id=across, device_id_type=mesh_kind,
        )
        far.start()
        near = pltpu.make_async_remote_copy(
            src_ref=block, dst_ref=block, send_sem=cs_send.at[index], recv_sem=cs_recv.at[index],
            device_id=partner, device_id_type=mesh_kind,
        )
        near.start()
        second.append((far, near))
        if index >= 1:
            third.append(relay(index - 1, second[index - 1][0]))
    third.append(relay(count - 1, second[count - 1][0]))
    for index in range(count):
        own, copies = first[index]
        for copy in copies:
            copy.wait_send()
        far, near = second[index]
        far.wait_send()
        near.wait_send()
        near.wait_recv()
        third[index].wait_send()
        third[index].wait_recv()


def dispatch(wires):
    groups = wires[0].shape[0]
    count = len(wires)
    tail = wires[0].shape[1:]
    dma = pltpu.SemaphoreType.DMA
    return pl.pallas_call(
        functools.partial(dispatch_kernel, groups),
        out_shape=[jax.ShapeDtypeStruct((2, 2, groups) + tail, wires[0].dtype)] * count,
        in_specs=[pl.BlockSpec(memory_space=pl.ANY)] * count,
        out_specs=[pl.BlockSpec(memory_space=pl.ANY)] * count,
        scratch_shapes=[
            dma((count,)),
            dma((count, groups)),
            dma((count, groups)),
            dma((count,)),
            dma((count,)),
            dma((count,)),
            dma((count,)),
            dma((count,)),
            dma((count,)),
        ],
        compiler_params=pltpu.CompilerParams(collective_id=0, has_side_effects=True),
    )(*wires)


def to_wire(rows, *lead):
    return rows.reshape(*lead, -1, 128)


def return_kernel(groups, *refs):
    count = len(refs) - 4
    sources = refs[:count]
    out, local_sem, send1, recv1 = refs[count:]
    mesh_kind = pl.DeviceIdType.MESH
    pipe = lax.axis_index("pipe")
    me = lax.axis_index("eg")
    chip = lax.axis_index("ez")
    core = lax.axis_index("ec")
    peers = [(pipe, lax.rem(me + step, groups), chip, core) for step in range(1, groups)]
    barrier = pltpu.get_barrier_semaphore()
    for peer in peers:
        pl.semaphore_signal(barrier, 1, device_id=peer, device_id_type=mesh_kind)
    pl.semaphore_wait(barrier, len(peers))
    started = []
    for index, source in enumerate(sources):
        own = pltpu.make_async_copy(source.at[me], out.at[index, me], local_sem.at[index])
        own.start()
        copies = []
        for step in range(1, groups):
            copy = pltpu.make_async_remote_copy(
                src_ref=source.at[peers[step - 1][1]],
                dst_ref=out.at[index, me],
                send_sem=send1.at[index, step],
                recv_sem=recv1.at[index, step],
                device_id=peers[step - 1],
                device_id_type=mesh_kind,
            )
            copy.start()
            copies.append(copy)
        started.append((own, copies))
    for own, copies in started:
        own.wait()
        for copy in copies:
            copy.wait_send()
            copy.wait_recv()


def send_home(wires, tag):
    groups = wires[0].shape[0]
    count = len(wires)
    dma = pltpu.SemaphoreType.DMA
    return pl.pallas_call(
        functools.partial(return_kernel, groups),
        out_shape=jax.ShapeDtypeStruct((count,) + wires[0].shape, wires[0].dtype),
        in_specs=[pl.BlockSpec(memory_space=pl.ANY)] * count,
        out_specs=pl.BlockSpec(memory_space=pl.ANY),
        scratch_shapes=[dma((count,)), dma((count, groups)), dma((count, groups))],
        compiler_params=pltpu.CompilerParams(collective_id=tag, has_side_effects=True),
    )(*wires)


def group_sum(parts, experts):
    model_width = parts.shape[-1]
    blocks = parts.reshape(2, 2, -1, model_width)
    pair = lax.psum_scatter(blocks, "ec", scatter_dimension=0, tiled=True)
    pair = pair.reshape(blocks.shape[1:])
    summed = lax.psum_scatter(pair, "ez", scatter_dimension=0, tiled=True)
    summed = summed.reshape(pair.shape[1:])
    return to_wire(summed, experts)


def expert_forward(rows, up_proj, down_proj):
    pre = jnp.einsum("...d,df->...f", rows, up_proj, preferred_element_type=jnp.float32)
    act = jax.nn.silu(pre).astype(jnp.bfloat16)
    return jnp.einsum(
        "...f,fd->...d", act, down_proj, preferred_element_type=jnp.float32
    ).astype(jnp.bfloat16)


def expert_backward(rows, grad_rows, up_proj, down_proj):
    pre = jnp.einsum("...d,df->...f", rows, up_proj, preferred_element_type=jnp.float32)
    act = jax.nn.silu(pre).astype(jnp.bfloat16)
    dact = jnp.einsum("...d,fd->...f", grad_rows, down_proj, preferred_element_type=jnp.float32)
    dpre = (dact * silu_grad(pre)).astype(jnp.bfloat16)
    dpart = jnp.einsum(
        "...f,df->...d", dpre, up_proj, preferred_element_type=jnp.float32
    ).astype(jnp.bfloat16)
    grad_up = jnp.einsum("rd,rf->df", rows, dpre, preferred_element_type=jnp.float32)
    grad_down = jnp.einsum("rf,rd->fd", act, grad_rows, preferred_element_type=jnp.float32)
    return (dpart, grad_up, grad_down)


def local(
    fwd_acts, fwd_routes, fwd_gates, back_acts, back_routes, back_gates, back_grads, w_up, w_down
):
    devices = lax.axis_size("eg") * GROUP
    experts = devices // GROUP
    tok_rows = fwd_acts.shape[1]
    top_count = fwd_routes.shape[2]
    slot_cap = GROUP * (5 * tok_rows * top_count // (4 * devices))
    up_proj = w_up[0, 0]
    down_proj = w_down[0, 0]
    fwd_input = fwd_acts[0]
    back_input = back_acts[0]
    out_grad = back_grads[0]
    plain_f, gated_f = tables(fwd_routes[0], fwd_gates[0], experts, slot_cap)
    plain_b, gated_b = tables(back_routes[0], back_gates[0], experts, slot_cap)
    buffer_f = gather_rows(plain_f, fwd_input)
    buffer_x = gather_rows(plain_b, back_input)
    buffer_g = lax.dot_general(
        gated_b, out_grad.astype(jnp.float32), (((0,), (0,)), ((), ())), precision=HIGH
    ).astype(jnp.bfloat16)
    model_width = fwd_input.shape[-1]
    got = dispatch([to_wire(b, experts) for b in (buffer_f, buffer_x, buffer_g)])
    got_f, got_x, got_g = [got[index].reshape(-1, model_width) for index in range(3)]
    part = expert_forward(got_f, up_proj, down_proj)
    wire_f = group_sum(part, experts)
    dpart, grad_up, grad_down = expert_backward(got_x, got_g, up_proj, down_proj)
    wire_b = group_sum(dpart, experts)
    summed_f = send_home([wire_f], 1)[0].reshape(-1, model_width).astype(jnp.float32)
    summed_b = send_home([wire_b], 2)[0].reshape(-1, model_width).astype(jnp.float32)
    merged = jnp.dot(gated_f, summed_f, precision=HIGH)
    section_out = (fwd_input.astype(jnp.float32) + merged).astype(jnp.bfloat16)
    spread_back = jnp.dot(plain_b, summed_b, precision=HIGH)
    section_grad = (out_grad.astype(jnp.float32) + spread_back).astype(jnp.bfloat16)
    fwd_next = passed_along(section_out[None], "pipe", 1)
    back_next = passed_along(section_grad[None], "pipe", -1)
    return (fwd_next, back_next, grad_up[None, None], grad_down[None, None])


def solution(mesh):
    groups = mesh.shape["expert"] // GROUP
    devices = mesh.devices.reshape(mesh.shape["pipe"], groups, 2, GROUP // 2)
    mesh = jax.sharding.Mesh(devices, ("pipe", "eg", "ez", "ec"))
    in_specs = (
        P("pipe", ("eg", "ez", "ec"), None),
        P("pipe", ("eg", "ez", "ec"), None),
        P("pipe", ("eg", "ez", "ec"), None),
        P("pipe", ("eg", "ez", "ec"), None),
        P("pipe", ("eg", "ez", "ec"), None),
        P("pipe", ("eg", "ez", "ec"), None),
        P("pipe", ("eg", "ez", "ec"), None),
        P("pipe", ("eg", "ez", "ec"), None, None),
        P("pipe", ("eg", "ez", "ec"), None, None),
    )
    out_specs = (
        P("pipe", ("eg", "ez", "ec"), None),
        P("pipe", ("eg", "ez", "ec"), None),
        P("pipe", ("eg", "ez", "ec"), None, None),
        P("pipe", ("eg", "ez", "ec"), None, None),
    )
    return jax.shard_map(local, mesh=mesh, in_specs=in_specs, out_specs=out_specs, check_vma=False)
```

```python
import jax
import jax.numpy as jnp
from jax import lax
from jax.sharding import PartitionSpec as P
from jax.experimental import pallas as pl
from jax.experimental.pallas import tpu as pltpu
import functools

GROUP = 4


HIGH = lax.Precision.HIGHEST


def passed_along(value, axis, steps):
    count = lax.axis_size(axis)
    pairs = [(source, (source + steps) % count) for source in range(count)]
    return lax.ppermute(value, axis, pairs)


def silu_grad(value):
    sigma = jax.nn.sigmoid(value)
    return sigma * (1.0 + value * (1.0 - sigma))


def tables(routes, gates, experts, slot_cap):
    tok_rows, top_count = routes.shape
    flat = routes.reshape(tok_rows * top_count)
    onehot = (flat[:, None] == jnp.arange(experts, dtype=jnp.int32)[None, :]).astype(jnp.int32)
    before = jnp.cumsum(onehot, axis=0) - onehot
    slots = jnp.sum(before * onehot, axis=1)
    places = flat * slot_cap + slots
    columns = jnp.arange(experts * slot_cap, dtype=jnp.int32)
    hits = (
        (places[:, None] == columns[None, :])
        .astype(jnp.float32)
        .reshape(tok_rows, top_count, experts * slot_cap)
    )
    plain = jnp.sum(hits, axis=1)
    gated = jnp.sum(hits * gates[:, :, None], axis=1)
    return (plain, gated)


def gather_rows(plain, values):
    return lax.dot_general(
        plain.astype(jnp.bfloat16),
        values,
        (((0,), (0,)), ((), ())),
        preferred_element_type=jnp.float32,
    ).astype(jnp.bfloat16)


def to_wire(rows, *lead):
    return rows.reshape(*lead, -1, 128)


def dispatch_kernel(groups, *refs):
    sources = refs[:3]
    outs = refs[3:6]
    local_sem, send1, recv1, xs_send, xs_recv, cs_send, cs_recv, fw_send, fw_recv = refs[6:]
    mesh_kind = pl.DeviceIdType.MESH
    pipe = lax.axis_index("pipe")
    me = lax.axis_index("eg")
    chip = lax.axis_index("ez")
    core = lax.axis_index("ec")
    across = (pipe, me, 1 - chip, core)
    partner = (pipe, me, chip, 1 - core)
    peers = [(pipe, lax.rem(me + step, groups), chip, core) for step in range(1, groups)]
    barrier = pltpu.get_barrier_semaphore()
    for peer in peers + [across, partner]:
        pl.semaphore_signal(barrier, 1, device_id=peer, device_id_type=mesh_kind)
    pl.semaphore_wait(barrier, len(peers) + 2)
    def launch(index):
        source = sources[index]
        own = pltpu.make_async_copy(source.at[me], outs[index].at[core, chip, me], local_sem.at[index])
        own.start()
        copies = []
        for step in range(1, groups):
            copy = pltpu.make_async_remote_copy(
                src_ref=source.at[peers[step - 1][1]],
                dst_ref=outs[index].at[core, chip, me],
                send_sem=send1.at[index, step],
                recv_sem=recv1.at[index, step],
                device_id=peers[step - 1],
                device_id_type=mesh_kind,
            )
            copy.start()
            copies.append(copy)
        return own, copies

    def relay(index, far):
        far.wait_recv()
        held = outs[index].at[core, 1 - chip]
        onward = pltpu.make_async_remote_copy(
            src_ref=held, dst_ref=held, send_sem=fw_send.at[index], recv_sem=fw_recv.at[index],
            device_id=partner, device_id_type=mesh_kind,
        )
        onward.start()
        return onward

    count = len(sources)
    first = [launch(0)]
    second = []
    third = []
    for index in range(count):
        own, copies = first[index]
        own.wait()
        for copy in copies:
            copy.wait_recv()
        if index + 1 < count:
            first.append(launch(index + 1))
        block = outs[index].at[core, chip]
        far = pltpu.make_async_remote_copy(
            src_ref=block, dst_ref=block, send_sem=xs_send.at[index], recv_sem=xs_recv.at[index],
            device_id=across, device_id_type=mesh_kind,
        )
        far.start()
        near = pltpu.make_async_remote_copy(
            src_ref=block, dst_ref=block, send_sem=cs_send.at[index], recv_sem=cs_recv.at[index],
            device_id=partner, device_id_type=mesh_kind,
        )
        near.start()
        second.append((far, near))
        if index >= 1:
            third.append(relay(index - 1, second[index - 1][0]))
    third.append(relay(count - 1, second[count - 1][0]))
    for index in range(count):
        own, copies = first[index]
        for copy in copies:
            copy.wait_send()
        far, near = second[index]
        far.wait_send()
        near.wait_send()
        near.wait_recv()
        third[index].wait_send()
        third[index].wait_recv()


def dispatch(wires):
    groups = wires[0].shape[0]
    count = len(wires)
    tail = wires[0].shape[1:]
    dma = pltpu.SemaphoreType.DMA
    return pl.pallas_call(
        functools.partial(dispatch_kernel, groups),
        out_shape=[jax.ShapeDtypeStruct((2, 2, groups) + tail, wires[0].dtype)] * count,
        in_specs=[pl.BlockSpec(memory_space=pl.ANY)] * count,
        out_specs=[pl.BlockSpec(memory_space=pl.ANY)] * count,
        scratch_shapes=[
            dma((count,)),
            dma((count, groups)),
            dma((count, groups)),
            dma((count,)),
            dma((count,)),
            dma((count,)),
            dma((count,)),
            dma((count,)),
            dma((count,)),
        ],
        compiler_params=pltpu.CompilerParams(collective_id=0, has_side_effects=True),
    )(*wires)


def to_wire(rows, *lead):
    return rows.reshape(*lead, -1, 128)


def return_kernel(groups, *refs):
    count = len(refs) - 4
    sources = refs[:count]
    out, local_sem, send1, recv1 = refs[count:]
    mesh_kind = pl.DeviceIdType.MESH
    pipe = lax.axis_index("pipe")
    me = lax.axis_index("eg")
    chip = lax.axis_index("ez")
    core = lax.axis_index("ec")
    peers = [(pipe, lax.rem(me + step, groups), chip, core) for step in range(1, groups)]
    barrier = pltpu.get_barrier_semaphore()
    for peer in peers:
        pl.semaphore_signal(barrier, 1, device_id=peer, device_id_type=mesh_kind)
    pl.semaphore_wait(barrier, len(peers))
    started = []
    for index, source in enumerate(sources):
        own = pltpu.make_async_copy(source.at[me], out.at[index, me], local_sem.at[index])
        own.start()
        copies = []
        for step in range(1, groups):
            copy = pltpu.make_async_remote_copy(
                src_ref=source.at[peers[step - 1][1]],
                dst_ref=out.at[index, me],
                send_sem=send1.at[index, step],
                recv_sem=recv1.at[index, step],
                device_id=peers[step - 1],
                device_id_type=mesh_kind,
            )
            copy.start()
            copies.append(copy)
        started.append((own, copies))
    for own, copies in started:
        own.wait()
        for copy in copies:
            copy.wait_send()
            copy.wait_recv()


def send_home(wires, tag):
    groups = wires[0].shape[0]
    count = len(wires)
    dma = pltpu.SemaphoreType.DMA
    return pl.pallas_call(
        functools.partial(return_kernel, groups),
        out_shape=jax.ShapeDtypeStruct((count,) + wires[0].shape, wires[0].dtype),
        in_specs=[pl.BlockSpec(memory_space=pl.ANY)] * count,
        out_specs=pl.BlockSpec(memory_space=pl.ANY),
        scratch_shapes=[dma((count,)), dma((count, groups)), dma((count, groups))],
        compiler_params=pltpu.CompilerParams(collective_id=tag, has_side_effects=True),
    )(*wires)


def group_sum(parts, experts):
    model_width = parts.shape[-1]
    blocks = parts.reshape(2, 2, -1, model_width)
    pair = lax.psum_scatter(blocks, "ec", scatter_dimension=0, tiled=True)
    pair = pair.reshape(blocks.shape[1:])
    chip = lax.axis_index("ez")
    keep = lax.dynamic_index_in_dim(pair, chip, axis=0, keepdims=False)
    send = lax.dynamic_index_in_dim(pair, 1 - chip, axis=0, keepdims=False)
    got = passed_along(send, "ez", 1)
    summed = (keep.astype(jnp.float32) + got.astype(jnp.float32)).astype(jnp.bfloat16)
    return to_wire(summed, experts)


def expert_forward(rows, up_proj, down_proj):
    pre = jnp.einsum("...d,df->...f", rows, up_proj, preferred_element_type=jnp.float32)
    act = jax.nn.silu(pre).astype(jnp.bfloat16)
    return jnp.einsum(
        "...f,fd->...d", act, down_proj, preferred_element_type=jnp.float32
    ).astype(jnp.bfloat16)


def expert_backward(rows, grad_rows, up_proj, down_proj):
    pre = jnp.einsum("...d,df->...f", rows, up_proj, preferred_element_type=jnp.float32)
    act = jax.nn.silu(pre).astype(jnp.bfloat16)
    dact = jnp.einsum("...d,fd->...f", grad_rows, down_proj, preferred_element_type=jnp.float32)
    dpre = (dact * silu_grad(pre)).astype(jnp.bfloat16)
    dpart = jnp.einsum(
        "...f,df->...d", dpre, up_proj, preferred_element_type=jnp.float32
    ).astype(jnp.bfloat16)
    grad_up = jnp.einsum("rd,rf->df", rows, dpre, preferred_element_type=jnp.float32)
    grad_down = jnp.einsum("rf,rd->fd", act, grad_rows, preferred_element_type=jnp.float32)
    return (dpart, grad_up, grad_down)


def local(
    fwd_acts, fwd_routes, fwd_gates, back_acts, back_routes, back_gates, back_grads, w_up, w_down
):
    devices = lax.axis_size("eg") * GROUP
    experts = devices // GROUP
    tok_rows = fwd_acts.shape[1]
    top_count = fwd_routes.shape[2]
    slot_cap = GROUP * (5 * tok_rows * top_count // (4 * devices))
    up_proj = w_up[0, 0]
    down_proj = w_down[0, 0]
    fwd_input = fwd_acts[0]
    back_input = back_acts[0]
    out_grad = back_grads[0]
    plain_f, gated_f = tables(fwd_routes[0], fwd_gates[0], experts, slot_cap)
    plain_b, gated_b = tables(back_routes[0], back_gates[0], experts, slot_cap)
    buffer_f = gather_rows(plain_f, fwd_input)
    buffer_x = gather_rows(plain_b, back_input)
    buffer_g = lax.dot_general(
        gated_b, out_grad.astype(jnp.float32), (((0,), (0,)), ((), ())), precision=HIGH
    ).astype(jnp.bfloat16)
    model_width = fwd_input.shape[-1]
    got = dispatch([to_wire(b, experts) for b in (buffer_f, buffer_x, buffer_g)])
    got_f, got_x, got_g = [got[index].reshape(-1, model_width) for index in range(3)]
    part = expert_forward(got_f, up_proj, down_proj)
    wire_f = group_sum(part, experts)
    dpart, grad_up, grad_down = expert_backward(got_x, got_g, up_proj, down_proj)
    wire_b = group_sum(dpart, experts)
    summed_f = send_home([wire_f], 1)[0].reshape(-1, model_width).astype(jnp.float32)
    summed_b = send_home([wire_b], 2)[0].reshape(-1, model_width).astype(jnp.float32)
    merged = jnp.dot(gated_f, summed_f, precision=HIGH)
    section_out = (fwd_input.astype(jnp.float32) + merged).astype(jnp.bfloat16)
    spread_back = jnp.dot(plain_b, summed_b, precision=HIGH)
    section_grad = (out_grad.astype(jnp.float32) + spread_back).astype(jnp.bfloat16)
    fwd_next = passed_along(section_out[None], "pipe", 1)
    back_next = passed_along(section_grad[None], "pipe", -1)
    return (fwd_next, back_next, grad_up[None, None], grad_down[None, None])


def solution(mesh):
    groups = mesh.shape["expert"] // GROUP
    devices = mesh.devices.reshape(mesh.shape["pipe"], groups, 2, GROUP // 2)
    mesh = jax.sharding.Mesh(devices, ("pipe", "eg", "ez", "ec"))
    in_specs = (
        P("pipe", ("eg", "ez", "ec"), None),
        P("pipe", ("eg", "ez", "ec"), None),
        P("pipe", ("eg", "ez", "ec"), None),
        P("pipe", ("eg", "ez", "ec"), None),
        P("pipe", ("eg", "ez", "ec"), None),
        P("pipe", ("eg", "ez", "ec"), None),
        P("pipe", ("eg", "ez", "ec"), None),
        P("pipe", ("eg", "ez", "ec"), None, None),
        P("pipe", ("eg", "ez", "ec"), None, None),
    )
    out_specs = (
        P("pipe", ("eg", "ez", "ec"), None),
        P("pipe", ("eg", "ez", "ec"), None),
        P("pipe", ("eg", "ez", "ec"), None, None),
        P("pipe", ("eg", "ez", "ec"), None, None),
    )
    return jax.shard_map(local, mesh=mesh, in_specs=in_specs, out_specs=out_specs, check_vma=False)
```

```python
import jax
import jax.numpy as jnp
from jax import lax
from jax.sharding import PartitionSpec as P
from jax.experimental import pallas as pl
from jax.experimental.pallas import tpu as pltpu
import functools

GROUP = 4


HIGH = lax.Precision.HIGHEST


def passed_along(value, axis, steps):
    count = lax.axis_size(axis)
    pairs = [(source, (source + steps) % count) for source in range(count)]
    return lax.ppermute(value, axis, pairs)


def silu_grad(value):
    sigma = jax.nn.sigmoid(value)
    return sigma * (1.0 + value * (1.0 - sigma))


def tables(routes, gates, experts, slot_cap):
    tok_rows, top_count = routes.shape
    flat = routes.reshape(tok_rows * top_count)
    onehot = (flat[:, None] == jnp.arange(experts, dtype=jnp.int32)[None, :]).astype(jnp.int32)
    before = jnp.cumsum(onehot, axis=0) - onehot
    slots = jnp.sum(before * onehot, axis=1)
    places = flat * slot_cap + slots
    columns = jnp.arange(experts * slot_cap, dtype=jnp.int32)
    hits = (
        (places[:, None] == columns[None, :])
        .astype(jnp.float32)
        .reshape(tok_rows, top_count, experts * slot_cap)
    )
    plain = jnp.sum(hits, axis=1)
    gated = jnp.sum(hits * gates[:, :, None], axis=1)
    return (plain, gated)


def gather_rows(plain, values):
    return lax.dot_general(
        plain.astype(jnp.bfloat16),
        values,
        (((0,), (0,)), ((), ())),
        preferred_element_type=jnp.float32,
    ).astype(jnp.bfloat16)


def to_wire(rows, *lead):
    return rows.reshape(*lead, -1, 128)


def dispatch_kernel(groups, *refs):
    sources = refs[:3]
    outs = refs[3:6]
    local_sem, send1, recv1, xs_send, xs_recv, cs_send, cs_recv, fw_send, fw_recv = refs[6:]
    mesh_kind = pl.DeviceIdType.MESH
    pipe = lax.axis_index("pipe")
    me = lax.axis_index("eg")
    chip = lax.axis_index("ez")
    core = lax.axis_index("ec")
    across = (pipe, me, 1 - chip, core)
    partner = (pipe, me, chip, 1 - core)
    peers = [(pipe, lax.rem(me + step, groups), chip, core) for step in range(1, groups)]
    barrier = pltpu.get_barrier_semaphore()
    for peer in peers + [across, partner]:
        pl.semaphore_signal(barrier, 1, device_id=peer, device_id_type=mesh_kind)
    pl.semaphore_wait(barrier, len(peers) + 2)
    def launch(index):
        source = sources[index]
        own = pltpu.make_async_copy(source.at[me], outs[index].at[core, chip, me], local_sem.at[index])
        own.start()
        copies = []
        for step in range(1, groups):
            copy = pltpu.make_async_remote_copy(
                src_ref=source.at[peers[step - 1][1]],
                dst_ref=outs[index].at[core, chip, me],
                send_sem=send1.at[index, step],
                recv_sem=recv1.at[index, step],
                device_id=peers[step - 1],
                device_id_type=mesh_kind,
            )
            copy.start()
            copies.append(copy)
        return own, copies

    def relay(index, far):
        far.wait_recv()
        held = outs[index].at[core, 1 - chip]
        onward = pltpu.make_async_remote_copy(
            src_ref=held, dst_ref=held, send_sem=fw_send.at[index], recv_sem=fw_recv.at[index],
            device_id=partner, device_id_type=mesh_kind,
        )
        onward.start()
        return onward

    count = len(sources)
    first = [launch(0)]
    second = []
    third = []
    for index in range(count):
        own, copies = first[index]
        own.wait()
        for copy in copies:
            copy.wait_recv()
        if index + 1 < count:
            first.append(launch(index + 1))
        block = outs[index].at[core, chip]
        far = pltpu.make_async_remote_copy(
            src_ref=block, dst_ref=block, send_sem=xs_send.at[index], recv_sem=xs_recv.at[index],
            device_id=across, device_id_type=mesh_kind,
        )
        far.start()
        near = pltpu.make_async_remote_copy(
            src_ref=block, dst_ref=block, send_sem=cs_send.at[index], recv_sem=cs_recv.at[index],
            device_id=partner, device_id_type=mesh_kind,
        )
        near.start()
        second.append((far, near))
        if index >= 1:
            third.append(relay(index - 1, second[index - 1][0]))
    third.append(relay(count - 1, second[count - 1][0]))
    for index in range(count):
        own, copies = first[index]
        for copy in copies:
            copy.wait_send()
        far, near = second[index]
        far.wait_send()
        near.wait_send()
        near.wait_recv()
        third[index].wait_send()
        third[index].wait_recv()


def dispatch(wires):
    groups = wires[0].shape[0]
    count = len(wires)
    tail = wires[0].shape[1:]
    dma = pltpu.SemaphoreType.DMA
    return pl.pallas_call(
        functools.partial(dispatch_kernel, groups),
        out_shape=[jax.ShapeDtypeStruct((2, 2, groups) + tail, wires[0].dtype)] * count,
        in_specs=[pl.BlockSpec(memory_space=pl.ANY)] * count,
        out_specs=[pl.BlockSpec(memory_space=pl.ANY)] * count,
        scratch_shapes=[
            dma((count,)),
            dma((count, groups)),
            dma((count, groups)),
            dma((count,)),
            dma((count,)),
            dma((count,)),
            dma((count,)),
            dma((count,)),
            dma((count,)),
        ],
        compiler_params=pltpu.CompilerParams(collective_id=0, has_side_effects=True),
    )(*wires)


def to_wire(rows, *lead):
    return rows.reshape(*lead, -1, 128)


def return_kernel(groups, *refs):
    count = len(refs) - 4
    sources = refs[:count]
    out, local_sem, send1, recv1 = refs[count:]
    mesh_kind = pl.DeviceIdType.MESH
    pipe = lax.axis_index("pipe")
    me = lax.axis_index("eg")
    chip = lax.axis_index("ez")
    core = lax.axis_index("ec")
    peers = [(pipe, lax.rem(me + step, groups), chip, core) for step in range(1, groups)]
    barrier = pltpu.get_barrier_semaphore()
    for peer in peers:
        pl.semaphore_signal(barrier, 1, device_id=peer, device_id_type=mesh_kind)
    pl.semaphore_wait(barrier, len(peers))
    started = []
    for index, source in enumerate(sources):
        own = pltpu.make_async_copy(source.at[me], out.at[index, me], local_sem.at[index])
        own.start()
        copies = []
        for step in range(1, groups):
            copy = pltpu.make_async_remote_copy(
                src_ref=source.at[peers[step - 1][1]],
                dst_ref=out.at[index, me],
                send_sem=send1.at[index, step],
                recv_sem=recv1.at[index, step],
                device_id=peers[step - 1],
                device_id_type=mesh_kind,
            )
            copy.start()
            copies.append(copy)
        started.append((own, copies))
    for own, copies in started:
        own.wait()
        for copy in copies:
            copy.wait_send()
            copy.wait_recv()


def send_home(wires, tag):
    groups = wires[0].shape[0]
    count = len(wires)
    dma = pltpu.SemaphoreType.DMA
    return pl.pallas_call(
        functools.partial(return_kernel, groups),
        out_shape=jax.ShapeDtypeStruct((count,) + wires[0].shape, wires[0].dtype),
        in_specs=[pl.BlockSpec(memory_space=pl.ANY)] * count,
        out_specs=pl.BlockSpec(memory_space=pl.ANY),
        scratch_shapes=[dma((count,)), dma((count, groups)), dma((count, groups))],
        compiler_params=pltpu.CompilerParams(collective_id=tag, has_side_effects=True),
    )(*wires)


def group_sum(parts, experts):
    model_width = parts.shape[-1]
    blocks = parts.reshape(2, 2, -1, model_width)
    core = lax.axis_index("ec")
    mine = lax.dynamic_index_in_dim(blocks, core, axis=0, keepdims=False)
    theirs = lax.dynamic_index_in_dim(blocks, 1 - core, axis=0, keepdims=False)
    came = passed_along(theirs, "ec", 1)
    pair = (mine.astype(jnp.float32) + came.astype(jnp.float32)).astype(jnp.bfloat16)
    chip = lax.axis_index("ez")
    keep = lax.dynamic_index_in_dim(pair, chip, axis=0, keepdims=False)
    send = lax.dynamic_index_in_dim(pair, 1 - chip, axis=0, keepdims=False)
    got = passed_along(send, "ez", 1)
    summed = (keep.astype(jnp.float32) + got.astype(jnp.float32)).astype(jnp.bfloat16)
    return to_wire(summed, experts)


def expert_forward(rows, up_proj, down_proj):
    pre = jnp.einsum("...d,df->...f", rows, up_proj, preferred_element_type=jnp.float32)
    act = jax.nn.silu(pre).astype(jnp.bfloat16)
    return jnp.einsum(
        "...f,fd->...d", act, down_proj, preferred_element_type=jnp.float32
    ).astype(jnp.bfloat16)


def expert_backward(rows, grad_rows, up_proj, down_proj):
    pre = jnp.einsum("...d,df->...f", rows, up_proj, preferred_element_type=jnp.float32)
    act = jax.nn.silu(pre).astype(jnp.bfloat16)
    dact = jnp.einsum("...d,fd->...f", grad_rows, down_proj, preferred_element_type=jnp.float32)
    dpre = (dact * silu_grad(pre)).astype(jnp.bfloat16)
    dpart = jnp.einsum(
        "...f,df->...d", dpre, up_proj, preferred_element_type=jnp.float32
    ).astype(jnp.bfloat16)
    grad_up = jnp.einsum("rd,rf->df", rows, dpre, preferred_element_type=jnp.float32)
    grad_down = jnp.einsum("rf,rd->fd", act, grad_rows, preferred_element_type=jnp.float32)
    return (dpart, grad_up, grad_down)


def local(
    fwd_acts, fwd_routes, fwd_gates, back_acts, back_routes, back_gates, back_grads, w_up, w_down
):
    devices = lax.axis_size("eg") * GROUP
    experts = devices // GROUP
    tok_rows = fwd_acts.shape[1]
    top_count = fwd_routes.shape[2]
    slot_cap = GROUP * (5 * tok_rows * top_count // (4 * devices))
    up_proj = w_up[0, 0]
    down_proj = w_down[0, 0]
    fwd_input = fwd_acts[0]
    back_input = back_acts[0]
    out_grad = back_grads[0]
    plain_f, gated_f = tables(fwd_routes[0], fwd_gates[0], experts, slot_cap)
    plain_b, gated_b = tables(back_routes[0], back_gates[0], experts, slot_cap)
    buffer_f = gather_rows(plain_f, fwd_input)
    buffer_x = gather_rows(plain_b, back_input)
    buffer_g = lax.dot_general(
        gated_b, out_grad.astype(jnp.float32), (((0,), (0,)), ((), ())), precision=HIGH
    ).astype(jnp.bfloat16)
    model_width = fwd_input.shape[-1]
    got = dispatch([to_wire(b, experts) for b in (buffer_f, buffer_x, buffer_g)])
    got_f, got_x, got_g = [got[index].reshape(-1, model_width) for index in range(3)]
    part = expert_forward(got_f, up_proj, down_proj)
    wire_f = group_sum(part, experts)
    dpart, grad_up, grad_down = expert_backward(got_x, got_g, up_proj, down_proj)
    wire_b = group_sum(dpart, experts)
    summed_f = send_home([wire_f], 1)[0].reshape(-1, model_width).astype(jnp.float32)
    summed_b = send_home([wire_b], 2)[0].reshape(-1, model_width).astype(jnp.float32)
    merged = jnp.dot(gated_f, summed_f, precision=HIGH)
    section_out = (fwd_input.astype(jnp.float32) + merged).astype(jnp.bfloat16)
    spread_back = jnp.dot(plain_b, summed_b, precision=HIGH)
    section_grad = (out_grad.astype(jnp.float32) + spread_back).astype(jnp.bfloat16)
    fwd_next = passed_along(section_out[None], "pipe", 1)
    back_next = passed_along(section_grad[None], "pipe", -1)
    return (fwd_next, back_next, grad_up[None, None], grad_down[None, None])


def solution(mesh):
    groups = mesh.shape["expert"] // GROUP
    devices = mesh.devices.reshape(mesh.shape["pipe"], groups, 2, GROUP // 2)
    mesh = jax.sharding.Mesh(devices, ("pipe", "eg", "ez", "ec"))
    in_specs = (
        P("pipe", ("eg", "ez", "ec"), None),
        P("pipe", ("eg", "ez", "ec"), None),
        P("pipe", ("eg", "ez", "ec"), None),
        P("pipe", ("eg", "ez", "ec"), None),
        P("pipe", ("eg", "ez", "ec"), None),
        P("pipe", ("eg", "ez", "ec"), None),
        P("pipe", ("eg", "ez", "ec"), None),
        P("pipe", ("eg", "ez", "ec"), None, None),
        P("pipe", ("eg", "ez", "ec"), None, None),
    )
    out_specs = (
        P("pipe", ("eg", "ez", "ec"), None),
        P("pipe", ("eg", "ez", "ec"), None),
        P("pipe", ("eg", "ez", "ec"), None, None),
        P("pipe", ("eg", "ez", "ec"), None, None),
    )
    return jax.shard_map(local, mesh=mesh, in_specs=in_specs, out_specs=out_specs, check_vma=False)
```

```python
import jax
import jax.numpy as jnp
from jax import lax
from jax.sharding import PartitionSpec as P
from jax.experimental import pallas as pl
from jax.experimental.pallas import tpu as pltpu
import functools

GROUP = 4


HIGH = lax.Precision.HIGHEST


def passed_along(value, axis, steps):
    count = lax.axis_size(axis)
    pairs = [(source, (source + steps) % count) for source in range(count)]
    return lax.ppermute(value, axis, pairs)


def silu_grad(value):
    sigma = jax.nn.sigmoid(value)
    return sigma * (1.0 + value * (1.0 - sigma))


def tables(routes, gates, experts, slot_cap):
    tok_rows, top_count = routes.shape
    flat = routes.reshape(tok_rows * top_count)
    onehot = (flat[:, None] == jnp.arange(experts, dtype=jnp.int32)[None, :]).astype(jnp.int32)
    before = jnp.cumsum(onehot, axis=0) - onehot
    slots = jnp.sum(before * onehot, axis=1)
    places = flat * slot_cap + slots
    columns = jnp.arange(experts * slot_cap, dtype=jnp.int32)
    hits = (
        (places[:, None] == columns[None, :])
        .astype(jnp.float32)
        .reshape(tok_rows, top_count, experts * slot_cap)
    )
    plain = jnp.sum(hits, axis=1)
    gated = jnp.sum(hits * gates[:, :, None], axis=1)
    return (plain, gated)


def gather_rows(plain, values):
    return lax.dot_general(
        plain.astype(jnp.bfloat16),
        values,
        (((0,), (0,)), ((), ())),
        preferred_element_type=jnp.float32,
    ).astype(jnp.bfloat16)


def to_wire(rows, *lead):
    return rows.reshape(*lead, -1, 128)


def dispatch_kernel(groups, *refs):
    sources = refs[:3]
    outs = refs[3:6]
    local_sem, send1, recv1, xs_send, xs_recv, cs_send, cs_recv, fw_send, fw_recv = refs[6:]
    mesh_kind = pl.DeviceIdType.MESH
    pipe = lax.axis_index("pipe")
    me = lax.axis_index("eg")
    chip = lax.axis_index("ez")
    core = lax.axis_index("ec")
    across = (pipe, me, 1 - chip, core)
    partner = (pipe, me, chip, 1 - core)
    peers = [(pipe, lax.rem(me + step, groups), chip, core) for step in range(1, groups)]
    barrier = pltpu.get_barrier_semaphore()
    for peer in peers + [across, partner]:
        pl.semaphore_signal(barrier, 1, device_id=peer, device_id_type=mesh_kind)
    pl.semaphore_wait(barrier, len(peers) + 2)
    def launch(index):
        source = sources[index]
        own = pltpu.make_async_copy(source.at[me], outs[index].at[core, chip, me], local_sem.at[index])
        own.start()
        copies = []
        for step in range(1, groups):
            copy = pltpu.make_async_remote_copy(
                src_ref=source.at[peers[step - 1][1]],
                dst_ref=outs[index].at[core, chip, me],
                send_sem=send1.at[index, step],
                recv_sem=recv1.at[index, step],
                device_id=peers[step - 1],
                device_id_type=mesh_kind,
            )
            copy.start()
            copies.append(copy)
        return own, copies

    def relay(index, far):
        far.wait_recv()
        held = outs[index].at[core, 1 - chip]
        onward = pltpu.make_async_remote_copy(
            src_ref=held, dst_ref=held, send_sem=fw_send.at[index], recv_sem=fw_recv.at[index],
            device_id=partner, device_id_type=mesh_kind,
        )
        onward.start()
        return onward

    count = len(sources)
    first = [launch(0)]
    second = []
    third = []
    for index in range(count):
        own, copies = first[index]
        own.wait()
        for copy in copies:
            copy.wait_recv()
        if index + 1 < count:
            first.append(launch(index + 1))
        block = outs[index].at[core, chip]
        far = pltpu.make_async_remote_copy(
            src_ref=block, dst_ref=block, send_sem=xs_send.at[index], recv_sem=xs_recv.at[index],
            device_id=across, device_id_type=mesh_kind,
        )
        far.start()
        near = pltpu.make_async_remote_copy(
            src_ref=block, dst_ref=block, send_sem=cs_send.at[index], recv_sem=cs_recv.at[index],
            device_id=partner, device_id_type=mesh_kind,
        )
        near.start()
        second.append((far, near))
        if index >= 1:
            third.append(relay(index - 1, second[index - 1][0]))
    third.append(relay(count - 1, second[count - 1][0]))
    for index in range(count):
        own, copies = first[index]
        for copy in copies:
            copy.wait_send()
        far, near = second[index]
        far.wait_send()
        near.wait_send()
        near.wait_recv()
        third[index].wait_send()
        third[index].wait_recv()


def dispatch(wires):
    groups = wires[0].shape[0]
    count = len(wires)
    tail = wires[0].shape[1:]
    dma = pltpu.SemaphoreType.DMA
    return pl.pallas_call(
        functools.partial(dispatch_kernel, groups),
        out_shape=[jax.ShapeDtypeStruct((2, 2, groups) + tail, wires[0].dtype)] * count,
        in_specs=[pl.BlockSpec(memory_space=pl.ANY)] * count,
        out_specs=[pl.BlockSpec(memory_space=pl.ANY)] * count,
        scratch_shapes=[
            dma((count,)),
            dma((count, groups)),
            dma((count, groups)),
            dma((count,)),
            dma((count,)),
            dma((count,)),
            dma((count,)),
            dma((count,)),
            dma((count,)),
        ],
        compiler_params=pltpu.CompilerParams(collective_id=0, has_side_effects=True),
    )(*wires)


def to_wire(rows, *lead):
    return rows.reshape(*lead, -1, 128)


def return_kernel(groups, *refs):
    count = len(refs) - 4
    sources = refs[:count]
    out, local_sem, send1, recv1 = refs[count:]
    mesh_kind = pl.DeviceIdType.MESH
    pipe = lax.axis_index("pipe")
    me = lax.axis_index("eg")
    chip = lax.axis_index("ez")
    core = lax.axis_index("ec")
    peers = [(pipe, lax.rem(me + step, groups), chip, core) for step in range(1, groups)]
    barrier = pltpu.get_barrier_semaphore()
    for peer in peers:
        pl.semaphore_signal(barrier, 1, device_id=peer, device_id_type=mesh_kind)
    pl.semaphore_wait(barrier, len(peers))
    started = []
    for index, source in enumerate(sources):
        own = pltpu.make_async_copy(source.at[me], out.at[index, me], local_sem.at[index])
        own.start()
        copies = []
        for step in range(1, groups):
            copy = pltpu.make_async_remote_copy(
                src_ref=source.at[peers[step - 1][1]],
                dst_ref=out.at[index, me],
                send_sem=send1.at[index, step],
                recv_sem=recv1.at[index, step],
                device_id=peers[step - 1],
                device_id_type=mesh_kind,
            )
            copy.start()
            copies.append(copy)
        started.append((own, copies))
    for own, copies in started:
        own.wait()
        for copy in copies:
            copy.wait_send()
            copy.wait_recv()


def send_home(wires, tag):
    groups = wires[0].shape[0]
    count = len(wires)
    dma = pltpu.SemaphoreType.DMA
    return pl.pallas_call(
        functools.partial(return_kernel, groups),
        out_shape=jax.ShapeDtypeStruct((count,) + wires[0].shape, wires[0].dtype),
        in_specs=[pl.BlockSpec(memory_space=pl.ANY)] * count,
        out_specs=pl.BlockSpec(memory_space=pl.ANY),
        scratch_shapes=[dma((count,)), dma((count, groups)), dma((count, groups))],
        compiler_params=pltpu.CompilerParams(collective_id=tag, has_side_effects=True),
    )(*wires)


def group_sum(parts, experts):
    model_width = parts.shape[-1]
    blocks = parts.reshape(2, 2, -1, model_width)
    core = lax.axis_index("ec")
    mine = lax.dynamic_index_in_dim(blocks, core, axis=0, keepdims=False)
    theirs = lax.dynamic_index_in_dim(blocks, 1 - core, axis=0, keepdims=False)
    came = passed_along(theirs, "ec", 1)
    pair = (mine.astype(jnp.float32) + came.astype(jnp.float32)).astype(jnp.bfloat16)
    chip = lax.axis_index("ez")
    keep = lax.dynamic_index_in_dim(pair, chip, axis=0, keepdims=False)
    send = lax.dynamic_index_in_dim(pair, 1 - chip, axis=0, keepdims=False)
    got = passed_along(send, "ez", 1)
    summed = (keep.astype(jnp.float32) + got.astype(jnp.float32)).astype(jnp.bfloat16)
    return to_wire(summed, experts)


def expert_forward(rows, up_proj, down_proj):
    pre = jnp.einsum("...d,df->...f", rows, up_proj, preferred_element_type=jnp.float32)
    act = jax.nn.silu(pre).astype(jnp.bfloat16)
    return jnp.einsum(
        "...f,fd->...d", act, down_proj, preferred_element_type=jnp.float32
    ).astype(jnp.bfloat16)


def expert_backward(rows, grad_rows, up_proj, down_proj):
    pre = jnp.einsum("...d,df->...f", rows, up_proj, preferred_element_type=jnp.float32)
    act = jax.nn.silu(pre).astype(jnp.bfloat16)
    dact = jnp.einsum("...d,fd->...f", grad_rows, down_proj, preferred_element_type=jnp.float32)
    dpre = (dact * silu_grad(pre)).astype(jnp.bfloat16)
    dpart = jnp.einsum(
        "...f,df->...d", dpre, up_proj, preferred_element_type=jnp.float32
    ).astype(jnp.bfloat16)
    grad_up = jnp.einsum("rd,rf->df", rows, dpre, preferred_element_type=jnp.float32)
    grad_down = jnp.einsum("rf,rd->fd", act, grad_rows, preferred_element_type=jnp.float32)
    return (dpart, grad_up, grad_down)


def local(
    fwd_acts, fwd_routes, fwd_gates, back_acts, back_routes, back_gates, back_grads, w_up, w_down
):
    devices = lax.axis_size("eg") * GROUP
    experts = devices // GROUP
    tok_rows = fwd_acts.shape[1]
    top_count = fwd_routes.shape[2]
    slot_cap = GROUP * (5 * tok_rows * top_count // (4 * devices))
    up_proj = w_up[0, 0]
    down_proj = w_down[0, 0]
    fwd_input = fwd_acts[0]
    back_input = back_acts[0]
    out_grad = back_grads[0]
    plain_f, gated_f = tables(fwd_routes[0], fwd_gates[0], experts, slot_cap)
    plain_b, gated_b = tables(back_routes[0], back_gates[0], experts, slot_cap)
    buffer_f = gather_rows(plain_f, fwd_input)
    buffer_x = gather_rows(plain_b, back_input)
    buffer_g = lax.dot_general(
        gated_b, out_grad.astype(jnp.float32), (((0,), (0,)), ((), ())), precision=HIGH
    ).astype(jnp.bfloat16)
    model_width = fwd_input.shape[-1]
    got = dispatch([to_wire(b, experts) for b in (buffer_f, buffer_x, buffer_g)])
    got_f, got_x, got_g = [got[index].reshape(-1, model_width) for index in range(3)]
    part = expert_forward(got_f, up_proj, down_proj)
    wire_f = group_sum(part, experts)
    summed_f = send_home([wire_f], 1)[0].reshape(-1, model_width).astype(jnp.float32)
    merged = jnp.dot(gated_f, summed_f, precision=HIGH)
    section_out = (fwd_input.astype(jnp.float32) + merged).astype(jnp.bfloat16)
    section_out, got_x, got_g = lax.optimization_barrier((section_out, got_x, got_g))
    dpart, grad_up, grad_down = expert_backward(got_x, got_g, up_proj, down_proj)
    wire_b = group_sum(dpart, experts)
    summed_b = send_home([wire_b], 2)[0].reshape(-1, model_width).astype(jnp.float32)
    spread_back = jnp.dot(plain_b, summed_b, precision=HIGH)
    section_grad = (out_grad.astype(jnp.float32) + spread_back).astype(jnp.bfloat16)
    fwd_next = passed_along(section_out[None], "pipe", 1)
    back_next = passed_along(section_grad[None], "pipe", -1)
    return (fwd_next, back_next, grad_up[None, None], grad_down[None, None])


def solution(mesh):
    groups = mesh.shape["expert"] // GROUP
    devices = mesh.devices.reshape(mesh.shape["pipe"], groups, 2, GROUP // 2)
    mesh = jax.sharding.Mesh(devices, ("pipe", "eg", "ez", "ec"))
    in_specs = (
        P("pipe", ("eg", "ez", "ec"), None),
        P("pipe", ("eg", "ez", "ec"), None),
        P("pipe", ("eg", "ez", "ec"), None),
        P("pipe", ("eg", "ez", "ec"), None),
        P("pipe", ("eg", "ez", "ec"), None),
        P("pipe", ("eg", "ez", "ec"), None),
        P("pipe", ("eg", "ez", "ec"), None),
        P("pipe", ("eg", "ez", "ec"), None, None),
        P("pipe", ("eg", "ez", "ec"), None, None),
    )
    out_specs = (
        P("pipe", ("eg", "ez", "ec"), None),
        P("pipe", ("eg", "ez", "ec"), None),
        P("pipe", ("eg", "ez", "ec"), None, None),
        P("pipe", ("eg", "ez", "ec"), None, None),
    )
    return jax.shard_map(local, mesh=mesh, in_specs=in_specs, out_specs=out_specs, check_vma=False)
```
